32 devices in a mesh: groups: 2 (over y), seq: 16 (over z, x, core).
Axes of the slice: x: 2, y: 2, z: 4, core: 2. Of those that a mesh axis runs over, the one named last changes fastest.
Arguments:
- hidden: bfloat16 [4, 4, 8192], P('groups', None, 'seq'), parts along dimension 0, may hold values from -1200 to 1200
- norm_gain: bfloat16 [8192], P('seq'), may hold values from 0.099609375 to 1.8984375
- q_weight: bfloat16 [8192, 8192], P('seq'), may hold values from -0.0625 to 0.0625
- kv_weight: bfloat16 [8192, 2048], P('seq'), may hold values from -0.0625 to 0.0625
- out_weight: bfloat16 [8192, 8192], P('seq'), may hold values from -0.09375 to 0.09375
- head_kind: int32 [8], replicated, may hold values from 0 to 1, as said below
- ret_keys: bfloat16 [4, 4, 32768, 128], P('groups', None, 'seq'), parts along dimension 0, may hold values from -600 to 600
- ret_values: bfloat16 [4, 4, 32768, 128], P('groups', None, 'seq'), parts along dimension 0, may hold values from -8 to 8
- stream_keys: bfloat16 [4, 4, 2048, 128], P('groups', None, 'seq'), parts along dimension 0, may hold values from -600 to 600
- stream_values: bfloat16 [4, 4, 2048, 128], P('groups', None, 'seq'), parts along dimension 0, may hold values from -8 to 8
- cache_len: int32 [4], P('groups'), parts along dimension 0, may hold values from 1 to 32768, as said below
- sink_len: int32 [4], P('groups'), parts along dimension 0, may hold values from 1 to 128, as said below
- window_len: int32 [4], P('groups'), parts along dimension 0, may hold values from 1 to 1920, as said below
Outputs:
- layer_output: bfloat16 [4, 4, 8192], P('groups', None, 'seq'), parts along dimension 0
- new_entries: bfloat16 [4, 4, 2048], P('groups'), parts along dimension 0
The draws below stay inside these ranges and needn't reach their ends.
There are 2 independent parts, one for each index of `groups`. The reference program is written for one: setup_inputs(seed, part) draws one part's arguments, and reference() takes and returns one part's arrays. A program takes and returns all parts, laid end to end along the dimension named above; an argument that names none is the same for every part. Nothing has to cross between parts.
Inputs may be any that keep to these rules, and one draw needn't show every extreme that they name: `head_kind`: exactly 4 of the 8 entries are 1, the others 0. `cache_len`: in every draw some request has all 32768 positions filled. `sink_len`: in every draw some request holds 128 sink tokens. `window_len`: in every draw some request holds 1920 recent tokens.
All inputs are finite; a program needn't handle non-finite values.
Results may differ from the reference program's by a relative error of at most 0.0075.
The reference program's roundings to bfloat16 on the way (of `normed`, `queries`, `rounded` and `attention`) count: a program that leaves them out, or rounds other values in their place, can miss the bound.
Values may be sent and summed in bfloat16 or wider, within the bound.
No kernel may reach another device: no remote copies, remote signals or barrier semaphores. Data moves between devices by JAX's collectives and lax.ppermute only.
A program may use at most 128 MiB of HBM per device.

```python
import math
import jax
import jax.numpy as jnp
from jax import lax

D = 8192
H = 64
KVH = 8
HD = 128
RET = 4
STR = 4
REQS = 2
DRAFT = 4
CACHE_DEV = 2048
CACHE_LEN = 32768
SLOTS = 2048
SINK_CAP = 128
N_SEQ = 16


def draw_hidden(key, part):
    key_list = jax.random.split(key, 3)
    column = jnp.arange(D, dtype=jnp.float32) / (D - 1)
    noise_draw = jnp.clip(jax.random.normal(key_list[0], (REQS, DRAFT, D), jnp.float32), -4.0, 4.0)
    rising = jnp.sqrt(1.0 + 2.0 * column)
    column_scale = jnp.exp(jax.random.uniform(key_list[1], (D,), jnp.float32, 0.0, math.log(10.0)))
    row_scale = jnp.exp(jax.random.uniform(key_list[2], (REQS, DRAFT, 1), jnp.float32, 0.0, math.log(10.0)))
    return (noise_draw * column_scale * rising * row_scale).astype(jnp.bfloat16)


def scaled_keys(key, shape, head_top):
    key_list = jax.random.split(key, 3)
    base_draw = jnp.clip(jax.random.normal(key_list[0], shape, jnp.float32), -5.0, 5.0)
    head_scale = jnp.exp(jax.random.uniform(key_list[1], (shape[0], shape[1], 1, 1), jnp.float32, 0.0, math.log(head_top)))
    slot_scale = jnp.exp(jax.random.uniform(key_list[2], (shape[0], shape[1], shape[2], 1), jnp.float32, math.log(0.3), math.log(3.0)))
    return base_draw * head_scale * slot_scale


def draw_ret_keys(key, part):
    return scaled_keys(key, (REQS, RET, CACHE_LEN, HD), 2.0).astype(jnp.bfloat16)


def draw_stream_keys(key, part):
    return scaled_keys(key, (REQS, STR, SLOTS, HD), 2.0).astype(jnp.bfloat16)


def draw_head_kind(key, part):
    shuffled = jax.random.permutation(key, KVH)
    return (shuffled < RET).astype(jnp.int32)


def filled_counts(key, most):
    chosen = jax.random.randint(jax.random.fold_in(key, 7), (), 0, REQS)
    others = jax.random.randint(jax.random.fold_in(key, 11), (REQS,), 1, most + 1)
    return jnp.where(jnp.arange(REQS) == chosen, most, others).astype(jnp.int32)


def draw_cache_len(key, part):
    return filled_counts(key, CACHE_LEN)


def draw_sink_len(key, part):
    return filled_counts(key, SINK_CAP)


def draw_window_len(key, part):
    return filled_counts(key, SLOTS - SINK_CAP)


def spiked(drawn, rng, source, target, blocks, factor):
    owner, partner = [(jnp.arange(drawn.shape[axis_at]) // (drawn.shape[axis_at] // blocks)).reshape([-1 if axis == axis_at else 1 for axis in range(drawn.ndim)]) for axis_at in (source, target)]
    chosen = jax.random.permutation(rng, blocks)[partner]
    strong = (owner == chosen) | (owner == (partner + blocks // 2) % blocks)
    return jnp.where(strong, factor * drawn, drawn)


def shard_levels(key, dims, cuts, smallest, largest):
    def one(axis_at, parts):
        heights = jax.random.uniform(jax.random.fold_in(jax.random.fold_in(key, 6), axis_at), (parts,), jnp.float32, smallest / len(cuts), largest / len(cuts))
        return jnp.repeat(jnp.exp(heights), dims[axis_at] // parts).reshape((-1,) + (1,) * (len(dims) - axis_at - 1))

    gain = one(*cuts[0])
    for cut in cuts[1:]:
        gain = gain * one(*cut)
    return gain


def normal_values(own_key, shape, width, most, cuts=(), kind=jnp.bfloat16):
    drawn = jax.random.normal(own_key, shape, jnp.float32) * width
    if len(cuts) > 0:
        drawn = shard_levels(own_key, shape, cuts, -0.22, 0.18) * drawn
    return jnp.clip(drawn, min=-most, max=most).astype(kind)


def gaussian_with(rng, dims, spread, limit, shards, heavy, kind=jnp.bfloat16):
    array = spread * jax.random.normal(rng, dims, jnp.float32)
    if shards:
        array = array * shard_levels(rng, dims, shards, -0.22, 0.18)
    return jnp.clip(spiked(array, jax.random.fold_in(rng, 3), *heavy), -limit, limit).astype(kind)


def setup_inputs(seed: int = 0, part: int = 0) -> dict:
    arg_keys = jax.random.split(jax.random.key(seed), 14)
    own_keys = jax.random.split(jax.random.fold_in(arg_keys[13], part), 14)
    return {
        "hidden": draw_hidden(jax.random.fold_in(jax.random.fold_in(arg_keys[13], part), 71), part),
        "norm_gain": jnp.clip(1.0 + 0.18 * jax.random.normal(arg_keys[1], (D,), jnp.float32), 0.099609375, 1.8984375).astype(jnp.bfloat16),
        "q_weight": normal_values(arg_keys[2], (D, H * HD), D ** -0.5, 0.0625, ((0, 16),)),
        "kv_weight": normal_values(arg_keys[3], (D, 2 * KVH * HD), D ** -0.5, 0.0625, ((0, 16),)),
        "out_weight": gaussian_with(arg_keys[4], (H * HD, D), (H * HD) ** -0.5, 0.09375, ((0, 16),), (0, 1, 16, 2.0)),
        "head_kind": draw_head_kind(jax.random.fold_in(arg_keys[13], 71), part),
        "ret_keys": draw_ret_keys(jax.random.fold_in(jax.random.fold_in(arg_keys[13], part), 71), part),
        "ret_values": normal_values(own_keys[7], (REQS, RET, CACHE_LEN, HD), 2.0, 8.0, ((2, 16),)),
        "stream_keys": draw_stream_keys(jax.random.fold_in(jax.random.fold_in(arg_keys[13], part), 71), part),
        "stream_values": normal_values(own_keys[9], (REQS, STR, SLOTS, HD), 2.0, 8.0, ((2, 16),)),
        "cache_len": draw_cache_len(jax.random.fold_in(jax.random.fold_in(arg_keys[13], part), 71), part),
        "sink_len": draw_sink_len(jax.random.fold_in(jax.random.fold_in(arg_keys[13], part), 71), part),
        "window_len": draw_window_len(jax.random.fold_in(jax.random.fold_in(arg_keys[13], part), 71), part),
    }


epsilon = 1e-05
floor_score = -1e+30

def block_stats(queries, cache_keys, cache_values, visible, score_scale):
    scores = jnp.einsum('bhqd,bhld->bhql', queries.astype(jnp.float32), cache_keys.astype(jnp.float32)) * score_scale
    scores = jnp.where(visible, scores, floor_score)
    peak_score = lax.optimization_barrier(jnp.max(scores, axis=-1))
    weights = jnp.where(visible, jnp.exp(scores - peak_score[..., None]), 0.0)
    weight_total = lax.optimization_barrier(jnp.sum(weights, axis=-1))
    rounded = lax.optimization_barrier(weights.astype(jnp.bfloat16))
    block_out = jnp.einsum('bhql,bhld->bhqd', rounded.astype(jnp.float32), cache_values.astype(jnp.float32))
    return (peak_score, weight_total, block_out)

def reference(hidden, norm_gain, q_weight, kv_weight, out_weight, head_kind, ret_keys, ret_values, stream_keys, stream_values, cache_len, sink_len, window_len):
    hidden32 = hidden.astype(jnp.float32)
    inverse = lax.rsqrt(lax.optimization_barrier(jnp.mean(hidden32 * hidden32, axis=-1, keepdims=True)) + epsilon)
    normed = (hidden32 * inverse * norm_gain.astype(jnp.float32)).astype(jnp.bfloat16)
    flat_rows = normed.reshape(REQS * DRAFT, D)
    queries = jnp.dot(flat_rows, q_weight, preferred_element_type=jnp.float32).astype(jnp.bfloat16)
    new_entries = jnp.dot(flat_rows, kv_weight, preferred_element_type=jnp.float32).astype(jnp.bfloat16)
    group_size = H // KVH
    query_rows = DRAFT * group_size
    grouped = queries.reshape(REQS, DRAFT, KVH, group_size, HD).transpose(0, 2, 1, 3, 4).reshape(REQS, KVH, query_rows, HD)
    fresh_split = new_entries.reshape(REQS, DRAFT, 2, KVH, HD)
    new_keys = fresh_split[:, :, 0].transpose(0, 2, 1, 3)
    new_values = fresh_split[:, :, 1].transpose(0, 2, 1, 3)
    order_key = (1 - head_kind) * KVH + jnp.arange(KVH, dtype=jnp.int32)
    head_order = jnp.argsort(order_key).astype(jnp.int32)
    ret_heads = head_order[:RET]
    str_heads = head_order[RET:]
    score_scale = HD ** (-0.5)
    ret_queries = grouped[:, ret_heads]
    str_queries = grouped[:, str_heads]
    slot_block = SLOTS // N_SEQ

    def retrieval_block(block_index):
        first_pos = block_index * CACHE_DEV
        keys_block = lax.dynamic_slice_in_dim(ret_keys, first_pos, CACHE_DEV, 2)
        values_block = lax.dynamic_slice_in_dim(ret_values, first_pos, CACHE_DEV, 2)
        positions = first_pos + jnp.arange(CACHE_DEV, dtype=jnp.int32)
        visible = (positions[None, :] < cache_len[:, None])[:, None, None, :]
        return block_stats(ret_queries, keys_block, values_block, visible, score_scale)

    def running_block(block_index):
        first_pos = block_index * slot_block
        keys_block = lax.dynamic_slice_in_dim(stream_keys, first_pos, slot_block, 2)
        values_block = lax.dynamic_slice_in_dim(stream_values, first_pos, slot_block, 2)
        positions = (first_pos + jnp.arange(slot_block, dtype=jnp.int32))[None, :]
        sinks = positions < sink_len[:, None]
        recent = (positions >= SINK_CAP) & (positions < SINK_CAP + window_len[:, None])
        visible = (sinks | recent)[:, None, None, :]
        return block_stats(str_queries, keys_block, values_block, visible, score_scale)
    block_ids = jnp.arange(N_SEQ, dtype=jnp.int32)
    ret_peak, ret_total, ret_out = lax.map(retrieval_block, block_ids)
    str_peak, str_total, str_out = lax.map(running_block, block_ids)
    peak_all = jnp.zeros((N_SEQ, REQS, KVH, query_rows), jnp.float32).at[:, :, ret_heads].set(ret_peak).at[:, :, str_heads].set(str_peak)
    total_all = jnp.zeros((N_SEQ, REQS, KVH, query_rows), jnp.float32).at[:, :, ret_heads].set(ret_total).at[:, :, str_heads].set(str_total)
    out_all = jnp.zeros((N_SEQ, REQS, KVH, query_rows, HD), jnp.float32).at[:, :, ret_heads].set(ret_out).at[:, :, str_heads].set(str_out)
    token_of_row = jnp.arange(query_rows, dtype=jnp.int32) // group_size
    new_visible = jnp.arange(DRAFT, dtype=jnp.int32)[None, :] <= token_of_row[:, None]
    new_peak, new_total, new_out = block_stats(grouped, new_keys, new_values, new_visible, score_scale)
    top_score = jnp.maximum(lax.optimization_barrier(jnp.max(peak_all, axis=0)), new_peak)
    cache_factor = jnp.exp(peak_all - top_score[None])
    new_factor = jnp.exp(new_peak - top_score)
    denominator = lax.optimization_barrier(jnp.sum(cache_factor * total_all, axis=0)) + new_factor * new_total
    numerator = lax.optimization_barrier(jnp.sum(cache_factor[..., None] * out_all, axis=0)) + new_factor[..., None] * new_out
    attended = numerator / denominator[..., None]
    attention = attended.reshape(REQS, KVH, DRAFT, group_size, HD).transpose(0, 2, 1, 3, 4).reshape(REQS * DRAFT, H * HD).astype(jnp.bfloat16)
    layer_output = jnp.dot(attention, out_weight, preferred_element_type=jnp.float32).astype(jnp.bfloat16)
    return (layer_output.reshape(REQS, DRAFT, D), new_entries.reshape(REQS, DRAFT, 2 * KVH * HD))
```

```python
import jax
import jax.numpy as jnp
from jax import lax
from jax.sharding import PartitionSpec as P

SINK_CAP = 128


epsilon = 1e-05
floor_score = -1e30


def exchanged(parts):
    return lax.all_to_all(parts, "seq", 0, 0, tiled=True)


def summed_over_devices(value):
    devices = lax.axis_size("seq")
    step = 1
    while step < devices:
        value = value + lax.ppermute(value, "seq", [(i, i ^ step) for i in range(devices)])
        step *= 2
    return value


def column_blocks(rows, blocks):
    return rows.reshape(rows.shape[0], blocks, -1).transpose(1, 0, 2)


def block_stats(queries, cache_keys, cache_values, visible, score_scale):
    scores = (
        jnp.einsum("bhqd,bhld->bhql", queries, cache_keys, preferred_element_type=jnp.float32)
        * score_scale
    )
    scores = jnp.where(visible, scores, floor_score)
    peak_score = jnp.max(scores, axis=-1)
    weights = jnp.where(visible, jnp.exp(scores - peak_score[..., None]), 0.0)
    weight_total = jnp.sum(weights, axis=-1)
    block_out = jnp.einsum(
        "bhql,bhld->bhqd",
        weights.astype(jnp.bfloat16),
        cache_values,
        preferred_element_type=jnp.float32,
    )
    return (peak_score, weight_total, block_out)


def spread_rows(values_in, selector):
    return jnp.einsum("brq,gr->bgq", values_in, selector, precision=lax.Precision.HIGHEST)


def spread_vectors(values_in, selector):
    return jnp.einsum("brqd,gr->bgqd", values_in, selector, precision=lax.Precision.HIGHEST)


def per_device(
    hidden,
    norm_gain,
    q_weight,
    kv_weight,
    out_weight,
    head_kind,
    ret_keys,
    ret_values,
    stream_keys,
    stream_values,
    cache_len,
    sink_len,
    window_len,
):
    requests, drafts, local_width = hidden.shape
    kv_heads = head_kind.shape[0]
    head_dim = ret_keys.shape[3]
    retrieval = ret_keys.shape[1]
    running = stream_keys.shape[1]
    head_count = q_weight.shape[1] // head_dim
    group_size = head_count // kv_heads
    query_rows = drafts * group_size
    devices = lax.axis_size("seq")
    position = lax.axis_index("seq")
    tokens = requests * drafts
    hidden32 = hidden.astype(jnp.float32)
    squares = summed_over_devices(jnp.sum(hidden32 * hidden32, axis=-1))
    inverse = lax.rsqrt(squares / (local_width * devices) + epsilon)
    normed = (hidden32 * inverse[..., None] * norm_gain.astype(jnp.float32)).astype(jnp.bfloat16)
    flat_rows = normed.reshape(tokens, local_width)
    part_query = jnp.dot(flat_rows, q_weight, preferred_element_type=jnp.float32)
    part_fresh = jnp.dot(flat_rows, kv_weight, preferred_element_type=jnp.float32)
    sums = jnp.sum(
        exchanged(
            jnp.concatenate(
                [column_blocks(part_query, devices), column_blocks(part_fresh, devices)], axis=-1
            )
        ),
        axis=0,
    ).astype(jnp.bfloat16)
    gathered = exchanged(jnp.broadcast_to(sums[None], (devices, *sums.shape)))
    query_width = q_weight.shape[1] // devices
    queries = gathered[..., :query_width].transpose(1, 0, 2).reshape(tokens, -1)
    new_entries = gathered[..., query_width:].transpose(1, 0, 2).reshape(tokens, -1)
    grouped = (
        queries.reshape(requests, drafts, kv_heads, group_size, head_dim)
        .transpose(0, 2, 1, 3, 4)
        .reshape(requests, kv_heads, query_rows, head_dim)
    )
    fresh_split = new_entries.reshape(requests, drafts, 2, kv_heads, head_dim)
    new_keys = fresh_split[:, :, 0].transpose(0, 2, 1, 3)
    new_values = fresh_split[:, :, 1].transpose(0, 2, 1, 3)
    kind_flag = head_kind == 1
    rank_ret = jnp.cumsum(head_kind) - 1
    rank_str = jnp.cumsum(1 - head_kind) - 1
    select_ret = (
        kind_flag[:, None] & (rank_ret[:, None] == jnp.arange(retrieval)[None, :])
    ).astype(jnp.float32)
    select_str = (
        jnp.logical_not(kind_flag)[:, None] & (rank_str[:, None] == jnp.arange(running)[None, :])
    ).astype(jnp.float32)
    ret_queries = jnp.einsum(
        "bgqd,gr->brqd",
        grouped,
        select_ret.astype(jnp.bfloat16),
        preferred_element_type=jnp.float32,
    ).astype(jnp.bfloat16)
    str_queries = jnp.einsum(
        "bgqd,gr->brqd",
        grouped,
        select_str.astype(jnp.bfloat16),
        preferred_element_type=jnp.float32,
    ).astype(jnp.bfloat16)
    score_scale = head_dim ** (-0.5)
    cache_block = ret_keys.shape[2]
    cache_pos = position * cache_block + jnp.arange(cache_block)
    ret_visible = (cache_pos[None, :] < cache_len[:, None])[:, None, None, :]
    slot_block = stream_keys.shape[2]
    slot_pos = (position * slot_block + jnp.arange(slot_block))[None, :]
    sink_part = slot_pos < sink_len[:, None]
    recent_part = (slot_pos >= SINK_CAP) & (slot_pos < SINK_CAP + window_len[:, None])
    str_visible = (sink_part | recent_part)[:, None, None, :]
    ret_peak, ret_total, ret_out = block_stats(
        ret_queries, ret_keys, ret_values, ret_visible, score_scale
    )
    str_peak, str_total, str_out = block_stats(
        str_queries, stream_keys, stream_values, str_visible, score_scale
    )
    peak_all = spread_rows(ret_peak, select_ret) + spread_rows(str_peak, select_str)
    total_all = spread_rows(ret_total, select_ret) + spread_rows(str_total, select_str)
    out_all = spread_vectors(ret_out, select_ret) + spread_vectors(str_out, select_str)
    token_of_row = jnp.arange(query_rows) // group_size
    new_visible = jnp.arange(drafts)[None, :] <= token_of_row[:, None]
    new_peak, new_total, new_out = block_stats(
        grouped, new_keys, new_values, new_visible, score_scale
    )
    own_width = out_weight.shape[0]
    block_heads = max(1, own_width // head_dim)

    def by_token(value):
        split = value.reshape(requests, kv_heads, drafts, group_size, -1)
        return split.transpose(0, 2, 1, 3, 4).reshape(tokens, head_count, -1)

    first_head = (jnp.arange(devices) * own_width) // head_dim
    block_head = first_head[:, None] + jnp.arange(block_heads)[None, :]

    def head_blocks(value):
        rows = by_token(value).reshape(tokens, head_count)
        return jnp.take(rows, block_head.reshape(-1), axis=1).reshape(tokens, devices, -1).transpose(1, 0, 2)

    received = exchanged(
        jnp.concatenate(
            [
                column_blocks(by_token(out_all).reshape(tokens, -1), devices),
                head_blocks(peak_all),
                head_blocks(total_all),
            ],
            axis=-1,
        )
    )
    got_out = received[..., :own_width].reshape(devices, tokens, block_heads, -1)
    got_peak = received[..., own_width : own_width + block_heads]
    got_total = received[..., own_width + block_heads :]

    def own_heads(value):
        blocks = column_blocks(by_token(value).reshape(tokens, -1), devices)
        return lax.dynamic_index_in_dim(blocks, position, 0, False).reshape(tokens, block_heads, -1)

    own_new_out = own_heads(new_out)
    own_new_peak = lax.dynamic_index_in_dim(head_blocks(new_peak), position, 0, False)
    own_new_total = lax.dynamic_index_in_dim(head_blocks(new_total), position, 0, False)
    top_score = jnp.maximum(jnp.max(got_peak, axis=0), own_new_peak)
    cache_factor = jnp.exp(got_peak - top_score[None])
    new_factor = jnp.exp(own_new_peak - top_score)
    denominator = jnp.sum(got_total * cache_factor, axis=0) + own_new_total * new_factor
    attended = (
        jnp.sum(got_out * cache_factor[..., None], axis=0) + own_new_out * new_factor[..., None]
    ) / denominator[..., None]
    own_attention = attended.reshape(tokens, own_width).astype(jnp.bfloat16)
    part_output = jnp.dot(own_attention, out_weight, preferred_element_type=jnp.float32)
    own_output = jnp.sum(exchanged(column_blocks(part_output, devices)), axis=0)
    layer_output = own_output.reshape(requests, drafts, local_width).astype(jnp.bfloat16)
    return (layer_output, new_entries.reshape(requests, drafts, 2 * kv_heads * head_dim))


def solution(mesh):
    in_specs = (
        P("groups", None, "seq"),
        P("seq"),
        P("seq", None),
        P("seq", None),
        P("seq", None),
        P(),
        P("groups", None, "seq", None),
        P("groups", None, "seq", None),
        P("groups", None, "seq", None),
        P("groups", None, "seq", None),
        P("groups"),
        P("groups"),
        P("groups"),
    )
    out_specs = (P("groups", None, "seq"), P("groups", None, None))
    return jax.shard_map(
        per_device, mesh=mesh, in_specs=in_specs, out_specs=out_specs, check_vma=False
    )
```

```python
import functools

import jax
import jax.numpy as jnp
from jax import lax
from jax.experimental import pallas as pl
from jax.experimental.pallas import tpu as pltpu
from jax.sharding import PartitionSpec as P


SINK_CAP = 128


epsilon = 1e-05
floor_score = -1e30


def exchanged(parts):
    return lax.all_to_all(parts, "seq", 0, 0, tiled=True)


def summed_over_devices(value):
    devices = lax.axis_size("seq")
    step = 1
    while step < devices:
        value = value + lax.ppermute(value, "seq", [(i, i ^ step) for i in range(devices)])
        step *= 2
    return value


def column_blocks(rows, blocks):
    return rows.reshape(rows.shape[0], blocks, -1).transpose(1, 0, 2)


def block_stats(queries, cache_keys, cache_values, visible, score_scale):
    scores = (
        jnp.einsum("bhqd,bhld->bhql", queries, cache_keys, preferred_element_type=jnp.float32)
        * score_scale
    )
    scores = jnp.where(visible, scores, floor_score)
    peak_score = jnp.max(scores, axis=-1)
    weights = jnp.where(visible, jnp.exp(scores - peak_score[..., None]), 0.0)
    weight_total = jnp.sum(weights, axis=-1)
    block_out = jnp.einsum(
        "bhql,bhld->bhqd",
        weights.astype(jnp.bfloat16),
        cache_values,
        preferred_element_type=jnp.float32,
    )
    return (peak_score, weight_total, block_out)


def spread_rows(values_in, selector):
    return jnp.einsum("brq,gr->bgq", values_in, selector, precision=lax.Precision.HIGHEST)


def spread_vectors(values_in, selector):
    return jnp.einsum("brqd,gr->bgqd", values_in, selector, precision=lax.Precision.HIGHEST)


def per_device_any(
    hidden,
    norm_gain,
    q_weight,
    kv_weight,
    out_weight,
    head_kind,
    ret_keys,
    ret_values,
    stream_keys,
    stream_values,
    cache_len,
    sink_len,
    window_len,
):
    requests, drafts, local_width = hidden.shape
    kv_heads = head_kind.shape[0]
    head_dim = ret_keys.shape[3]
    retrieval = ret_keys.shape[1]
    running = stream_keys.shape[1]
    head_count = q_weight.shape[1] // head_dim
    group_size = head_count // kv_heads
    query_rows = drafts * group_size
    devices = lax.axis_size("seq")
    position = lax.axis_index("seq")
    tokens = requests * drafts
    hidden32 = hidden.astype(jnp.float32)
    squares = summed_over_devices(jnp.sum(hidden32 * hidden32, axis=-1))
    inverse = lax.rsqrt(squares / (local_width * devices) + epsilon)
    normed = (hidden32 * inverse[..., None] * norm_gain.astype(jnp.float32)).astype(jnp.bfloat16)
    flat_rows = normed.reshape(tokens, local_width)
    part_query = jnp.dot(flat_rows, q_weight, preferred_element_type=jnp.float32)
    part_fresh = jnp.dot(flat_rows, kv_weight, preferred_element_type=jnp.float32)
    sums = jnp.sum(
        exchanged(
            jnp.concatenate(
                [column_blocks(part_query, devices), column_blocks(part_fresh, devices)], axis=-1
            )
        ),
        axis=0,
    ).astype(jnp.bfloat16)
    gathered = exchanged(jnp.broadcast_to(sums[None], (devices, *sums.shape)))
    query_width = q_weight.shape[1] // devices
    queries = gathered[..., :query_width].transpose(1, 0, 2).reshape(tokens, -1)
    new_entries = gathered[..., query_width:].transpose(1, 0, 2).reshape(tokens, -1)
    grouped = (
        queries.reshape(requests, drafts, kv_heads, group_size, head_dim)
        .transpose(0, 2, 1, 3, 4)
        .reshape(requests, kv_heads, query_rows, head_dim)
    )
    fresh_split = new_entries.reshape(requests, drafts, 2, kv_heads, head_dim)
    new_keys = fresh_split[:, :, 0].transpose(0, 2, 1, 3)
    new_values = fresh_split[:, :, 1].transpose(0, 2, 1, 3)
    kind_flag = head_kind == 1
    rank_ret = jnp.cumsum(head_kind) - 1
    rank_str = jnp.cumsum(1 - head_kind) - 1
    select_ret = (
        kind_flag[:, None] & (rank_ret[:, None] == jnp.arange(retrieval)[None, :])
    ).astype(jnp.float32)
    select_str = (
        jnp.logical_not(kind_flag)[:, None] & (rank_str[:, None] == jnp.arange(running)[None, :])
    ).astype(jnp.float32)
    ret_queries = jnp.einsum(
        "bgqd,gr->brqd",
        grouped,
        select_ret.astype(jnp.bfloat16),
        preferred_element_type=jnp.float32,
    ).astype(jnp.bfloat16)
    str_queries = jnp.einsum(
        "bgqd,gr->brqd",
        grouped,
        select_str.astype(jnp.bfloat16),
        preferred_element_type=jnp.float32,
    ).astype(jnp.bfloat16)
    score_scale = head_dim ** (-0.5)
    cache_block = ret_keys.shape[2]
    cache_pos = position * cache_block + jnp.arange(cache_block)
    ret_visible = (cache_pos[None, :] < cache_len[:, None])[:, None, None, :]
    slot_block = stream_keys.shape[2]
    slot_pos = (position * slot_block + jnp.arange(slot_block))[None, :]
    sink_part = slot_pos < sink_len[:, None]
    recent_part = (slot_pos >= SINK_CAP) & (slot_pos < SINK_CAP + window_len[:, None])
    str_visible = (sink_part | recent_part)[:, None, None, :]
    ret_peak, ret_total, ret_out = block_stats(
        ret_queries, ret_keys, ret_values, ret_visible, score_scale
    )
    str_peak, str_total, str_out = block_stats(
        str_queries, stream_keys, stream_values, str_visible, score_scale
    )
    peak_all = spread_rows(ret_peak, select_ret) + spread_rows(str_peak, select_str)
    total_all = spread_rows(ret_total, select_ret) + spread_rows(str_total, select_str)
    out_all = spread_vectors(ret_out, select_ret) + spread_vectors(str_out, select_str)
    token_of_row = jnp.arange(query_rows) // group_size
    new_visible = jnp.arange(drafts)[None, :] <= token_of_row[:, None]
    new_peak, new_total, new_out = block_stats(
        grouped, new_keys, new_values, new_visible, score_scale
    )
    own_width = out_weight.shape[0]
    block_heads = max(1, own_width // head_dim)

    def by_token(value):
        split = value.reshape(requests, kv_heads, drafts, group_size, -1)
        return split.transpose(0, 2, 1, 3, 4).reshape(tokens, head_count, -1)

    first_head = (jnp.arange(devices) * own_width) // head_dim
    block_head = first_head[:, None] + jnp.arange(block_heads)[None, :]

    def head_blocks(value):
        rows = by_token(value).reshape(tokens, head_count)
        return jnp.take(rows, block_head.reshape(-1), axis=1).reshape(tokens, devices, -1).transpose(1, 0, 2)

    received = exchanged(
        jnp.concatenate(
            [
                column_blocks(by_token(out_all).reshape(tokens, -1), devices),
                head_blocks(peak_all),
                head_blocks(total_all),
            ],
            axis=-1,
        )
    )
    got_out = received[..., :own_width].reshape(devices, tokens, block_heads, -1)
    got_peak = received[..., own_width : own_width + block_heads]
    got_total = received[..., own_width + block_heads :]

    def own_heads(value):
        blocks = column_blocks(by_token(value).reshape(tokens, -1), devices)
        return lax.dynamic_index_in_dim(blocks, position, 0, False).reshape(tokens, block_heads, -1)

    own_new_out = own_heads(new_out)
    own_new_peak = lax.dynamic_index_in_dim(head_blocks(new_peak), position, 0, False)
    own_new_total = lax.dynamic_index_in_dim(head_blocks(new_total), position, 0, False)
    top_score = jnp.maximum(jnp.max(got_peak, axis=0), own_new_peak)
    cache_factor = jnp.exp(got_peak - top_score[None])
    new_factor = jnp.exp(own_new_peak - top_score)
    denominator = jnp.sum(got_total * cache_factor, axis=0) + own_new_total * new_factor
    attended = (
        jnp.sum(got_out * cache_factor[..., None], axis=0) + own_new_out * new_factor[..., None]
    ) / denominator[..., None]
    own_attention = attended.reshape(tokens, own_width).astype(jnp.bfloat16)
    part_output = jnp.dot(own_attention, out_weight, preferred_element_type=jnp.float32)
    own_output = jnp.sum(exchanged(column_blocks(part_output, devices)), axis=0)
    layer_output = own_output.reshape(requests, drafts, local_width).astype(jnp.bfloat16)
    return (layer_output, new_entries.reshape(requests, drafts, 2 * kv_heads * head_dim))


def flat_tokens(ref):
    return jnp.concatenate([ref[b].astype(jnp.float32) for b in range(ref.shape[0])], axis=0)


def squares_kernel(hidden_ref, out_ref):
    rows = flat_tokens(hidden_ref)
    out_ref[...] = jnp.broadcast_to(jnp.sum(rows * rows, axis=1, keepdims=True), out_ref.shape)


def from_peers(value, low, radix):
    devices = lax.axis_size("seq")
    return [
        lax.ppermute(value, "seq", [(i, i ^ (low * step)) for i in range(devices)])
        for step in range(1, radix)
    ]


def projection_kernel(width, parts, *refs):
    squares = refs[:parts]
    hidden_ref, gain_ref, query_ref, fresh_ref, out_ref, normed_ref = refs[parts:]

    @pl.when(pl.program_id(0) == 0)
    def _():
        total = squares[0][...]
        for ref in squares[1:]:
            total = total + ref[...]
        inverse = lax.rsqrt(total[:, :1] / width + epsilon)
        gain = gain_ref[...].astype(jnp.float32)
        normed_ref[...] = (flat_tokens(hidden_ref) * inverse * gain).astype(jnp.bfloat16)

    normed = normed_ref[...]
    lanes = out_ref.shape[2]
    tokens = normed.shape[0]
    part = jnp.dot(normed, query_ref[...], preferred_element_type=jnp.float32)
    pieces = part.shape[1] // lanes
    for piece in range(pieces):
        out_ref[0, piece * tokens : (piece + 1) * tokens, :] = part[
            :, piece * lanes : (piece + 1) * lanes
        ]
    out_ref[0, pieces * tokens :, :] = jnp.dot(
        normed, fresh_ref[...], preferred_element_type=jnp.float32
    )


def round_kernel(parts_ref, out_ref):
    total = jnp.sum(parts_ref[...], axis=0).astype(jnp.bfloat16)
    for target in range(out_ref.shape[0]):
        out_ref[target] = total


def head_of(table_ref, kv_heads, flag, rank):
    found, before = jnp.int32(0), jnp.int32(0)
    for head in range(kv_heads):
        is_kind = table_ref[head] == flag
        found = jnp.where(is_kind & (before == rank), head, found)
        before = before + is_kind.astype(jnp.int32)
    return found


def diagonal_of(rows, lanes):
    return lax.broadcasted_iota(jnp.int32, (rows, lanes), 0) == lax.broadcasted_iota(
        jnp.int32, (rows, lanes), 1
    )


def as_row(column, lanes):
    return jnp.sum(
        jnp.where(diagonal_of(column.shape[0], lanes), column, 0.0), axis=0, keepdims=True
    )


def as_column(row, rows):
    return jnp.sum(jnp.where(diagonal_of(rows, row.shape[1]), row, 0.0), axis=1, keepdims=True)


def masked_weights(scores, visible):
    scores = jnp.where(visible, scores, floor_score)
    peak = jnp.max(scores, axis=1, keepdims=True)
    weights = jnp.where(visible, jnp.exp(scores - peak), 0.0)
    return peak, jnp.sum(weights, axis=1, keepdims=True), weights.astype(jnp.bfloat16)


def dot_keys(queries, keys):
    return lax.dot_general(
        queries, keys, (((1,), (1,)), ((), ())), preferred_element_type=jnp.float32
    )


def stat_rows(peak, total, lanes, sublanes):
    pad = jnp.zeros((sublanes - 2, lanes), jnp.float32)
    return jnp.concatenate([as_row(peak, lanes), as_row(total, lanes), pad], axis=0)


def attention_kernel(
    kv_heads,
    drafts,
    table_ref,
    entries_ref,
    ret_key_ref,
    ret_value_ref,
    str_key_ref,
    str_value_ref,
    out_ref,
):
    rank = pl.program_id(0)
    requests = ret_key_ref.shape[0]
    tokens = requests * drafts
    chunks, all_rows, head_dim = entries_ref.shape
    head_rows = all_rows - tokens
    per_head = chunks // kv_heads
    rows = per_head * head_rows
    position = table_ref[kv_heads + 3 * requests]
    row = lax.broadcasted_iota(jnp.int32, (rows, 1), 0)
    request_of_row = (row % tokens) // drafts

    def by_request(values):
        picked = values[0]
        for b in range(1, requests):
            picked = jnp.where(request_of_row == b, values[b], picked)
        return picked

    def limit(which):
        return by_request([table_ref[kv_heads + which * requests + b] for b in range(requests)])

    def one(head, key_ref, value_ref, visible):
        queries = jnp.concatenate(
            [entries_ref[head * per_head + half, :head_rows, :] for half in range(per_head)], axis=0
        )
        scores = by_request([dot_keys(queries, key_ref[b, 0]) for b in range(requests)])
        peak, total, weights = masked_weights(scores * head_dim ** (-0.5), visible)
        mixed = by_request(
            [
                jnp.dot(weights, value_ref[b, 0], preferred_element_type=jnp.float32)
                for b in range(requests)
            ]
        )
        for half in range(per_head):
            span = slice(half * head_rows, (half + 1) * head_rows)
            out_ref[head * per_head + half, :head_rows, :] = mixed[span]
            out_ref[head * per_head + half, head_rows:, :] = stat_rows(
                peak[span], total[span], head_dim, tokens
            )

    block = ret_key_ref.shape[2]
    place = position * block + lax.broadcasted_iota(jnp.int32, (rows, block), 1)
    one(head_of(table_ref, kv_heads, 1, rank), ret_key_ref, ret_value_ref, place < limit(0))
    slots = str_key_ref.shape[2]
    slot = position * slots + lax.broadcasted_iota(jnp.int32, (rows, slots), 1)
    recent = (slot >= SINK_CAP) & (slot < SINK_CAP + limit(2))
    head = head_of(table_ref, kv_heads, 0, rank)
    one(head, str_key_ref, str_value_ref, (slot < limit(1)) | recent)


def fresh_kernel(kv_heads, requests, drafts, table_ref, entries_ref, out_ref):
    position = table_ref[kv_heads + 3 * requests]
    tokens = requests * drafts
    chunks, all_rows, head_dim = entries_ref.shape
    rows = all_rows - tokens
    head = position // (chunks // kv_heads)
    queries = entries_ref[position, :rows, :]
    keys = entries_ref[head, rows:, :]
    values = entries_ref[kv_heads + head, rows:, :]
    of_row = lax.broadcasted_iota(jnp.int32, (rows, tokens), 0) % tokens
    of_key = lax.broadcasted_iota(jnp.int32, (rows, tokens), 1)
    visible = (of_row // drafts == of_key // drafts) & (of_key <= of_row)
    peak, total, weights = masked_weights(dot_keys(queries, keys) * head_dim ** (-0.5), visible)
    out_ref[:rows, :] = jnp.dot(weights, values, preferred_element_type=jnp.float32)
    out_ref[rows:, :] = stat_rows(peak, total, head_dim, tokens)


def output_kernel(tokens, parts_ref, fresh_ref, weight_ref, out_ref, attention_ref):
    @pl.when(pl.program_id(0) == 0)
    def _():
        sources, all_rows, head_dim = parts_ref.shape
        rows = all_rows - tokens
        peaks = jnp.concatenate([parts_ref[s, rows : rows + 1, :] for s in range(sources)], axis=0)
        totals = jnp.concatenate(
            [parts_ref[s, rows + 1 : rows + 2, :] for s in range(sources)], axis=0
        )
        new_peak = fresh_ref[rows : rows + 1, :]
        top = jnp.maximum(jnp.max(peaks, axis=0, keepdims=True), new_peak)
        factors = jnp.exp(peaks - top)
        new_factor = jnp.exp(new_peak - top)
        denominator = (
            jnp.sum(factors * totals, axis=0, keepdims=True)
            + new_factor * fresh_ref[rows + 1 : rows + 2, :]
        )
        numerator = as_column(new_factor, rows) * fresh_ref[:rows, :]
        for s in range(sources):
            numerator = numerator + as_column(factors[s : s + 1], rows) * parts_ref[s, :rows, :]
        attended = numerator / as_column(denominator, rows)
        attention_ref[...] = jnp.concatenate(
            [attended[r : r + tokens] for r in range(0, rows, tokens)], axis=1
        ).astype(jnp.bfloat16)

    out_ref[0] = jnp.dot(
        attention_ref[...], weight_ref[...], preferred_element_type=jnp.float32
    )


def whole(array):
    return pl.BlockSpec(array.shape, lambda *_: (0,) * array.ndim)


def shaped(*shape, dtype=jnp.float32):
    return jax.ShapeDtypeStruct(shape, dtype)


def per_device_heads(
    hidden,
    norm_gain,
    q_weight,
    kv_weight,
    out_weight,
    head_kind,
    ret_keys,
    ret_values,
    stream_keys,
    stream_values,
    cache_len,
    sink_len,
    window_len,
):
    requests, drafts, local_width = hidden.shape
    kv_heads = head_kind.shape[0]
    head_dim = ret_keys.shape[3]
    retrieval = ret_keys.shape[1]
    devices = lax.axis_size("seq")
    position = lax.axis_index("seq")
    tokens = requests * drafts
    query_width = q_weight.shape[1] // devices
    fresh_width = kv_weight.shape[1] // devices
    rows = tokens * (query_width // head_dim)
    smem = pl.BlockSpec(memory_space=pltpu.SMEM)
    table = jnp.concatenate(
        [head_kind, cache_len, sink_len, window_len, position.astype(jnp.int32)[None]]
    )

    squares = pl.pallas_call(squares_kernel, out_shape=shaped(tokens, head_dim))(hidden)
    near = min(4, devices)
    squares = functools.reduce(jnp.add, from_peers(squares, 1, near), squares)
    parts = [squares, *from_peers(squares, near, devices // near)]
    gain = norm_gain[None, :]
    part_entries = pl.pallas_call(
        functools.partial(projection_kernel, local_width * devices, len(parts)),
        grid=(devices,),
        in_specs=[
            *(whole(part) for part in parts),
            whole(hidden),
            whole(gain),
            pl.BlockSpec((local_width, query_width), lambda c: (0, c)),
            pl.BlockSpec((local_width, fresh_width), lambda c: (0, c)),
        ],
        out_specs=pl.BlockSpec((1, rows + tokens, head_dim), lambda c: (c, 0, 0)),
        out_shape=shaped(devices, rows + tokens, head_dim),
        scratch_shapes=[pltpu.VMEM((tokens, local_width), jnp.bfloat16)],
    )(*parts, hidden, gain, q_weight, kv_weight)

    own_entries = pl.pallas_call(
        round_kernel, out_shape=shaped(*part_entries.shape, dtype=jnp.bfloat16)
    )(exchanged(part_entries))
    entries = exchanged(own_entries)
    new_entries = entries[:, rows:, :].transpose(1, 0, 2).reshape(requests, drafts, -1)

    def heads_spec(array):
        shape = (requests, 1, *array.shape[2:])
        return pl.BlockSpec(shape, lambda r: (0, r, 0, 0))

    caches = (ret_keys, ret_values, stream_keys, stream_values)
    part_out = pl.pallas_call(
        functools.partial(attention_kernel, kv_heads, drafts),
        grid=(retrieval,),
        in_specs=[smem, whole(entries), *(heads_spec(cache) for cache in caches)],
        out_specs=pl.BlockSpec((devices, rows + tokens, head_dim), lambda r: (0, 0, 0)),
        out_shape=shaped(devices, rows + tokens, head_dim),
    )(table, entries, *caches)
    received = exchanged(part_out)
    fresh = pl.pallas_call(
        functools.partial(fresh_kernel, kv_heads, requests, drafts),
        in_specs=[smem, pl.BlockSpec(memory_space=pltpu.VMEM)],
        out_shape=shaped(rows + tokens, head_dim),
    )(table, entries)

    own_rows, width = out_weight.shape
    part_output = pl.pallas_call(
        functools.partial(output_kernel, tokens),
        grid=(devices,),
        in_specs=[
            whole(received),
            whole(fresh),
            pl.BlockSpec((own_rows, width // devices), lambda c: (0, c)),
        ],
        out_specs=pl.BlockSpec((1, tokens, width // devices), lambda c: (c, 0, 0)),
        out_shape=shaped(devices, tokens, width // devices),
        scratch_shapes=[pltpu.VMEM((tokens, own_rows), jnp.bfloat16)],
    )(received, fresh, out_weight)
    own_output = jnp.sum(exchanged(part_output), axis=0)
    layer_output = own_output.reshape(requests, drafts, local_width).astype(jnp.bfloat16)
    return (layer_output, new_entries)


def per_device(*args):
    hidden, _, q_weight, kv_weight, _, head_kind, ret_keys, _, stream_keys = args[:9]
    devices = lax.axis_size("seq")
    kv_heads, head_dim = head_kind.shape[0], ret_keys.shape[3]
    whole_heads = (
        (hidden.shape[0] * hidden.shape[1]) % 8 == 0
        and q_weight.shape[1] % (devices * head_dim) == 0
        and kv_weight.shape[1] == devices * head_dim
        and devices == 2 * kv_heads
        and ret_keys.shape[1] == stream_keys.shape[1]
    )
    return (per_device_heads if whole_heads else per_device_any)(*args)


def solution(mesh):
    in_specs = (
        P("groups", None, "seq"),
        P("seq"),
        P("seq", None),
        P("seq", None),
        P("seq", None),
        P(),
        P("groups", None, "seq", None),
        P("groups", None, "seq", None),
        P("groups", None, "seq", None),
        P("groups", None, "seq", None),
        P("groups"),
        P("groups"),
        P("groups"),
    )
    out_specs = (P("groups", None, "seq"), P("groups", None, None))
    return jax.shard_map(
        per_device, mesh=mesh, in_specs=in_specs, out_specs=out_specs, check_vma=False
    )
```

```python
import functools

import jax
import jax.numpy as jnp
from jax import lax
from jax.experimental import pallas as pl
from jax.experimental.pallas import tpu as pltpu
from jax.sharding import PartitionSpec as P


SINK_CAP = 128


epsilon = 1e-05
floor_score = -1e30


def exchanged(parts):
    return lax.all_to_all(parts, "seq", 0, 0, tiled=True)


def summed_over_devices(value):
    devices = lax.axis_size("seq")
    step = 1
    while step < devices:
        value = value + lax.ppermute(value, "seq", [(i, i ^ step) for i in range(devices)])
        step *= 2
    return value


def column_blocks(rows, blocks):
    return rows.reshape(rows.shape[0], blocks, -1).transpose(1, 0, 2)


def block_stats(queries, cache_keys, cache_values, visible, score_scale):
    scores = (
        jnp.einsum("bhqd,bhld->bhql", queries, cache_keys, preferred_element_type=jnp.float32)
        * score_scale
    )
    scores = jnp.where(visible, scores, floor_score)
    peak_score = jnp.max(scores, axis=-1)
    weights = jnp.where(visible, jnp.exp(scores - peak_score[..., None]), 0.0)
    weight_total = jnp.sum(weights, axis=-1)
    block_out = jnp.einsum(
        "bhql,bhld->bhqd",
        weights.astype(jnp.bfloat16),
        cache_values,
        preferred_element_type=jnp.float32,
    )
    return (peak_score, weight_total, block_out)


def spread_rows(values_in, selector):
    return jnp.einsum("brq,gr->bgq", values_in, selector, precision=lax.Precision.HIGHEST)


def spread_vectors(values_in, selector):
    return jnp.einsum("brqd,gr->bgqd", values_in, selector, precision=lax.Precision.HIGHEST)


def per_device_any(
    hidden,
    norm_gain,
    q_weight,
    kv_weight,
    out_weight,
    head_kind,
    ret_keys,
    ret_values,
    stream_keys,
    stream_values,
    cache_len,
    sink_len,
    window_len,
):
    requests, drafts, local_width = hidden.shape
    kv_heads = head_kind.shape[0]
    head_dim = ret_keys.shape[3]
    retrieval = ret_keys.shape[1]
    running = stream_keys.shape[1]
    head_count = q_weight.shape[1] // head_dim
    group_size = head_count // kv_heads
    query_rows = drafts * group_size
    devices = lax.axis_size("seq")
    position = lax.axis_index("seq")
    tokens = requests * drafts
    hidden32 = hidden.astype(jnp.float32)
    squares = summed_over_devices(jnp.sum(hidden32 * hidden32, axis=-1))
    inverse = lax.rsqrt(squares / (local_width * devices) + epsilon)
    normed = (hidden32 * inverse[..., None] * norm_gain.astype(jnp.float32)).astype(jnp.bfloat16)
    flat_rows = normed.reshape(tokens, local_width)
    part_query = jnp.dot(flat_rows, q_weight, preferred_element_type=jnp.float32)
    part_fresh = jnp.dot(flat_rows, kv_weight, preferred_element_type=jnp.float32)
    sums = jnp.sum(
        exchanged(
            jnp.concatenate(
                [column_blocks(part_query, devices), column_blocks(part_fresh, devices)], axis=-1
            )
        ),
        axis=0,
    ).astype(jnp.bfloat16)
    gathered = exchanged(jnp.broadcast_to(sums[None], (devices, *sums.shape)))
    query_width = q_weight.shape[1] // devices
    queries = gathered[..., :query_width].transpose(1, 0, 2).reshape(tokens, -1)
    new_entries = gathered[..., query_width:].transpose(1, 0, 2).reshape(tokens, -1)
    grouped = (
        queries.reshape(requests, drafts, kv_heads, group_size, head_dim)
        .transpose(0, 2, 1, 3, 4)
        .reshape(requests, kv_heads, query_rows, head_dim)
    )
    fresh_split = new_entries.reshape(requests, drafts, 2, kv_heads, head_dim)
    new_keys = fresh_split[:, :, 0].transpose(0, 2, 1, 3)
    new_values = fresh_split[:, :, 1].transpose(0, 2, 1, 3)
    kind_flag = head_kind == 1
    rank_ret = jnp.cumsum(head_kind) - 1
    rank_str = jnp.cumsum(1 - head_kind) - 1
    select_ret = (
        kind_flag[:, None] & (rank_ret[:, None] == jnp.arange(retrieval)[None, :])
    ).astype(jnp.float32)
    select_str = (
        jnp.logical_not(kind_flag)[:, None] & (rank_str[:, None] == jnp.arange(running)[None, :])
    ).astype(jnp.float32)
    ret_queries = jnp.einsum(
        "bgqd,gr->brqd",
        grouped,
        select_ret.astype(jnp.bfloat16),
        preferred_element_type=jnp.float32,
    ).astype(jnp.bfloat16)
    str_queries = jnp.einsum(
        "bgqd,gr->brqd",
        grouped,
        select_str.astype(jnp.bfloat16),
        preferred_element_type=jnp.float32,
    ).astype(jnp.bfloat16)
    score_scale = head_dim ** (-0.5)
    cache_block = ret_keys.shape[2]
    cache_pos = position * cache_block + jnp.arange(cache_block)
    ret_visible = (cache_pos[None, :] < cache_len[:, None])[:, None, None, :]
    slot_block = stream_keys.shape[2]
    slot_pos = (position * slot_block + jnp.arange(slot_block))[None, :]
    sink_part = slot_pos < sink_len[:, None]
    recent_part = (slot_pos >= SINK_CAP) & (slot_pos < SINK_CAP + window_len[:, None])
    str_visible = (sink_part | recent_part)[:, None, None, :]
    ret_peak, ret_total, ret_out = block_stats(
        ret_queries, ret_keys, ret_values, ret_visible, score_scale
    )
    str_peak, str_total, str_out = block_stats(
        str_queries, stream_keys, stream_values, str_visible, score_scale
    )
    peak_all = spread_rows(ret_peak, select_ret) + spread_rows(str_peak, select_str)
    total_all = spread_rows(ret_total, select_ret) + spread_rows(str_total, select_str)
    out_all = spread_vectors(ret_out, select_ret) + spread_vectors(str_out, select_str)
    token_of_row = jnp.arange(query_rows) // group_size
    new_visible = jnp.arange(drafts)[None, :] <= token_of_row[:, None]
    new_peak, new_total, new_out = block_stats(
        grouped, new_keys, new_values, new_visible, score_scale
    )
    own_width = out_weight.shape[0]
    block_heads = max(1, own_width // head_dim)

    def by_token(value):
        split = value.reshape(requests, kv_heads, drafts, group_size, -1)
        return split.transpose(0, 2, 1, 3, 4).reshape(tokens, head_count, -1)

    first_head = (jnp.arange(devices) * own_width) // head_dim
    block_head = first_head[:, None] + jnp.arange(block_heads)[None, :]

    def head_blocks(value):
        rows = by_token(value).reshape(tokens, head_count)
        return jnp.take(rows, block_head.reshape(-1), axis=1).reshape(tokens, devices, -1).transpose(1, 0, 2)

    received = exchanged(
        jnp.concatenate(
            [
                column_blocks(by_token(out_all).reshape(tokens, -1), devices),
                head_blocks(peak_all),
                head_blocks(total_all),
            ],
            axis=-1,
        )
    )
    got_out = received[..., :own_width].reshape(devices, tokens, block_heads, -1)
    got_peak = received[..., own_width : own_width + block_heads]
    got_total = received[..., own_width + block_heads :]

    def own_heads(value):
        blocks = column_blocks(by_token(value).reshape(tokens, -1), devices)
        return lax.dynamic_index_in_dim(blocks, position, 0, False).reshape(tokens, block_heads, -1)

    own_new_out = own_heads(new_out)
    own_new_peak = lax.dynamic_index_in_dim(head_blocks(new_peak), position, 0, False)
    own_new_total = lax.dynamic_index_in_dim(head_blocks(new_total), position, 0, False)
    top_score = jnp.maximum(jnp.max(got_peak, axis=0), own_new_peak)
    cache_factor = jnp.exp(got_peak - top_score[None])
    new_factor = jnp.exp(own_new_peak - top_score)
    denominator = jnp.sum(got_total * cache_factor, axis=0) + own_new_total * new_factor
    attended = (
        jnp.sum(got_out * cache_factor[..., None], axis=0) + own_new_out * new_factor[..., None]
    ) / denominator[..., None]
    own_attention = attended.reshape(tokens, own_width).astype(jnp.bfloat16)
    part_output = jnp.dot(own_attention, out_weight, preferred_element_type=jnp.float32)
    own_output = jnp.sum(exchanged(column_blocks(part_output, devices)), axis=0)
    layer_output = own_output.reshape(requests, drafts, local_width).astype(jnp.bfloat16)
    return (layer_output, new_entries.reshape(requests, drafts, 2 * kv_heads * head_dim))


def flat_tokens(ref):
    return jnp.concatenate([ref[b].astype(jnp.float32) for b in range(ref.shape[0])], axis=0)


def squares_kernel(hidden_ref, out_ref):
    rows = flat_tokens(hidden_ref)
    out_ref[...] = jnp.broadcast_to(jnp.sum(rows * rows, axis=1, keepdims=True), out_ref.shape)


def from_peers(value, low, radix):
    devices = lax.axis_size("seq")
    return [
        lax.ppermute(value, "seq", [(i, i ^ (low * step)) for i in range(devices)])
        for step in range(1, radix)
    ]


def projection_kernel(width, parts, *refs):
    squares = refs[:parts]
    hidden_ref, gain_ref, query_ref, fresh_ref, out_ref = refs[parts:]
    total = squares[0][...]
    for ref in squares[1:]:
        total = total + ref[...]
    inverse = lax.rsqrt(total[:, :1] / width + epsilon)
    gain = gain_ref[...].astype(jnp.float32)
    normed = (flat_tokens(hidden_ref) * inverse * gain).astype(jnp.bfloat16)
    tokens = normed.shape[0]
    chunks, _, lanes = out_ref.shape
    query_width = query_ref.shape[1] // chunks
    pieces = query_width // lanes
    for chunk in range(chunks):
        part = jnp.dot(
            normed,
            query_ref[:, chunk * query_width : (chunk + 1) * query_width],
            preferred_element_type=jnp.float32,
        )
        for piece in range(pieces):
            out_ref[chunk, piece * tokens : (piece + 1) * tokens, :] = part[
                :, piece * lanes : (piece + 1) * lanes
            ]
        out_ref[chunk, pieces * tokens :, :] = jnp.dot(
            normed,
            fresh_ref[:, chunk * lanes : (chunk + 1) * lanes],
            preferred_element_type=jnp.float32,
        )


def round_kernel(parts_ref, out_ref):
    total = jnp.sum(parts_ref[...], axis=0).astype(jnp.bfloat16)
    for target in range(out_ref.shape[0]):
        out_ref[target] = total


def head_of(table_ref, kv_heads, flag, rank):
    found, before = jnp.int32(0), jnp.int32(0)
    for head in range(kv_heads):
        is_kind = table_ref[head] == flag
        found = jnp.where(is_kind & (before == rank), head, found)
        before = before + is_kind.astype(jnp.int32)
    return found


def diagonal_of(rows, lanes):
    return lax.broadcasted_iota(jnp.int32, (rows, lanes), 0) == lax.broadcasted_iota(
        jnp.int32, (rows, lanes), 1
    )


def as_row(column, lanes):
    return jnp.sum(
        jnp.where(diagonal_of(column.shape[0], lanes), column, 0.0), axis=0, keepdims=True
    )


def as_column(row, rows):
    return jnp.sum(jnp.where(diagonal_of(rows, row.shape[1]), row, 0.0), axis=1, keepdims=True)


def masked_weights(scores, visible):
    scores = jnp.where(visible, scores, floor_score)
    peak = jnp.max(scores, axis=1, keepdims=True)
    weights = jnp.exp(scores - jnp.maximum(peak, 0.5 * floor_score))
    return peak, jnp.sum(weights, axis=1, keepdims=True), weights.astype(jnp.bfloat16)


def dot_keys(queries, keys):
    return lax.dot_general(
        queries, keys, (((1,), (1,)), ((), ())), preferred_element_type=jnp.float32
    )


def stat_rows(peak, total, lanes, sublanes):
    pad = jnp.zeros((sublanes - 2, lanes), jnp.float32)
    return jnp.concatenate([as_row(peak, lanes), as_row(total, lanes), pad], axis=0)


def attention_kernel(
    kv_heads,
    drafts,
    table_ref,
    entries_ref,
    str_key_ref,
    str_value_ref,
    far_key_ref,
    far_value_ref,
    out_ref,
    ret_key_ref,
    ret_value_ref,
    key_sem,
    value_sem,
):
    requests, retrieval, block, head_dim = ret_key_ref.shape

    def fetches(rank):
        return [
            pltpu.make_async_copy(far.at[:, rank], near.at[:, rank], sem.at[rank])
            for far, near, sem in (
                (far_key_ref, ret_key_ref, key_sem),
                (far_value_ref, ret_value_ref, value_sem),
            )
        ]

    for rank in range(retrieval):
        for fetch in fetches(rank):
            fetch.start()
    tokens = requests * drafts
    chunks, all_rows, _ = entries_ref.shape
    head_rows = all_rows - tokens
    per_head = chunks // kv_heads
    rows = per_head * head_rows
    position = table_ref[kv_heads + 3 * requests]
    row = lax.broadcasted_iota(jnp.int32, (rows, 1), 0)
    request_of_row = (row % tokens) // drafts

    def by_request(values):
        picked = values[0]
        for b in range(1, requests):
            picked = jnp.where(request_of_row == b, values[b], picked)
        return picked

    def limit(which):
        return by_request([table_ref[kv_heads + which * requests + b] for b in range(requests)])

    def one(flag, rank, keys, values, visible):
        head = head_of(table_ref, kv_heads, flag, rank)
        queries = jnp.concatenate(
            [entries_ref[head * per_head + half, :head_rows, :] for half in range(per_head)], axis=0
        )
        own = [jnp.where(request_of_row == b, queries, 0) for b in range(requests)]
        scores = dot_keys(jnp.concatenate(own, axis=1), jnp.concatenate(keys(), axis=1))
        peak, total, weights = masked_weights(scores * head_dim ** (-0.5), visible)
        mixed = jnp.dot(
            weights, jnp.concatenate(values(), axis=1), preferred_element_type=jnp.float32
        )
        mixed = by_request([mixed[:, b * head_dim : (b + 1) * head_dim] for b in range(requests)])
        for half in range(per_head):
            span = slice(half * head_rows, (half + 1) * head_rows)
            out_ref[head * per_head + half, :head_rows, :] = mixed[span]
            out_ref[head * per_head + half, head_rows:, :] = stat_rows(
                peak[span], total[span], head_dim, tokens
            )

    def reader(ref, rank, fetch=None):
        def read():
            if fetch is not None:
                fetch.wait()
            return [ref[b, rank] for b in range(requests)]

        return read

    slots = str_key_ref.shape[2]
    slot = position * slots + lax.broadcasted_iota(jnp.int32, (rows, slots), 1)
    recent = (slot >= SINK_CAP) & (slot < SINK_CAP + limit(2))
    held = (slot < limit(1)) | recent
    for rank in range(str_key_ref.shape[1]):
        one(0, rank, reader(str_key_ref, rank), reader(str_value_ref, rank), held)
    place = position * block + lax.broadcasted_iota(jnp.int32, (rows, block), 1)
    filled = place < limit(0)
    for rank in range(retrieval):
        key_fetch, value_fetch = fetches(rank)
        one(
            1,
            rank,
            reader(ret_key_ref, rank, key_fetch),
            reader(ret_value_ref, rank, value_fetch),
            filled,
        )


def fresh_kernel(kv_heads, requests, drafts, table_ref, entries_ref, out_ref):
    position = table_ref[kv_heads + 3 * requests]
    tokens = requests * drafts
    chunks, all_rows, head_dim = entries_ref.shape
    rows = all_rows - tokens
    head = position // (chunks // kv_heads)
    queries = entries_ref[position, :rows, :]
    keys = entries_ref[head, rows:, :]
    values = entries_ref[kv_heads + head, rows:, :]
    of_row = lax.broadcasted_iota(jnp.int32, (rows, tokens), 0) % tokens
    of_key = lax.broadcasted_iota(jnp.int32, (rows, tokens), 1)
    visible = (of_row // drafts == of_key // drafts) & (of_key <= of_row)
    peak, total, weights = masked_weights(dot_keys(queries, keys) * head_dim ** (-0.5), visible)
    out_ref[:rows, :] = jnp.dot(weights, values, preferred_element_type=jnp.float32)
    out_ref[rows:, :] = stat_rows(peak, total, head_dim, tokens)


def output_kernel(tokens, parts_ref, fresh_ref, far_ref, out_ref, weight_ref, weight_sem):
    pieces = weight_sem.shape[0]
    piece_width = weight_ref.shape[1] // pieces

    def fetch(piece):
        span = pl.ds(piece * piece_width, piece_width)
        return pltpu.make_async_copy(
            far_ref.at[:, span], weight_ref.at[:, span], weight_sem.at[piece]
        )

    for piece in range(pieces):
        fetch(piece).start()
    sources, all_rows, head_dim = parts_ref.shape
    rows = all_rows - tokens
    peaks = jnp.concatenate([parts_ref[s, rows : rows + 1, :] for s in range(sources)], axis=0)
    totals = jnp.concatenate(
        [parts_ref[s, rows + 1 : rows + 2, :] for s in range(sources)], axis=0
    )
    new_peak = fresh_ref[rows : rows + 1, :]
    top = jnp.maximum(jnp.max(peaks, axis=0, keepdims=True), new_peak)
    factors = jnp.exp(peaks - top)
    new_factor = jnp.exp(new_peak - top)
    denominator = (
        jnp.sum(factors * totals, axis=0, keepdims=True)
        + new_factor * fresh_ref[rows + 1 : rows + 2, :]
    )
    numerator = as_column(new_factor, rows) * fresh_ref[:rows, :]
    for s in range(sources):
        numerator = numerator + as_column(factors[s : s + 1], rows) * parts_ref[s, :rows, :]
    attended = numerator / as_column(denominator, rows)
    attention = jnp.concatenate(
        [attended[r : r + tokens] for r in range(0, rows, tokens)], axis=1
    ).astype(jnp.bfloat16)
    chunks, _, width = out_ref.shape
    for chunk in range(chunks):
        if chunk * width % piece_width == 0:
            fetch(chunk * width // piece_width).wait()
        out_ref[chunk] = jnp.dot(
            attention,
            weight_ref[:, chunk * width : (chunk + 1) * width],
            preferred_element_type=jnp.float32,
        )


def on_core(kernel, out_shape, limit, *args, streamed=(), scratch=(), cost=None):
    vmem = pl.BlockSpec(memory_space=pltpu.VMEM)
    smem = pl.BlockSpec(memory_space=pltpu.SMEM)
    scalars = [arg.dtype == jnp.int32 for arg in args]
    placed = [
        arg if scalar else pltpu.with_memory_space_constraint(arg, pltpu.VMEM)
        for arg, scalar in zip(args, scalars)
    ]
    specs = [smem if scalar else vmem for scalar in scalars]
    return pl.pallas_call(
        kernel,
        out_shape=out_shape,
        in_specs=specs + [pl.BlockSpec(memory_space=pltpu.HBM)] * len(streamed),
        scratch_shapes=scratch,
        compiler_params=pltpu.CompilerParams(vmem_limit_bytes=limit * 2**20),
        cost_estimate=cost,
    )(*placed, *(pltpu.with_memory_space_constraint(arg, pltpu.HBM) for arg in streamed))


def shaped(*shape, dtype=jnp.float32):
    return jax.ShapeDtypeStruct(shape, dtype)


def per_device_heads(
    hidden,
    norm_gain,
    q_weight,
    kv_weight,
    out_weight,
    head_kind,
    ret_keys,
    ret_values,
    stream_keys,
    stream_values,
    cache_len,
    sink_len,
    window_len,
):
    requests, drafts, local_width = hidden.shape
    kv_heads = head_kind.shape[0]
    head_dim = ret_keys.shape[3]
    devices = lax.axis_size("seq")
    position = lax.axis_index("seq")
    tokens = requests * drafts
    query_width = q_weight.shape[1] // devices
    rows = tokens * (query_width // head_dim)
    table = jnp.concatenate(
        [head_kind, cache_len, sink_len, window_len, position.astype(jnp.int32)[None]]
    )

    squares = on_core(
        squares_kernel,
        shaped(tokens, head_dim),
        4,
        hidden,
        cost=pl.CostEstimate(
            flops=2 * tokens * devices * devices * q_weight.size, bytes_accessed=hidden.size, transcendentals=0
        ),
    )
    near = min(4, devices)
    squares = functools.reduce(jnp.add, from_peers(squares, 1, near), squares)
    parts = [squares, *from_peers(squares, near, devices // near)]
    gain = norm_gain[None, :]
    part_entries = on_core(
        functools.partial(projection_kernel, local_width * devices, len(parts)),
        shaped(devices, rows + tokens, head_dim),
        8,
        *parts,
        hidden,
        gain,
        q_weight,
        kv_weight,
    )
    own_entries = on_core(
        round_kernel,
        shaped(*part_entries.shape, dtype=jnp.bfloat16),
        4,
        exchanged(part_entries),
    )
    entries = exchanged(own_entries)
    new_entries = entries[:, rows:, :].transpose(1, 0, 2).reshape(requests, drafts, -1)

    part_out = on_core(
        functools.partial(attention_kernel, kv_heads, drafts),
        shaped(devices, rows + tokens, head_dim),
        16,
        table,
        entries,
        stream_keys,
        stream_values,
        streamed=(ret_keys, ret_values),
        scratch=[
            pltpu.VMEM(ret_keys.shape, ret_keys.dtype),
            pltpu.VMEM(ret_values.shape, ret_values.dtype),
            pltpu.SemaphoreType.DMA((ret_keys.shape[1],)),
            pltpu.SemaphoreType.DMA((ret_keys.shape[1],)),
        ],
    )
    received = exchanged(part_out)
    fresh = on_core(
        functools.partial(fresh_kernel, kv_heads, requests, drafts),
        shaped(rows + tokens, head_dim),
        4,
        table,
        entries,
    )
    part_output = on_core(
        functools.partial(output_kernel, tokens),
        shaped(devices, tokens, out_weight.shape[1] // devices),
        16,
        received,
        fresh,
        streamed=(out_weight,),
        scratch=[
            pltpu.VMEM(out_weight.shape, out_weight.dtype),
            pltpu.SemaphoreType.DMA((max(1, devices // 2),)),
        ],
    )
    own_output = jnp.sum(exchanged(part_output), axis=0)
    layer_output = own_output.reshape(requests, drafts, local_width).astype(jnp.bfloat16)
    return (layer_output, new_entries)


def per_device(*args):
    hidden, _, q_weight, kv_weight, _, head_kind, ret_keys, _, stream_keys = args[:9]
    devices = lax.axis_size("seq")
    kv_heads, head_dim = head_kind.shape[0], ret_keys.shape[3]
    whole_heads = (
        (hidden.shape[0] * hidden.shape[1]) % 8 == 0
        and q_weight.shape[1] % (devices * head_dim) == 0
        and kv_weight.shape[1] == devices * head_dim
        and devices == 2 * kv_heads
        and ret_keys.shape[1] == stream_keys.shape[1]
    )
    return (per_device_heads if whole_heads else per_device_any)(*args)


def solution(mesh):
    in_specs = (
        P("groups", None, "seq"),
        P("seq"),
        P("seq", None),
        P("seq", None),
        P("seq", None),
        P(),
        P("groups", None, "seq", None),
        P("groups", None, "seq", None),
        P("groups", None, "seq", None),
        P("groups", None, "seq", None),
        P("groups"),
        P("groups"),
        P("groups"),
    )
    out_specs = (P("groups", None, "seq"), P("groups", None, None))
    return jax.shard_map(
        per_device, mesh=mesh, in_specs=in_specs, out_specs=out_specs, check_vma=False
    )
```

```python
import functools

import jax
import jax.numpy as jnp
from jax import lax
from jax.experimental import pallas as pl
from jax.experimental.pallas import tpu as pltpu
from jax.sharding import PartitionSpec as P


SINK_CAP = 128


epsilon = 1e-05
floor_score = -1e30


def exchanged(parts):
    return lax.all_to_all(parts, "seq", 0, 0, tiled=True)


def summed_over_devices(value):
    devices = lax.axis_size("seq")
    step = 1
    while step < devices:
        value = value + lax.ppermute(value, "seq", [(i, i ^ step) for i in range(devices)])
        step *= 2
    return value


def column_blocks(rows, blocks):
    return rows.reshape(rows.shape[0], blocks, -1).transpose(1, 0, 2)


def block_stats(queries, cache_keys, cache_values, visible, score_scale):
    scores = (
        jnp.einsum("bhqd,bhld->bhql", queries, cache_keys, preferred_element_type=jnp.float32)
        * score_scale
    )
    scores = jnp.where(visible, scores, floor_score)
    peak_score = jnp.max(scores, axis=-1)
    weights = jnp.where(visible, jnp.exp(scores - peak_score[..., None]), 0.0)
    weight_total = jnp.sum(weights, axis=-1)
    block_out = jnp.einsum(
        "bhql,bhld->bhqd",
        weights.astype(jnp.bfloat16),
        cache_values,
        preferred_element_type=jnp.float32,
    )
    return (peak_score, weight_total, block_out)


def spread_rows(values_in, selector):
    return jnp.einsum("brq,gr->bgq", values_in, selector, precision=lax.Precision.HIGHEST)


def spread_vectors(values_in, selector):
    return jnp.einsum("brqd,gr->bgqd", values_in, selector, precision=lax.Precision.HIGHEST)


def per_device_any(
    hidden,
    norm_gain,
    q_weight,
    kv_weight,
    out_weight,
    head_kind,
    ret_keys,
    ret_values,
    stream_keys,
    stream_values,
    cache_len,
    sink_len,
    window_len,
):
    requests, drafts, local_width = hidden.shape
    kv_heads = head_kind.shape[0]
    head_dim = ret_keys.shape[3]
    retrieval = ret_keys.shape[1]
    running = stream_keys.shape[1]
    head_count = q_weight.shape[1] // head_dim
    group_size = head_count // kv_heads
    query_rows = drafts * group_size
    devices = lax.axis_size("seq")
    position = lax.axis_index("seq")
    tokens = requests * drafts
    hidden32 = hidden.astype(jnp.float32)
    squares = summed_over_devices(jnp.sum(hidden32 * hidden32, axis=-1))
    inverse = lax.rsqrt(squares / (local_width * devices) + epsilon)
    normed = (hidden32 * inverse[..., None] * norm_gain.astype(jnp.float32)).astype(jnp.bfloat16)
    flat_rows = normed.reshape(tokens, local_width)
    part_query = jnp.dot(flat_rows, q_weight, preferred_element_type=jnp.float32)
    part_fresh = jnp.dot(flat_rows, kv_weight, preferred_element_type=jnp.float32)
    sums = jnp.sum(
        exchanged(
            jnp.concatenate(
                [column_blocks(part_query, devices), column_blocks(part_fresh, devices)], axis=-1
            )
        ),
        axis=0,
    ).astype(jnp.bfloat16)
    gathered = exchanged(jnp.broadcast_to(sums[None], (devices, *sums.shape)))
    query_width = q_weight.shape[1] // devices
    queries = gathered[..., :query_width].transpose(1, 0, 2).reshape(tokens, -1)
    new_entries = gathered[..., query_width:].transpose(1, 0, 2).reshape(tokens, -1)
    grouped = (
        queries.reshape(requests, drafts, kv_heads, group_size, head_dim)
        .transpose(0, 2, 1, 3, 4)
        .reshape(requests, kv_heads, query_rows, head_dim)
    )
    fresh_split = new_entries.reshape(requests, drafts, 2, kv_heads, head_dim)
    new_keys = fresh_split[:, :, 0].transpose(0, 2, 1, 3)
    new_values = fresh_split[:, :, 1].transpose(0, 2, 1, 3)
    kind_flag = head_kind == 1
    rank_ret = jnp.cumsum(head_kind) - 1
    rank_str = jnp.cumsum(1 - head_kind) - 1
    select_ret = (
        kind_flag[:, None] & (rank_ret[:, None] == jnp.arange(retrieval)[None, :])
    ).astype(jnp.float32)
    select_str = (
        jnp.logical_not(kind_flag)[:, None] & (rank_str[:, None] == jnp.arange(running)[None, :])
    ).astype(jnp.float32)
    ret_queries = jnp.einsum(
        "bgqd,gr->brqd",
        grouped,
        select_ret.astype(jnp.bfloat16),
        preferred_element_type=jnp.float32,
    ).astype(jnp.bfloat16)
    str_queries = jnp.einsum(
        "bgqd,gr->brqd",
        grouped,
        select_str.astype(jnp.bfloat16),
        preferred_element_type=jnp.float32,
    ).astype(jnp.bfloat16)
    score_scale = head_dim ** (-0.5)
    cache_block = ret_keys.shape[2]
    cache_pos = position * cache_block + jnp.arange(cache_block)
    ret_visible = (cache_pos[None, :] < cache_len[:, None])[:, None, None, :]
    slot_block = stream_keys.shape[2]
    slot_pos = (position * slot_block + jnp.arange(slot_block))[None, :]
    sink_part = slot_pos < sink_len[:, None]
    recent_part = (slot_pos >= SINK_CAP) & (slot_pos < SINK_CAP + window_len[:, None])
    str_visible = (sink_part | recent_part)[:, None, None, :]
    ret_peak, ret_total, ret_out = block_stats(
        ret_queries, ret_keys, ret_values, ret_visible, score_scale
    )
    str_peak, str_total, str_out = block_stats(
        str_queries, stream_keys, stream_values, str_visible, score_scale
    )
    peak_all = spread_rows(ret_peak, select_ret) + spread_rows(str_peak, select_str)
    total_all = spread_rows(ret_total, select_ret) + spread_rows(str_total, select_str)
    out_all = spread_vectors(ret_out, select_ret) + spread_vectors(str_out, select_str)
    token_of_row = jnp.arange(query_rows) // group_size
    new_visible = jnp.arange(drafts)[None, :] <= token_of_row[:, None]
    new_peak, new_total, new_out = block_stats(
        grouped, new_keys, new_values, new_visible, score_scale
    )
    own_width = out_weight.shape[0]
    block_heads = max(1, own_width // head_dim)

    def by_token(value):
        split = value.reshape(requests, kv_heads, drafts, group_size, -1)
        return split.transpose(0, 2, 1, 3, 4).reshape(tokens, head_count, -1)

    first_head = (jnp.arange(devices) * own_width) // head_dim
    block_head = first_head[:, None] + jnp.arange(block_heads)[None, :]

    def head_blocks(value):
        rows = by_token(value).reshape(tokens, head_count)
        return jnp.take(rows, block_head.reshape(-1), axis=1).reshape(tokens, devices, -1).transpose(1, 0, 2)

    received = exchanged(
        jnp.concatenate(
            [
                column_blocks(by_token(out_all).reshape(tokens, -1), devices),
                head_blocks(peak_all),
                head_blocks(total_all),
            ],
            axis=-1,
        )
    )
    got_out = received[..., :own_width].reshape(devices, tokens, block_heads, -1)
    got_peak = received[..., own_width : own_width + block_heads]
    got_total = received[..., own_width + block_heads :]

    def own_heads(value):
        blocks = column_blocks(by_token(value).reshape(tokens, -1), devices)
        return lax.dynamic_index_in_dim(blocks, position, 0, False).reshape(tokens, block_heads, -1)

    own_new_out = own_heads(new_out)
    own_new_peak = lax.dynamic_index_in_dim(head_blocks(new_peak), position, 0, False)
    own_new_total = lax.dynamic_index_in_dim(head_blocks(new_total), position, 0, False)
    top_score = jnp.maximum(jnp.max(got_peak, axis=0), own_new_peak)
    cache_factor = jnp.exp(got_peak - top_score[None])
    new_factor = jnp.exp(own_new_peak - top_score)
    denominator = jnp.sum(got_total * cache_factor, axis=0) + own_new_total * new_factor
    attended = (
        jnp.sum(got_out * cache_factor[..., None], axis=0) + own_new_out * new_factor[..., None]
    ) / denominator[..., None]
    own_attention = attended.reshape(tokens, own_width).astype(jnp.bfloat16)
    part_output = jnp.dot(own_attention, out_weight, preferred_element_type=jnp.float32)
    own_output = jnp.sum(exchanged(column_blocks(part_output, devices)), axis=0)
    layer_output = own_output.reshape(requests, drafts, local_width).astype(jnp.bfloat16)
    return (layer_output, new_entries.reshape(requests, drafts, 2 * kv_heads * head_dim))


def flat_tokens(ref):
    return jnp.concatenate([ref[b].astype(jnp.float32) for b in range(ref.shape[0])], axis=0)


def squares_kernel(hidden_ref, out_ref):
    rows = flat_tokens(hidden_ref)
    out_ref[...] = jnp.broadcast_to(jnp.sum(rows * rows, axis=1, keepdims=True), out_ref.shape)


def from_peers(value, low, radix):
    devices = lax.axis_size("seq")
    return [
        lax.ppermute(value, "seq", [(i, i ^ (low * step)) for i in range(devices)])
        for step in range(1, radix)
    ]


def projection_kernel(width, parts, *refs):
    squares = refs[:parts]
    hidden_ref, gain_ref, query_ref, fresh_ref, out_ref = refs[parts:]
    total = squares[0][...]
    for ref in squares[1:]:
        total = total + ref[...]
    inverse = lax.rsqrt(total[:, :1] / width + epsilon)
    gain = gain_ref[...].astype(jnp.float32)
    normed = (flat_tokens(hidden_ref) * inverse * gain).astype(jnp.bfloat16)
    tokens = normed.shape[0]
    chunks, _, lanes = out_ref.shape
    query_width = query_ref.shape[1] // chunks
    pieces = query_width // lanes
    for chunk in range(chunks):
        part = jnp.dot(
            normed,
            query_ref[:, chunk * query_width : (chunk + 1) * query_width],
            preferred_element_type=jnp.float32,
        )
        for piece in range(pieces):
            out_ref[chunk, piece * tokens : (piece + 1) * tokens, :] = part[
                :, piece * lanes : (piece + 1) * lanes
            ]
        out_ref[chunk, pieces * tokens :, :] = jnp.dot(
            normed,
            fresh_ref[:, chunk * lanes : (chunk + 1) * lanes],
            preferred_element_type=jnp.float32,
        )


def round_kernel(parts_ref, out_ref):
    total = jnp.sum(parts_ref[...], axis=0).astype(jnp.bfloat16)
    for target in range(out_ref.shape[0]):
        out_ref[target] = total


def head_of(table_ref, kv_heads, flag, rank):
    found, before = jnp.int32(0), jnp.int32(0)
    for head in range(kv_heads):
        is_kind = table_ref[head] == flag
        found = jnp.where(is_kind & (before == rank), head, found)
        before = before + is_kind.astype(jnp.int32)
    return found


def diagonal_of(rows, lanes):
    return lax.broadcasted_iota(jnp.int32, (rows, lanes), 0) == lax.broadcasted_iota(
        jnp.int32, (rows, lanes), 1
    )


def as_row(column, lanes):
    return jnp.sum(
        jnp.where(diagonal_of(column.shape[0], lanes), column, 0.0), axis=0, keepdims=True
    )


def as_column(row, rows):
    return jnp.sum(jnp.where(diagonal_of(rows, row.shape[1]), row, 0.0), axis=1, keepdims=True)


def masked_weights(scores, visible):
    scores = jnp.where(visible, scores, floor_score)
    peak = jnp.max(scores, axis=1, keepdims=True)
    weights = jnp.exp(scores - jnp.maximum(peak, 0.5 * floor_score))
    return peak, jnp.sum(weights, axis=1, keepdims=True), weights.astype(jnp.bfloat16)


def dot_keys(queries, keys):
    return lax.dot_general(
        queries, keys, (((1,), (1,)), ((), ())), preferred_element_type=jnp.float32
    )


def thirds(row):
    rest, pieces = row, []
    for _ in range(3):
        pieces.append(rest.astype(jnp.bfloat16))
        rest = rest - pieces[-1].astype(jnp.float32)
    return pieces


def stat_rows(peak, total, lanes, sublanes):
    pieces = [*thirds(as_row(peak, lanes)), *thirds(as_row(total, lanes))]
    wide = [piece.astype(jnp.float32) for piece in pieces]
    pad = jnp.zeros((sublanes - len(wide), lanes), jnp.float32)
    return jnp.concatenate([*wide, pad], axis=0)


def joined_thirds(rows):
    return (rows[0] + rows[1]) + rows[2]


def head_start_kernel(table_ref, far_key_ref, key_ref, sem):
    fetch = pltpu.make_async_copy(far_key_ref.at[:, pl.ds(0, key_ref.shape[1])], key_ref, sem)
    fetch.start()
    fetch.wait()


def attention_kernel(
    kv_heads,
    drafts,
    table_ref,
    entries_ref,
    first_key_ref,
    str_key_ref,
    str_value_ref,
    far_key_ref,
    far_value_ref,
    out_ref,
    rest_key_ref,
    ret_value_ref,
    key_sem,
    value_sem,
):
    requests, retrieval, block, head_dim = ret_value_ref.shape
    firsts = first_key_ref.shape[1]
    cuts = value_sem.shape[0]
    key_fetch = pltpu.make_async_copy(
        far_key_ref.at[:, pl.ds(firsts, retrieval - firsts)], rest_key_ref, key_sem
    )

    def span_of(cut):
        return pl.ds(cut * (block // cuts), block // cuts)

    def value_fetch(cut):
        return pltpu.make_async_copy(
            far_value_ref.at[:, :, span_of(cut)], ret_value_ref.at[:, :, span_of(cut)], value_sem.at[cut]
        )

    key_fetch.start()
    for cut in range(cuts):
        value_fetch(cut).start()
    tokens = requests * drafts
    chunks, all_rows, _ = entries_ref.shape
    head_rows = all_rows - tokens
    per_head = chunks // kv_heads
    rows = per_head * head_rows
    position = table_ref[kv_heads + 3 * requests]
    row = lax.broadcasted_iota(jnp.int32, (rows, 1), 0)
    request_of_row = (row % tokens) // drafts

    def by_request(values):
        picked = values[0]
        for b in range(1, requests):
            picked = jnp.where(request_of_row == b, values[b], picked)
        return picked

    def limit(which):
        return by_request([table_ref[kv_heads + which * requests + b] for b in range(requests)])

    def weighed(flag, rank, keys, visible):
        head = head_of(table_ref, kv_heads, flag, rank)
        queries = jnp.concatenate(
            [entries_ref[head * per_head + half, :head_rows, :] for half in range(per_head)], axis=0
        )
        own = [jnp.where(request_of_row == b, queries, 0) for b in range(requests)]
        scores = dot_keys(jnp.concatenate(own, axis=1), jnp.concatenate(keys, axis=1))
        return head, *masked_weights(scores * head_dim ** (-0.5), visible)

    def mix(weights, values):
        return jnp.dot(
            weights, jnp.concatenate(values, axis=1), preferred_element_type=jnp.float32
        )

    def store(head, peak, total, mixed):
        mixed = by_request([mixed[:, b * head_dim : (b + 1) * head_dim] for b in range(requests)])
        for half in range(per_head):
            span = slice(half * head_rows, (half + 1) * head_rows)
            block_rows = jnp.concatenate(
                [mixed[span], stat_rows(peak[span], total[span], head_dim, tokens)], axis=0
            )
            out_ref[head * per_head + half] = block_rows.astype(jnp.bfloat16)

    def of_rank(ref, rank):
        return [ref[b, rank] for b in range(requests)]

    slots = str_key_ref.shape[2]
    slot = position * slots + lax.broadcasted_iota(jnp.int32, (rows, slots), 1)
    recent = (slot >= SINK_CAP) & (slot < SINK_CAP + limit(2))
    held = (slot < limit(1)) | recent
    running = range(str_key_ref.shape[1])
    ready = [weighed(0, rank, of_rank(str_key_ref, rank), held) for rank in running]
    for rank in running:
        head, peak, total, weights = ready[rank]
        store(head, peak, total, mix(weights, of_rank(str_value_ref, rank)))
    place = position * block + lax.broadcasted_iota(jnp.int32, (rows, block), 1)
    filled = place < limit(0)
    ready = [weighed(1, rank, of_rank(first_key_ref, rank), filled) for rank in range(firsts)]
    key_fetch.wait()
    ready += [
        weighed(1, rank, of_rank(rest_key_ref, rank - firsts), filled)
        for rank in range(firsts, retrieval)
    ]
    mixed = [0.0] * retrieval
    for cut in range(cuts):
        value_fetch(cut).wait()
        low, size = cut * (block // cuts), block // cuts
        for rank in range(retrieval):
            values = [ret_value_ref[b, rank, low : low + size, :] for b in range(requests)]
            mixed[rank] = mixed[rank] + mix(ready[rank][3][:, low : low + size], values)
    for rank in range(retrieval):
        store(*ready[rank][:3], mixed[rank])


def fresh_kernel(
    kv_heads, requests, drafts, table_ref, entries_ref, far_ref, out_ref, weight_ref, sem
):
    fetch = pltpu.make_async_copy(far_ref.at[:, pl.ds(0, weight_ref.shape[1])], weight_ref, sem)
    fetch.start()
    position = table_ref[kv_heads + 3 * requests]
    tokens = requests * drafts
    chunks, all_rows, head_dim = entries_ref.shape
    rows = all_rows - tokens
    head = position // (chunks // kv_heads)
    queries = entries_ref[position, :rows, :]
    keys = entries_ref[head, rows:, :]
    values = entries_ref[kv_heads + head, rows:, :]
    of_row = lax.broadcasted_iota(jnp.int32, (rows, tokens), 0) % tokens
    of_key = lax.broadcasted_iota(jnp.int32, (rows, tokens), 1)
    visible = (of_row // drafts == of_key // drafts) & (of_key <= of_row)
    peak, total, weights = masked_weights(dot_keys(queries, keys) * head_dim ** (-0.5), visible)
    out_ref[:rows, :] = jnp.dot(weights, values, preferred_element_type=jnp.float32)
    out_ref[rows:, :] = stat_rows(peak, total, head_dim, tokens)
    fetch.wait()


def output_kernel(
    tokens, parts_ref, fresh_ref, first_ref, far_ref, out_ref, weight_ref, weight_sem
):
    firsts = first_ref.shape[1]
    pieces = weight_sem.shape[0]
    piece_width = weight_ref.shape[1] // pieces

    def fetch(piece):
        return pltpu.make_async_copy(
            far_ref.at[:, pl.ds(firsts + piece * piece_width, piece_width)],
            weight_ref.at[:, pl.ds(piece * piece_width, piece_width)],
            weight_sem.at[piece],
        )

    for piece in range(pieces):
        fetch(piece).start()
    sources, all_rows, head_dim = parts_ref.shape
    rows = all_rows - tokens
    stats = [parts_ref[s, rows:, :].astype(jnp.float32) for s in range(sources)]
    stats.append(fresh_ref[rows:, :])

    def stacked(first):
        return joined_thirds(
            [
                jnp.concatenate([stat[r : r + 1] for stat in stats], axis=0)
                for r in range(first, first + 3)
            ]
        )

    peaks, totals = stacked(0), stacked(3)
    factors = jnp.exp(peaks - jnp.max(peaks, axis=0, keepdims=True))
    denominator = jnp.sum(factors * totals, axis=0, keepdims=True)
    numerator = as_column(factors[sources:], rows) * fresh_ref[:rows, :]
    for s in range(sources):
        part = parts_ref[s, :rows, :].astype(jnp.float32)
        numerator = numerator + as_column(factors[s : s + 1], rows) * part
    attended = numerator / as_column(denominator, rows)
    attention = jnp.concatenate(
        [attended[r : r + tokens] for r in range(0, rows, tokens)], axis=1
    ).astype(jnp.bfloat16)
    chunks, _, width = out_ref.shape
    for chunk in range(chunks):
        low = chunk * width - firsts
        if low < 0:
            weight = first_ref[:, low + firsts : low + firsts + width]
        else:
            if low % piece_width == 0:
                fetch(low // piece_width).wait()
            weight = weight_ref[:, low : low + width]
        out_ref[chunk] = jnp.dot(
            attention, weight, preferred_element_type=jnp.float32
        ).astype(jnp.bfloat16)


def on_core(kernel, out_shape, limit, *args, streamed=(), scratch=(), cost=None):
    vmem = pl.BlockSpec(memory_space=pltpu.VMEM)
    smem = pl.BlockSpec(memory_space=pltpu.SMEM)
    scalars = [arg.dtype == jnp.int32 for arg in args]
    placed = [
        arg if scalar else pltpu.with_memory_space_constraint(arg, pltpu.VMEM)
        for arg, scalar in zip(args, scalars)
    ]
    specs = [smem if scalar else vmem for scalar in scalars]
    return pl.pallas_call(
        kernel,
        out_shape=out_shape,
        in_specs=specs + [pl.BlockSpec(memory_space=pltpu.HBM)] * len(streamed),
        scratch_shapes=scratch,
        compiler_params=pltpu.CompilerParams(vmem_limit_bytes=limit * 2**20),
        cost_estimate=cost,
    )(*placed, *(pltpu.with_memory_space_constraint(arg, pltpu.HBM) for arg in streamed))


def shaped(*shape, dtype=jnp.float32):
    return jax.ShapeDtypeStruct(shape, dtype)


def per_device_heads(
    hidden,
    norm_gain,
    q_weight,
    kv_weight,
    out_weight,
    head_kind,
    ret_keys,
    ret_values,
    stream_keys,
    stream_values,
    cache_len,
    sink_len,
    window_len,
):
    requests, drafts, local_width = hidden.shape
    kv_heads = head_kind.shape[0]
    head_dim = ret_keys.shape[3]
    devices = lax.axis_size("seq")
    position = lax.axis_index("seq")
    tokens = requests * drafts
    query_width = q_weight.shape[1] // devices
    rows = tokens * (query_width // head_dim)
    table = jnp.concatenate(
        [head_kind, cache_len, sink_len, window_len, position.astype(jnp.int32)[None]]
    )

    squares = on_core(
        squares_kernel,
        shaped(tokens, head_dim),
        4,
        hidden,
        cost=pl.CostEstimate(
            flops=2 * tokens * devices * devices * q_weight.size, bytes_accessed=hidden.size, transcendentals=0
        ),
    )
    near = min(4, devices)
    squares = functools.reduce(jnp.add, from_peers(squares, 1, near), squares)
    parts = [squares, *from_peers(squares, near, devices // near)]
    gain = norm_gain[None, :]
    part_entries = on_core(
        functools.partial(projection_kernel, local_width * devices, len(parts)),
        shaped(devices, rows + tokens, head_dim),
        8,
        *parts,
        hidden,
        gain,
        q_weight,
        kv_weight,
    )
    own_entries = on_core(
        round_kernel,
        shaped(*part_entries.shape, dtype=jnp.bfloat16),
        4,
        exchanged(part_entries),
    )
    entries = exchanged(own_entries)
    new_entries = entries[:, rows:, :].transpose(1, 0, 2).reshape(requests, drafts, -1)

    retrieval = ret_keys.shape[1]
    firsts = retrieval // 2
    head_start = (requests, firsts, *ret_keys.shape[2:])
    head_rest = (requests, retrieval - firsts, *ret_keys.shape[2:])
    dma = pltpu.SemaphoreType.DMA
    first_keys = on_core(
        head_start_kernel,
        pltpu.VMEM(head_start, ret_keys.dtype),
        4,
        lax.optimization_barrier((table, own_entries))[0],
        streamed=(ret_keys,),
        scratch=[dma],
    )
    part_out = on_core(
        functools.partial(attention_kernel, kv_heads, drafts),
        shaped(devices, rows + tokens, head_dim, dtype=jnp.bfloat16),
        20,
        table,
        entries,
        first_keys,
        stream_keys,
        stream_values,
        streamed=(ret_keys, ret_values),
        scratch=[
            pltpu.VMEM(head_rest, ret_keys.dtype),
            pltpu.VMEM(ret_values.shape, ret_values.dtype),
            dma,
            dma((4,)),
        ],
    )
    received = exchanged(part_out)
    own_rows, width = out_weight.shape
    chunk_width = width // devices
    first_width = chunk_width * (devices // 4)
    fresh, first_weight = on_core(
        functools.partial(fresh_kernel, kv_heads, requests, drafts),
        (shaped(rows + tokens, head_dim), pltpu.VMEM((own_rows, first_width), out_weight.dtype)),
        4,
        table,
        entries,
        streamed=(out_weight,),
        scratch=[dma],
    )
    part_output = on_core(
        functools.partial(output_kernel, tokens),
        shaped(devices, tokens, chunk_width, dtype=jnp.bfloat16),
        16,
        received,
        fresh,
        first_weight,
        streamed=(out_weight,),
        scratch=[
            pltpu.VMEM((own_rows, width - first_width), out_weight.dtype),
            dma(((width - first_width) // (2 * chunk_width),)),
        ],
    )
    own_output = jnp.sum(exchanged(part_output).astype(jnp.float32), axis=0)
    layer_output = own_output.reshape(requests, drafts, local_width).astype(jnp.bfloat16)
    return (layer_output, new_entries)


def per_device(*args):
    hidden, _, q_weight, kv_weight, _, head_kind, ret_keys, _, stream_keys = args[:9]
    devices = lax.axis_size("seq")
    kv_heads, head_dim = head_kind.shape[0], ret_keys.shape[3]
    whole_heads = (
        (hidden.shape[0] * hidden.shape[1]) % 8 == 0
        and q_weight.shape[1] % (devices * head_dim) == 0
        and kv_weight.shape[1] == devices * head_dim
        and devices == 2 * kv_heads
        and ret_keys.shape[1] == stream_keys.shape[1]
    )
    return (per_device_heads if whole_heads else per_device_any)(*args)


def solution(mesh):
    in_specs = (
        P("groups", None, "seq"),
        P("seq"),
        P("seq", None),
        P("seq", None),
        P("seq", None),
        P(),
        P("groups", None, "seq", None),
        P("groups", None, "seq", None),
        P("groups", None, "seq", None),
        P("groups", None, "seq", None),
        P("groups"),
        P("groups"),
        P("groups"),
    )
    out_specs = (P("groups", None, "seq"), P("groups", None, None))
    return jax.shard_map(
        per_device, mesh=mesh, in_specs=in_specs, out_specs=out_specs, check_vma=False
    )
```

```python
import functools

import jax
import jax.numpy as jnp
from jax import lax
from jax.experimental import pallas as pl
from jax.experimental.pallas import tpu as pltpu
from jax.sharding import PartitionSpec as P


SINK_CAP = 128


epsilon = 1e-05
floor_score = -1e30


def exchanged(parts):
    return lax.all_to_all(parts, "seq", 0, 0, tiled=True)


def summed_over_devices(value):
    devices = lax.axis_size("seq")
    step = 1
    while step < devices:
        value = value + lax.ppermute(value, "seq", [(i, i ^ step) for i in range(devices)])
        step *= 2
    return value


def column_blocks(rows, blocks):
    return rows.reshape(rows.shape[0], blocks, -1).transpose(1, 0, 2)


def block_stats(queries, cache_keys, cache_values, visible, score_scale):
    scores = (
        jnp.einsum("bhqd,bhld->bhql", queries, cache_keys, preferred_element_type=jnp.float32)
        * score_scale
    )
    scores = jnp.where(visible, scores, floor_score)
    peak_score = jnp.max(scores, axis=-1)
    weights = jnp.where(visible, jnp.exp(scores - peak_score[..., None]), 0.0)
    weight_total = jnp.sum(weights, axis=-1)
    block_out = jnp.einsum(
        "bhql,bhld->bhqd",
        weights.astype(jnp.bfloat16),
        cache_values,
        preferred_element_type=jnp.float32,
    )
    return (peak_score, weight_total, block_out)


def spread_rows(values_in, selector):
    return jnp.einsum("brq,gr->bgq", values_in, selector, precision=lax.Precision.HIGHEST)


def spread_vectors(values_in, selector):
    return jnp.einsum("brqd,gr->bgqd", values_in, selector, precision=lax.Precision.HIGHEST)


def per_device_any(
    hidden,
    norm_gain,
    q_weight,
    kv_weight,
    out_weight,
    head_kind,
    ret_keys,
    ret_values,
    stream_keys,
    stream_values,
    cache_len,
    sink_len,
    window_len,
):
    requests, drafts, local_width = hidden.shape
    kv_heads = head_kind.shape[0]
    head_dim = ret_keys.shape[3]
    retrieval = ret_keys.shape[1]
    running = stream_keys.shape[1]
    head_count = q_weight.shape[1] // head_dim
    group_size = head_count // kv_heads
    query_rows = drafts * group_size
    devices = lax.axis_size("seq")
    position = lax.axis_index("seq")
    tokens = requests * drafts
    hidden32 = hidden.astype(jnp.float32)
    squares = summed_over_devices(jnp.sum(hidden32 * hidden32, axis=-1))
    inverse = lax.rsqrt(squares / (local_width * devices) + epsilon)
    normed = (hidden32 * inverse[..., None] * norm_gain.astype(jnp.float32)).astype(jnp.bfloat16)
    flat_rows = normed.reshape(tokens, local_width)
    part_query = jnp.dot(flat_rows, q_weight, preferred_element_type=jnp.float32)
    part_fresh = jnp.dot(flat_rows, kv_weight, preferred_element_type=jnp.float32)
    sums = jnp.sum(
        exchanged(
            jnp.concatenate(
                [column_blocks(part_query, devices), column_blocks(part_fresh, devices)], axis=-1
            )
        ),
        axis=0,
    ).astype(jnp.bfloat16)
    gathered = exchanged(jnp.broadcast_to(sums[None], (devices, *sums.shape)))
    query_width = q_weight.shape[1] // devices
    queries = gathered[..., :query_width].transpose(1, 0, 2).reshape(tokens, -1)
    new_entries = gathered[..., query_width:].transpose(1, 0, 2).reshape(tokens, -1)
    grouped = (
        queries.reshape(requests, drafts, kv_heads, group_size, head_dim)
        .transpose(0, 2, 1, 3, 4)
        .reshape(requests, kv_heads, query_rows, head_dim)
    )
    fresh_split = new_entries.reshape(requests, drafts, 2, kv_heads, head_dim)
    new_keys = fresh_split[:, :, 0].transpose(0, 2, 1, 3)
    new_values = fresh_split[:, :, 1].transpose(0, 2, 1, 3)
    kind_flag = head_kind == 1
    rank_ret = jnp.cumsum(head_kind) - 1
    rank_str = jnp.cumsum(1 - head_kind) - 1
    select_ret = (
        kind_flag[:, None] & (rank_ret[:, None] == jnp.arange(retrieval)[None, :])
    ).astype(jnp.float32)
    select_str = (
        jnp.logical_not(kind_flag)[:, None] & (rank_str[:, None] == jnp.arange(running)[None, :])
    ).astype(jnp.float32)
    ret_queries = jnp.einsum(
        "bgqd,gr->brqd",
        grouped,
        select_ret.astype(jnp.bfloat16),
        preferred_element_type=jnp.float32,
    ).astype(jnp.bfloat16)
    str_queries = jnp.einsum(
        "bgqd,gr->brqd",
        grouped,
        select_str.astype(jnp.bfloat16),
        preferred_element_type=jnp.float32,
    ).astype(jnp.bfloat16)
    score_scale = head_dim ** (-0.5)
    cache_block = ret_keys.shape[2]
    cache_pos = position * cache_block + jnp.arange(cache_block)
    ret_visible = (cache_pos[None, :] < cache_len[:, None])[:, None, None, :]
    slot_block = stream_keys.shape[2]
    slot_pos = (position * slot_block + jnp.arange(slot_block))[None, :]
    sink_part = slot_pos < sink_len[:, None]
    recent_part = (slot_pos >= SINK_CAP) & (slot_pos < SINK_CAP + window_len[:, None])
    str_visible = (sink_part | recent_part)[:, None, None, :]
    ret_peak, ret_total, ret_out = block_stats(
        ret_queries, ret_keys, ret_values, ret_visible, score_scale
    )
    str_peak, str_total, str_out = block_stats(
        str_queries, stream_keys, stream_values, str_visible, score_scale
    )
    peak_all = spread_rows(ret_peak, select_ret) + spread_rows(str_peak, select_str)
    total_all = spread_rows(ret_total, select_ret) + spread_rows(str_total, select_str)
    out_all = spread_vectors(ret_out, select_ret) + spread_vectors(str_out, select_str)
    token_of_row = jnp.arange(query_rows) // group_size
    new_visible = jnp.arange(drafts)[None, :] <= token_of_row[:, None]
    new_peak, new_total, new_out = block_stats(
        grouped, new_keys, new_values, new_visible, score_scale
    )
    own_width = out_weight.shape[0]
    block_heads = max(1, own_width // head_dim)

    def by_token(value):
        split = value.reshape(requests, kv_heads, drafts, group_size, -1)
        return split.transpose(0, 2, 1, 3, 4).reshape(tokens, head_count, -1)

    first_head = (jnp.arange(devices) * own_width) // head_dim
    block_head = first_head[:, None] + jnp.arange(block_heads)[None, :]

    def head_blocks(value):
        rows = by_token(value).reshape(tokens, head_count)
        return jnp.take(rows, block_head.reshape(-1), axis=1).reshape(tokens, devices, -1).transpose(1, 0, 2)

    received = exchanged(
        jnp.concatenate(
            [
                column_blocks(by_token(out_all).reshape(tokens, -1), devices),
                head_blocks(peak_all),
                head_blocks(total_all),
            ],
            axis=-1,
        )
    )
    got_out = received[..., :own_width].reshape(devices, tokens, block_heads, -1)
    got_peak = received[..., own_width : own_width + block_heads]
    got_total = received[..., own_width + block_heads :]

    def own_heads(value):
        blocks = column_blocks(by_token(value).reshape(tokens, -1), devices)
        return lax.dynamic_index_in_dim(blocks, position, 0, False).reshape(tokens, block_heads, -1)

    own_new_out = own_heads(new_out)
    own_new_peak = lax.dynamic_index_in_dim(head_blocks(new_peak), position, 0, False)
    own_new_total = lax.dynamic_index_in_dim(head_blocks(new_total), position, 0, False)
    top_score = jnp.maximum(jnp.max(got_peak, axis=0), own_new_peak)
    cache_factor = jnp.exp(got_peak - top_score[None])
    new_factor = jnp.exp(own_new_peak - top_score)
    denominator = jnp.sum(got_total * cache_factor, axis=0) + own_new_total * new_factor
    attended = (
        jnp.sum(got_out * cache_factor[..., None], axis=0) + own_new_out * new_factor[..., None]
    ) / denominator[..., None]
    own_attention = attended.reshape(tokens, own_width).astype(jnp.bfloat16)
    part_output = jnp.dot(own_attention, out_weight, preferred_element_type=jnp.float32)
    own_output = jnp.sum(exchanged(column_blocks(part_output, devices)), axis=0)
    layer_output = own_output.reshape(requests, drafts, local_width).astype(jnp.bfloat16)
    return (layer_output, new_entries.reshape(requests, drafts, 2 * kv_heads * head_dim))


def flat_tokens(ref):
    return jnp.concatenate([ref[b].astype(jnp.float32) for b in range(ref.shape[0])], axis=0)


def squares_kernel(hidden_ref, out_ref):
    rows = flat_tokens(hidden_ref)
    out_ref[...] = jnp.broadcast_to(jnp.sum(rows * rows, axis=1, keepdims=True), out_ref.shape)


def from_peer(value, distance):
    devices = lax.axis_size("seq")
    return lax.ppermute(value, "seq", [(i, i ^ distance) for i in range(devices)])


def from_peers(value, low, radix):
    return [from_peer(value, low * step) for step in range(1, radix)]


def paired_sum(values):
    while len(values) > 1:
        values = [left + right for left, right in zip(values[::2], values[1::2])]
    return values[0]


def chunk_of(position, near, distance, far):
    return far * near + ((position & (near - 1)) ^ distance)


def projection_kernel(width, parts, *refs):
    squares = refs[:parts]
    hidden_ref, gain_ref, query_ref, fresh_ref = refs[parts : parts + 4]
    out_refs = refs[parts + 4 :]
    total = paired_sum([ref[...] for ref in squares])
    inverse = lax.rsqrt(total[:, :1] / width + epsilon)
    gain = gain_ref[...].astype(jnp.float32)
    normed = (flat_tokens(hidden_ref) * inverse * gain).astype(jnp.bfloat16)
    tokens = normed.shape[0]
    position = lax.axis_index("seq")
    near = len(out_refs)
    far, _, lanes = out_refs[0].shape
    query_width = query_ref.shape[1] // (near * far)
    pieces = query_width // lanes

    def times(ref, chunk, size):
        columns = ref[:, pl.ds(pl.multiple_of(chunk * size, size), size)]
        return jnp.dot(normed, columns, preferred_element_type=jnp.float32)

    for distance in range(near):
        for group in range(far):
            chunk = chunk_of(position, near, distance, group)
            part = times(query_ref, chunk, query_width)
            out = out_refs[distance]
            for piece in range(pieces):
                out[group, piece * tokens : (piece + 1) * tokens, :] = part[
                    :, piece * lanes : (piece + 1) * lanes
                ]
            out[group, pieces * tokens :, :] = times(fresh_ref, chunk, lanes)


def sum_kernel(*refs):
    refs[-1][...] = paired_sum([ref[...] for ref in refs[:-1]]).astype(refs[-1].dtype)


def head_of(kind_ref, flag, rank):
    found, before = jnp.int32(0), jnp.int32(0)
    for head in range(kind_ref.shape[0]):
        is_kind = kind_ref[head] == flag
        found = jnp.where(is_kind & (before == rank), head, found)
        before = before + is_kind.astype(jnp.int32)
    return found


def diagonal_of(rows, lanes):
    return lax.broadcasted_iota(jnp.int32, (rows, lanes), 0) == lax.broadcasted_iota(
        jnp.int32, (rows, lanes), 1
    )


def as_row(column, lanes):
    return jnp.sum(
        jnp.where(diagonal_of(column.shape[0], lanes), column, 0.0), axis=0, keepdims=True
    )


def as_column(row, rows):
    return jnp.sum(jnp.where(diagonal_of(rows, row.shape[1]), row, 0.0), axis=1, keepdims=True)


def masked_weights(scores, visible):
    scores = jnp.where(visible, scores, floor_score)
    peak = jnp.max(scores, axis=1, keepdims=True)
    weights = jnp.exp(scores - jnp.maximum(peak, 0.5 * floor_score))
    return peak, jnp.sum(weights, axis=1, keepdims=True), weights.astype(jnp.bfloat16)


def dot_keys(queries, keys):
    return lax.dot_general(
        queries, keys, (((1,), (1,)), ((), ())), preferred_element_type=jnp.float32
    )


def thirds(row):
    rest, pieces = row, []
    for _ in range(3):
        pieces.append(rest.astype(jnp.bfloat16))
        rest = rest - pieces[-1].astype(jnp.float32)
    return pieces


def stat_rows(peak, total, lanes, sublanes):
    pieces = [*thirds(as_row(peak, lanes)), *thirds(as_row(total, lanes))]
    wide = [piece.astype(jnp.float32) for piece in pieces]
    pad = jnp.zeros((sublanes - len(wide), lanes), jnp.float32)
    return jnp.concatenate([*wide, pad], axis=0)


def joined_thirds(rows):
    return (rows[0] + rows[1]) + rows[2]


def attention_kernel(
    drafts,
    kind_ref,
    cache_ref,
    sink_ref,
    window_ref,
    ret_key_ref,
    ret_value_ref,
    str_key_ref,
    str_value_ref,
    *refs,
):
    *part_refs, out_ref, entries_ref = refs
    requests, retrieval, block, head_dim = ret_value_ref.shape
    position = lax.axis_index("seq")
    for distance, part_ref in enumerate(part_refs):
        for group in range(part_ref.shape[0]):
            chunk = chunk_of(position, len(part_refs), distance, group)
            entries_ref[chunk] = part_ref[group]
    tokens = requests * drafts
    chunks, all_rows, _ = entries_ref.shape
    head_rows = all_rows - tokens
    per_head = chunks // kind_ref.shape[0]
    rows = per_head * head_rows
    row = lax.broadcasted_iota(jnp.int32, (rows, 1), 0)
    request_of_row = (row % tokens) // drafts

    def by_request(values):
        picked = values[0]
        for b in range(1, requests):
            picked = jnp.where(request_of_row == b, values[b], picked)
        return picked

    def limit(ref):
        return by_request([ref[b] for b in range(requests)])

    def weighed(flag, rank, keys, visible):
        head = head_of(kind_ref, flag, rank)
        queries = jnp.concatenate(
            [entries_ref[head * per_head + half, :head_rows, :] for half in range(per_head)], axis=0
        )
        own = [jnp.where(request_of_row == b, queries, 0) for b in range(requests)]
        scores = dot_keys(jnp.concatenate(own, axis=1), jnp.concatenate(keys, axis=1))
        return head, *masked_weights(scores * head_dim ** (-0.5), visible)

    def mix(weights, values):
        return jnp.dot(
            weights, jnp.concatenate(values, axis=1), preferred_element_type=jnp.float32
        )

    def store(head, peak, total, mixed):
        mixed = by_request([mixed[:, b * head_dim : (b + 1) * head_dim] for b in range(requests)])
        for half in range(per_head):
            span = slice(half * head_rows, (half + 1) * head_rows)
            block_rows = jnp.concatenate(
                [mixed[span], stat_rows(peak[span], total[span], head_dim, tokens)], axis=0
            )
            out_ref[head * per_head + half] = block_rows.astype(jnp.bfloat16)

    def of_rank(ref, rank):
        return [ref[b, rank] for b in range(requests)]

    slots = str_key_ref.shape[2]
    slot = position * slots + lax.broadcasted_iota(jnp.int32, (rows, slots), 1)
    recent = (slot >= SINK_CAP) & (slot < SINK_CAP + limit(window_ref))
    held = (slot < limit(sink_ref)) | recent
    running = range(str_key_ref.shape[1])
    ready = [weighed(0, rank, of_rank(str_key_ref, rank), held) for rank in running]
    for rank in running:
        head, peak, total, weights = ready[rank]
        store(head, peak, total, mix(weights, of_rank(str_value_ref, rank)))
    place = position * block + lax.broadcasted_iota(jnp.int32, (rows, block), 1)
    filled = place < limit(cache_ref)
    ready = [weighed(1, rank, of_rank(ret_key_ref, rank), filled) for rank in range(retrieval)]
    for rank in range(retrieval):
        head, peak, total, weights = ready[rank]
        store(head, peak, total, mix(weights, of_rank(ret_value_ref, rank)))


def fresh_kernel(
    kv_heads, requests, drafts, entries_ref, far_ref, out_ref, weight_ref, sem
):
    fetch = pltpu.make_async_copy(far_ref.at[:, pl.ds(0, weight_ref.shape[1])], weight_ref, sem)
    fetch.start()
    position = lax.axis_index("seq")
    tokens = requests * drafts
    chunks, all_rows, head_dim = entries_ref.shape
    rows = all_rows - tokens
    head = position // (chunks // kv_heads)
    queries = entries_ref[position, :rows, :]
    keys = entries_ref[head, rows:, :]
    values = entries_ref[kv_heads + head, rows:, :]
    of_row = lax.broadcasted_iota(jnp.int32, (rows, tokens), 0) % tokens
    of_key = lax.broadcasted_iota(jnp.int32, (rows, tokens), 1)
    visible = (of_row // drafts == of_key // drafts) & (of_key <= of_row)
    peak, total, weights = masked_weights(dot_keys(queries, keys) * head_dim ** (-0.5), visible)
    out_ref[:rows, :] = jnp.dot(weights, values, preferred_element_type=jnp.float32)
    out_ref[rows:, :] = stat_rows(peak, total, head_dim, tokens)
    fetch.wait()


def output_kernel(
    tokens, parts_ref, fresh_ref, first_ref, far_ref, out_ref, weight_ref, weight_sem
):
    firsts = first_ref.shape[1]
    pieces = weight_sem.shape[0]
    piece_width = weight_ref.shape[1] // pieces

    def fetch(piece):
        return pltpu.make_async_copy(
            far_ref.at[:, pl.ds(firsts + piece * piece_width, piece_width)],
            weight_ref.at[:, pl.ds(piece * piece_width, piece_width)],
            weight_sem.at[piece],
        )

    for piece in range(pieces):
        fetch(piece).start()
    sources, all_rows, head_dim = parts_ref.shape
    rows = all_rows - tokens
    stats = [parts_ref[s, rows:, :].astype(jnp.float32) for s in range(sources)]
    stats.append(fresh_ref[rows:, :])

    def stacked(first):
        return joined_thirds(
            [
                jnp.concatenate([stat[r : r + 1] for stat in stats], axis=0)
                for r in range(first, first + 3)
            ]
        )

    peaks, totals = stacked(0), stacked(3)
    factors = jnp.exp(peaks - jnp.max(peaks, axis=0, keepdims=True))
    denominator = jnp.sum(factors * totals, axis=0, keepdims=True)
    numerator = as_column(factors[sources:], rows) * fresh_ref[:rows, :]
    for s in range(sources):
        part = parts_ref[s, :rows, :].astype(jnp.float32)
        numerator = numerator + as_column(factors[s : s + 1], rows) * part
    attended = numerator / as_column(denominator, rows)
    attention = jnp.concatenate(
        [attended[r : r + tokens] for r in range(0, rows, tokens)], axis=1
    ).astype(jnp.bfloat16)
    chunks, _, width = out_ref.shape
    for chunk in range(chunks):
        low = chunk * width - firsts
        if low < 0:
            weight = first_ref[:, low + firsts : low + firsts + width]
        else:
            if low % piece_width == 0:
                fetch(low // piece_width).wait()
            weight = weight_ref[:, low : low + width]
        out_ref[chunk] = jnp.dot(
            attention, weight, preferred_element_type=jnp.float32
        ).astype(jnp.bfloat16)


def on_core(kernel, out_shape, limit, *args, streamed=(), scratch=(), cost=None):
    vmem = pl.BlockSpec(memory_space=pltpu.VMEM)
    smem = pl.BlockSpec(memory_space=pltpu.SMEM)
    scalars = [arg.dtype == jnp.int32 for arg in args]
    placed = [
        arg if scalar else pltpu.with_memory_space_constraint(arg, pltpu.VMEM)
        for arg, scalar in zip(args, scalars)
    ]
    specs = [smem if scalar else vmem for scalar in scalars]
    return pl.pallas_call(
        kernel,
        out_shape=out_shape,
        in_specs=specs + [pl.BlockSpec(memory_space=pltpu.HBM)] * len(streamed),
        scratch_shapes=scratch,
        compiler_params=pltpu.CompilerParams(vmem_limit_bytes=limit * 2**20),
        cost_estimate=cost,
    )(*placed, *(pltpu.with_memory_space_constraint(arg, pltpu.HBM) for arg in streamed))


def shaped(*shape, dtype=jnp.float32):
    return jax.ShapeDtypeStruct(shape, dtype)


def per_device_heads(
    hidden,
    norm_gain,
    q_weight,
    kv_weight,
    out_weight,
    head_kind,
    ret_keys,
    ret_values,
    stream_keys,
    stream_values,
    cache_len,
    sink_len,
    window_len,
):
    requests, drafts, local_width = hidden.shape
    kv_heads = head_kind.shape[0]
    head_dim = ret_keys.shape[3]
    devices = lax.axis_size("seq")
    position = lax.axis_index("seq")
    tokens = requests * drafts
    query_width = q_weight.shape[1] // devices
    rows = tokens * (query_width // head_dim)
    near = min(4, devices)
    far = devices // near
    hint = pl.CostEstimate(
        flops=2 * tokens * devices * devices * q_weight.size,
        bytes_accessed=hidden.size,
        transcendentals=0,
    )
    squares = on_core(squares_kernel, shaped(tokens, head_dim), 4, hidden, cost=hint)
    squares = paired_sum([squares, *from_peers(squares, 1, near)])
    squares = [squares, *from_peers(squares, near, far)]
    part_entries = on_core(
        functools.partial(projection_kernel, local_width * devices, far),
        [shaped(far, rows + tokens, head_dim)] * near,
        8,
        *squares,
        hidden,
        norm_gain[None, :],
        q_weight,
        kv_weight,
    )
    own, *others = part_entries
    others = [
        from_peer(part, distance) for distance, part in enumerate(others, start=1)
    ]
    chip_entries = on_core(
        sum_kernel, shaped(far, rows + tokens, head_dim), 4, own, *others, cost=hint
    )
    own_entries = on_core(
        sum_kernel,
        shaped(far, rows + tokens, head_dim, dtype=jnp.bfloat16),
        4,
        chip_entries,
        *from_peers(chip_entries, near, far),
    )
    part_out, entries = on_core(
        functools.partial(attention_kernel, drafts),
        (
            shaped(devices, rows + tokens, head_dim, dtype=jnp.bfloat16),
            pltpu.VMEM((devices, rows + tokens, head_dim), jnp.bfloat16),
        ),
        16,
        head_kind,
        cache_len,
        sink_len,
        window_len,
        ret_keys,
        ret_values,
        stream_keys,
        stream_values,
        own_entries,
        *from_peers(own_entries, 1, near),
    )
    new_entries = entries[:, rows:, :].transpose(1, 0, 2).reshape(requests, drafts, -1)
    received = exchanged(part_out)
    own_rows, width = out_weight.shape
    chunk_width = width // devices
    first_width = chunk_width * (devices // 4)
    dma = pltpu.SemaphoreType.DMA
    fresh, first_weight = on_core(
        functools.partial(fresh_kernel, kv_heads, requests, drafts),
        (shaped(rows + tokens, head_dim), pltpu.VMEM((own_rows, first_width), out_weight.dtype)),
        4,
        entries,
        streamed=(out_weight,),
        scratch=[dma],
    )
    part_output = on_core(
        functools.partial(output_kernel, tokens),
        shaped(devices, tokens, chunk_width, dtype=jnp.bfloat16),
        16,
        received,
        fresh,
        first_weight,
        streamed=(out_weight,),
        scratch=[
            pltpu.VMEM((own_rows, width - first_width), out_weight.dtype),
            dma(((width - first_width) // (2 * chunk_width),)),
        ],
    )
    own_output = jnp.sum(exchanged(part_output).astype(jnp.float32), axis=0)
    layer_output = own_output.reshape(requests, drafts, local_width).astype(jnp.bfloat16)
    return (layer_output, new_entries)


def per_device(*args):
    hidden, _, q_weight, kv_weight, _, head_kind, ret_keys, _, stream_keys = args[:9]
    devices = lax.axis_size("seq")
    kv_heads, head_dim = head_kind.shape[0], ret_keys.shape[3]
    whole_heads = (
        (hidden.shape[0] * hidden.shape[1]) % 8 == 0
        and q_weight.shape[1] % (devices * head_dim) == 0
        and kv_weight.shape[1] == devices * head_dim
        and devices == 2 * kv_heads
        and ret_keys.shape[1] == stream_keys.shape[1]
    )
    return (per_device_heads if whole_heads else per_device_any)(*args)


def solution(mesh):
    in_specs = (
        P("groups", None, "seq"),
        P("seq"),
        P("seq", None),
        P("seq", None),
        P("seq", None),
        P(),
        P("groups", None, "seq", None),
        P("groups", None, "seq", None),
        P("groups", None, "seq", None),
        P("groups", None, "seq", None),
        P("groups"),
        P("groups"),
        P("groups"),
    )
    out_specs = (P("groups", None, "seq"), P("groups", None, None))
    return jax.shard_map(
        per_device, mesh=mesh, in_specs=in_specs, out_specs=out_specs, check_vma=False
    )
```

```python
import functools

import jax
import jax.numpy as jnp
from jax import lax
from jax.experimental import pallas as pl
from jax.experimental.pallas import tpu as pltpu
from jax.sharding import PartitionSpec as P


SINK_CAP = 128


epsilon = 1e-05
floor_score = -1e30


def exchanged(parts):
    return lax.all_to_all(parts, "seq", 0, 0, tiled=True)


def summed_over_devices(value):
    devices = lax.axis_size("seq")
    step = 1
    while step < devices:
        value = value + lax.ppermute(value, "seq", [(i, i ^ step) for i in range(devices)])
        step *= 2
    return value


def column_blocks(rows, blocks):
    return rows.reshape(rows.shape[0], blocks, -1).transpose(1, 0, 2)


def block_stats(queries, cache_keys, cache_values, visible, score_scale):
    scores = (
        jnp.einsum("bhqd,bhld->bhql", queries, cache_keys, preferred_element_type=jnp.float32)
        * score_scale
    )
    scores = jnp.where(visible, scores, floor_score)
    peak_score = jnp.max(scores, axis=-1)
    weights = jnp.where(visible, jnp.exp(scores - peak_score[..., None]), 0.0)
    weight_total = jnp.sum(weights, axis=-1)
    block_out = jnp.einsum(
        "bhql,bhld->bhqd",
        weights.astype(jnp.bfloat16),
        cache_values,
        preferred_element_type=jnp.float32,
    )
    return (peak_score, weight_total, block_out)


def spread_rows(values_in, selector):
    return jnp.einsum("brq,gr->bgq", values_in, selector, precision=lax.Precision.HIGHEST)


def spread_vectors(values_in, selector):
    return jnp.einsum("brqd,gr->bgqd", values_in, selector, precision=lax.Precision.HIGHEST)


def per_device_any(
    hidden,
    norm_gain,
    q_weight,
    kv_weight,
    out_weight,
    head_kind,
    ret_keys,
    ret_values,
    stream_keys,
    stream_values,
    cache_len,
    sink_len,
    window_len,
):
    requests, drafts, local_width = hidden.shape
    kv_heads = head_kind.shape[0]
    head_dim = ret_keys.shape[3]
    retrieval = ret_keys.shape[1]
    running = stream_keys.shape[1]
    head_count = q_weight.shape[1] // head_dim
    group_size = head_count // kv_heads
    query_rows = drafts * group_size
    devices = lax.axis_size("seq")
    position = lax.axis_index("seq")
    tokens = requests * drafts
    hidden32 = hidden.astype(jnp.float32)
    squares = summed_over_devices(jnp.sum(hidden32 * hidden32, axis=-1))
    inverse = lax.rsqrt(squares / (local_width * devices) + epsilon)
    normed = (hidden32 * inverse[..., None] * norm_gain.astype(jnp.float32)).astype(jnp.bfloat16)
    flat_rows = normed.reshape(tokens, local_width)
    part_query = jnp.dot(flat_rows, q_weight, preferred_element_type=jnp.float32)
    part_fresh = jnp.dot(flat_rows, kv_weight, preferred_element_type=jnp.float32)
    sums = jnp.sum(
        exchanged(
            jnp.concatenate(
                [column_blocks(part_query, devices), column_blocks(part_fresh, devices)], axis=-1
            )
        ),
        axis=0,
    ).astype(jnp.bfloat16)
    gathered = exchanged(jnp.broadcast_to(sums[None], (devices, *sums.shape)))
    query_width = q_weight.shape[1] // devices
    queries = gathered[..., :query_width].transpose(1, 0, 2).reshape(tokens, -1)
    new_entries = gathered[..., query_width:].transpose(1, 0, 2).reshape(tokens, -1)
    grouped = (
        queries.reshape(requests, drafts, kv_heads, group_size, head_dim)
        .transpose(0, 2, 1, 3, 4)
        .reshape(requests, kv_heads, query_rows, head_dim)
    )
    fresh_split = new_entries.reshape(requests, drafts, 2, kv_heads, head_dim)
    new_keys = fresh_split[:, :, 0].transpose(0, 2, 1, 3)
    new_values = fresh_split[:, :, 1].transpose(0, 2, 1, 3)
    kind_flag = head_kind == 1
    rank_ret = jnp.cumsum(head_kind) - 1
    rank_str = jnp.cumsum(1 - head_kind) - 1
    select_ret = (
        kind_flag[:, None] & (rank_ret[:, None] == jnp.arange(retrieval)[None, :])
    ).astype(jnp.float32)
    select_str = (
        jnp.logical_not(kind_flag)[:, None] & (rank_str[:, None] == jnp.arange(running)[None, :])
    ).astype(jnp.float32)
    ret_queries = jnp.einsum(
        "bgqd,gr->brqd",
        grouped,
        select_ret.astype(jnp.bfloat16),
        preferred_element_type=jnp.float32,
    ).astype(jnp.bfloat16)
    str_queries = jnp.einsum(
        "bgqd,gr->brqd",
        grouped,
        select_str.astype(jnp.bfloat16),
        preferred_element_type=jnp.float32,
    ).astype(jnp.bfloat16)
    score_scale = head_dim ** (-0.5)
    cache_block = ret_keys.shape[2]
    cache_pos = position * cache_block + jnp.arange(cache_block)
    ret_visible = (cache_pos[None, :] < cache_len[:, None])[:, None, None, :]
    slot_block = stream_keys.shape[2]
    slot_pos = (position * slot_block + jnp.arange(slot_block))[None, :]
    sink_part = slot_pos < sink_len[:, None]
    recent_part = (slot_pos >= SINK_CAP) & (slot_pos < SINK_CAP + window_len[:, None])
    str_visible = (sink_part | recent_part)[:, None, None, :]
    ret_peak, ret_total, ret_out = block_stats(
        ret_queries, ret_keys, ret_values, ret_visible, score_scale
    )
    str_peak, str_total, str_out = block_stats(
        str_queries, stream_keys, stream_values, str_visible, score_scale
    )
    peak_all = spread_rows(ret_peak, select_ret) + spread_rows(str_peak, select_str)
    total_all = spread_rows(ret_total, select_ret) + spread_rows(str_total, select_str)
    out_all = spread_vectors(ret_out, select_ret) + spread_vectors(str_out, select_str)
    token_of_row = jnp.arange(query_rows) // group_size
    new_visible = jnp.arange(drafts)[None, :] <= token_of_row[:, None]
    new_peak, new_total, new_out = block_stats(
        grouped, new_keys, new_values, new_visible, score_scale
    )
    own_width = out_weight.shape[0]
    block_heads = max(1, own_width // head_dim)

    def by_token(value):
        split = value.reshape(requests, kv_heads, drafts, group_size, -1)
        return split.transpose(0, 2, 1, 3, 4).reshape(tokens, head_count, -1)

    first_head = (jnp.arange(devices) * own_width) // head_dim
    block_head = first_head[:, None] + jnp.arange(block_heads)[None, :]

    def head_blocks(value):
        rows = by_token(value).reshape(tokens, head_count)
        return jnp.take(rows, block_head.reshape(-1), axis=1).reshape(tokens, devices, -1).transpose(1, 0, 2)

    received = exchanged(
        jnp.concatenate(
            [
                column_blocks(by_token(out_all).reshape(tokens, -1), devices),
                head_blocks(peak_all),
                head_blocks(total_all),
            ],
            axis=-1,
        )
    )
    got_out = received[..., :own_width].reshape(devices, tokens, block_heads, -1)
    got_peak = received[..., own_width : own_width + block_heads]
    got_total = received[..., own_width + block_heads :]

    def own_heads(value):
        blocks = column_blocks(by_token(value).reshape(tokens, -1), devices)
        return lax.dynamic_index_in_dim(blocks, position, 0, False).reshape(tokens, block_heads, -1)

    own_new_out = own_heads(new_out)
    own_new_peak = lax.dynamic_index_in_dim(head_blocks(new_peak), position, 0, False)
    own_new_total = lax.dynamic_index_in_dim(head_blocks(new_total), position, 0, False)
    top_score = jnp.maximum(jnp.max(got_peak, axis=0), own_new_peak)
    cache_factor = jnp.exp(got_peak - top_score[None])
    new_factor = jnp.exp(own_new_peak - top_score)
    denominator = jnp.sum(got_total * cache_factor, axis=0) + own_new_total * new_factor
    attended = (
        jnp.sum(got_out * cache_factor[..., None], axis=0) + own_new_out * new_factor[..., None]
    ) / denominator[..., None]
    own_attention = attended.reshape(tokens, own_width).astype(jnp.bfloat16)
    part_output = jnp.dot(own_attention, out_weight, preferred_element_type=jnp.float32)
    own_output = jnp.sum(exchanged(column_blocks(part_output, devices)), axis=0)
    layer_output = own_output.reshape(requests, drafts, local_width).astype(jnp.bfloat16)
    return (layer_output, new_entries.reshape(requests, drafts, 2 * kv_heads * head_dim))


def flat_tokens(ref):
    return jnp.concatenate([ref[b].astype(jnp.float32) for b in range(ref.shape[0])], axis=0)


def squares_kernel(hidden_ref, out_ref):
    rows = flat_tokens(hidden_ref)
    out_ref[...] = jnp.broadcast_to(jnp.sum(rows * rows, axis=1, keepdims=True), out_ref.shape)


def from_peer(value, distance):
    devices = lax.axis_size("seq")
    return lax.ppermute(value, "seq", [(i, i ^ distance) for i in range(devices)])


def from_peers(value, low, radix):
    return [from_peer(value, low * step) for step in range(1, radix)]


def paired_sum(values):
    while len(values) > 1:
        values = [left + right for left, right in zip(values[::2], values[1::2])]
    return values[0]


def chunk_of(position, near, distance, far):
    return far * near + ((position & (near - 1)) ^ distance)


def projection_kernel(width, parts, near, distances, *refs):
    squares = refs[:parts]
    hidden_ref, gain_ref, query_ref, fresh_ref = refs[parts : parts + 4]
    out_refs = refs[parts + 4 :]
    total = paired_sum([ref[...] for ref in squares])
    inverse = lax.rsqrt(total[:, :1] / width + epsilon)
    gain = gain_ref[...].astype(jnp.float32)
    normed = (flat_tokens(hidden_ref) * inverse * gain).astype(jnp.bfloat16)
    tokens = normed.shape[0]
    position = lax.axis_index("seq")
    far, _, lanes = out_refs[0].shape
    query_width = query_ref.shape[1] // (near * far)
    pieces = query_width // lanes

    def times(ref, chunk, size):
        columns = ref[:, pl.ds(pl.multiple_of(chunk * size, size), size)]
        return jnp.dot(normed, columns, preferred_element_type=jnp.float32)

    for distance, out in zip(distances, out_refs):
        for group in range(far):
            chunk = chunk_of(position, near, distance, group)
            part = times(query_ref, chunk, query_width)
            for piece in range(pieces):
                out[group, piece * tokens : (piece + 1) * tokens, :] = part[
                    :, piece * lanes : (piece + 1) * lanes
                ]
            out[group, pieces * tokens :, :] = times(fresh_ref, chunk, lanes)


def sum_kernel(*refs):
    refs[-1][...] = paired_sum([ref[...] for ref in refs[:-1]]).astype(refs[-1].dtype)


def head_of(kind_ref, flag, rank):
    found, before = jnp.int32(0), jnp.int32(0)
    for head in range(kind_ref.shape[0]):
        is_kind = kind_ref[head] == flag
        found = jnp.where(is_kind & (before == rank), head, found)
        before = before + is_kind.astype(jnp.int32)
    return found


def diagonal_of(rows, lanes):
    return lax.broadcasted_iota(jnp.int32, (rows, lanes), 0) == lax.broadcasted_iota(
        jnp.int32, (rows, lanes), 1
    )


def as_row(column, lanes):
    return jnp.sum(
        jnp.where(diagonal_of(column.shape[0], lanes), column, 0.0), axis=0, keepdims=True
    )


def as_column(row, rows):
    return jnp.sum(jnp.where(diagonal_of(rows, row.shape[1]), row, 0.0), axis=1, keepdims=True)


def masked_weights(scores, visible):
    scores = jnp.where(visible, scores, floor_score)
    peak = jnp.max(scores, axis=1, keepdims=True)
    weights = jnp.exp(scores - jnp.maximum(peak, 0.5 * floor_score))
    return peak, jnp.sum(weights, axis=1, keepdims=True), weights.astype(jnp.bfloat16)


def dot_keys(queries, keys):
    return lax.dot_general(
        queries, keys, (((1,), (1,)), ((), ())), preferred_element_type=jnp.float32
    )


def thirds(row):
    rest, pieces = row, []
    for _ in range(3):
        pieces.append(rest.astype(jnp.bfloat16))
        rest = rest - pieces[-1].astype(jnp.float32)
    return pieces


def stat_rows(peak, total, lanes, sublanes):
    return row_stats(as_row(peak, lanes), as_row(total, lanes), sublanes)


def row_stats(peak, total, sublanes):
    lanes = peak.shape[1]
    pieces = [*thirds(peak), *thirds(total)]
    wide = [piece.astype(jnp.float32) for piece in pieces]
    pad = jnp.zeros((sublanes - len(wide), lanes), jnp.float32)
    return jnp.concatenate([*wide, pad], axis=0)


def joined_thirds(rows):
    return (rows[0] + rows[1]) + rows[2]


def attention_kernel(
    drafts,
    kind_ref,
    cache_ref,
    sink_ref,
    window_ref,
    ret_key_ref,
    ret_value_ref,
    str_key_ref,
    str_value_ref,
    *refs,
):
    near = (len(refs) - 2) // 2
    part_refs, out_refs = refs[:near], refs[near : 2 * near]
    entries_ref, out_ref = refs[2 * near :]
    requests, retrieval, block, head_dim = ret_value_ref.shape
    position = lax.axis_index("seq")
    for distance, part_ref in enumerate(part_refs):
        for group in range(part_ref.shape[0]):
            chunk = chunk_of(position, near, distance, group)
            entries_ref[chunk] = part_ref[group]
    tokens = requests * drafts
    chunks, all_rows, _ = entries_ref.shape
    head_rows = all_rows - tokens
    per_head = chunks // kind_ref.shape[0]
    rows = per_head * head_rows
    row = lax.broadcasted_iota(jnp.int32, (rows, 1), 0)
    request_of_row = (row % tokens) // drafts

    def by_request(values):
        picked = values[0]
        for b in range(1, requests):
            picked = jnp.where(request_of_row == b, values[b], picked)
        return picked

    def limit(ref):
        return by_request([ref[b] for b in range(requests)])

    def weighed(flag, rank, keys, visible):
        head = head_of(kind_ref, flag, rank)
        queries = jnp.concatenate(
            [entries_ref[head * per_head + half, :head_rows, :] for half in range(per_head)], axis=0
        )
        own = [jnp.where(request_of_row == b, queries, 0) for b in range(requests)]
        scores = dot_keys(jnp.concatenate(own, axis=1), jnp.concatenate(keys, axis=1))
        return head, *masked_weights(scores * head_dim ** (-0.5), visible)

    def mix(weights, values):
        return jnp.dot(
            weights, jnp.concatenate(values, axis=1), preferred_element_type=jnp.float32
        )

    def store(head, peak, total, mixed):
        mixed = by_request([mixed[:, b * head_dim : (b + 1) * head_dim] for b in range(requests)])
        for half in range(per_head):
            span = slice(half * head_rows, (half + 1) * head_rows)
            block_rows = jnp.concatenate(
                [mixed[span], stat_rows(peak[span], total[span], head_dim, tokens)], axis=0
            )
            out_ref[head * per_head + half] = block_rows.astype(jnp.bfloat16)

    def of_rank(ref, rank):
        return [ref[b, rank] for b in range(requests)]

    slots = str_key_ref.shape[2]
    slot = position * slots + lax.broadcasted_iota(jnp.int32, (rows, slots), 1)
    recent = (slot >= SINK_CAP) & (slot < SINK_CAP + limit(window_ref))
    held = (slot < limit(sink_ref)) | recent
    running = range(str_key_ref.shape[1])
    ready = [weighed(0, rank, of_rank(str_key_ref, rank), held) for rank in running]
    for rank in running:
        head, peak, total, weights = ready[rank]
        store(head, peak, total, mix(weights, of_rank(str_value_ref, rank)))
    place = position * block + lax.broadcasted_iota(jnp.int32, (rows, block), 1)
    filled = place < limit(cache_ref)
    ready = [weighed(1, rank, of_rank(ret_key_ref, rank), filled) for rank in range(retrieval)]
    for rank in range(retrieval):
        head, peak, total, weights = ready[rank]
        store(head, peak, total, mix(weights, of_rank(ret_value_ref, rank)))
    for distance, part_ref in enumerate(out_refs):
        for group in range(part_ref.shape[0]):
            part_ref[group] = out_ref[chunk_of(position, near, distance, group)]


def merged(parts, rows):
    stats = [part[rows:] for part in parts]

    def stacked(first):
        return joined_thirds(
            [
                jnp.concatenate([stat[r : r + 1] for stat in stats], axis=0)
                for r in range(first, first + 3)
            ]
        )

    peaks, totals = stacked(0), stacked(3)
    peak = jnp.max(peaks, axis=0, keepdims=True)
    factors = jnp.exp(peaks - peak)
    total = jnp.sum(factors * totals, axis=0, keepdims=True)
    mixed = [
        as_column(factors[index : index + 1], rows) * part[:rows]
        for index, part in enumerate(parts)
    ]
    return peak, total, functools.reduce(jnp.add, mixed)


def merge_kernel(tokens, near, *refs):
    parts, out_refs = refs[:near], refs[near:]
    rows = out_refs[0].shape[0] - tokens
    group = lax.axis_index("seq") // near
    for distance, out in enumerate(out_refs):
        chunk = group ^ distance
        peak, total, mixed = merged([part[chunk].astype(jnp.float32) for part in parts], rows)
        stats = row_stats(peak, total, tokens)
        out[...] = jnp.concatenate([mixed, stats], axis=0).astype(out.dtype)


def fresh_kernel(kv_heads, requests, drafts, entries_ref, out_ref):
    position = lax.axis_index("seq")
    tokens = requests * drafts
    chunks, all_rows, head_dim = entries_ref.shape
    rows = all_rows - tokens
    head = position // (chunks // kv_heads)
    queries = entries_ref[position, :rows, :]
    keys = entries_ref[head, rows:, :]
    values = entries_ref[kv_heads + head, rows:, :]
    of_row = lax.broadcasted_iota(jnp.int32, (rows, tokens), 0) % tokens
    of_key = lax.broadcasted_iota(jnp.int32, (rows, tokens), 1)
    visible = (of_row // drafts == of_key // drafts) & (of_key <= of_row)
    peak, total, weights = masked_weights(dot_keys(queries, keys) * head_dim ** (-0.5), visible)
    out_ref[:rows, :] = jnp.dot(weights, values, preferred_element_type=jnp.float32)
    out_ref[rows:, :] = stat_rows(peak, total, head_dim, tokens)


def output_kernel(tokens, *refs):
    *part_refs, fresh_ref, weight_ref, out_ref = refs
    rows = fresh_ref.shape[0] - tokens
    parts = [part[...].astype(jnp.float32) for part in part_refs]
    _, total, mixed = merged([*parts, fresh_ref[...]], rows)
    attended = mixed / as_column(total, rows)
    attention = jnp.concatenate(
        [attended[r : r + tokens] for r in range(0, rows, tokens)], axis=1
    ).astype(jnp.bfloat16)
    chunks, _, width = out_ref.shape
    for chunk in range(chunks):
        out_ref[chunk] = jnp.dot(
            attention,
            weight_ref[:, chunk * width : (chunk + 1) * width],
            preferred_element_type=jnp.float32,
        ).astype(jnp.bfloat16)


def on_core(kernel, out_shape, limit, *args, streamed=(), scratch=(), cost=None):
    vmem = pl.BlockSpec(memory_space=pltpu.VMEM)
    smem = pl.BlockSpec(memory_space=pltpu.SMEM)
    scalars = [arg.dtype == jnp.int32 for arg in args]
    placed = [
        arg if scalar else pltpu.with_memory_space_constraint(arg, pltpu.VMEM)
        for arg, scalar in zip(args, scalars)
    ]
    specs = [smem if scalar else vmem for scalar in scalars]
    return pl.pallas_call(
        kernel,
        out_shape=out_shape,
        in_specs=specs + [pl.BlockSpec(memory_space=pltpu.HBM)] * len(streamed),
        scratch_shapes=scratch,
        compiler_params=pltpu.CompilerParams(vmem_limit_bytes=limit * 2**20),
        cost_estimate=cost,
    )(*placed, *(pltpu.with_memory_space_constraint(arg, pltpu.HBM) for arg in streamed))


def shaped(*shape, dtype=jnp.float32):
    return jax.ShapeDtypeStruct(shape, dtype)


def per_device_heads(
    hidden,
    norm_gain,
    q_weight,
    kv_weight,
    out_weight,
    head_kind,
    ret_keys,
    ret_values,
    stream_keys,
    stream_values,
    cache_len,
    sink_len,
    window_len,
):
    requests, drafts, local_width = hidden.shape
    kv_heads = head_kind.shape[0]
    head_dim = ret_keys.shape[3]
    devices = lax.axis_size("seq")
    tokens = requests * drafts
    query_width = q_weight.shape[1] // devices
    rows = tokens * (query_width // head_dim)
    near = min(4, devices)
    far = devices // near
    hint = pl.CostEstimate(
        flops=2 * tokens * devices * devices * q_weight.size,
        bytes_accessed=hidden.size,
        transcendentals=0,
    )
    squares = on_core(squares_kernel, shaped(tokens, head_dim), 4, hidden, cost=hint)
    squares = paired_sum([squares, *from_peers(squares, 1, near)])
    squares = [squares, *from_peers(squares, near, far)]
    gain = norm_gain[None, :]

    def projected(distances):
        return on_core(
            functools.partial(projection_kernel, local_width * devices, far, near, distances),
            [shaped(far, rows + tokens, head_dim)] * len(distances),
            8,
            *squares,
            hidden,
            gain,
            q_weight,
            kv_weight,
        )

    distances = [*range(near // 2, near), *range(near // 2)]
    part_entries = projected(distances[: near // 2]) + projected(distances[near // 2 :])
    own = part_entries[distances.index(0)]
    others = [
        from_peer(part_entries[distances.index(distance)], distance) for distance in range(1, near)
    ]
    chip_entries = on_core(
        sum_kernel, shaped(far, rows + tokens, head_dim), 4, own, *others, cost=hint
    )
    own_entries = on_core(
        sum_kernel,
        shaped(far, rows + tokens, head_dim, dtype=jnp.bfloat16),
        4,
        chip_entries,
        *from_peers(chip_entries, near, far),
    )
    blocks = (devices, rows + tokens, head_dim)
    *part_out, entries = on_core(
        functools.partial(attention_kernel, drafts),
        [shaped(far, *blocks[1:], dtype=jnp.bfloat16)] * near
        + [pltpu.VMEM(blocks, jnp.bfloat16)],
        16,
        head_kind,
        cache_len,
        sink_len,
        window_len,
        ret_keys,
        ret_values,
        stream_keys,
        stream_values,
        own_entries,
        *from_peers(own_entries, 1, near),
        scratch=[pltpu.VMEM(blocks, jnp.bfloat16)],
    )
    new_entries = entries[:, rows:, :].transpose(1, 0, 2).reshape(requests, drafts, -1)
    own_out = part_out[0]
    near_out = [from_peer(part_out[distance], distance) for distance in range(1, near)]
    fresh = on_core(
        functools.partial(fresh_kernel, kv_heads, requests, drafts),
        shaped(rows + tokens, head_dim),
        4,
        entries,
    )
    chip_out = on_core(
        functools.partial(merge_kernel, tokens, near),
        [shaped(rows + tokens, head_dim, dtype=jnp.bfloat16)] * far,
        4,
        own_out,
        *near_out,
        cost=hint,
    )
    far_out = [from_peer(chip_out[distance], near * distance) for distance in range(1, far)]
    part_output = on_core(
        functools.partial(output_kernel, tokens),
        shaped(devices, tokens, out_weight.shape[1] // devices, dtype=jnp.bfloat16),
        8,
        chip_out[0],
        *far_out,
        fresh,
        out_weight,
    )
    own_output = jnp.sum(exchanged(part_output).astype(jnp.float32), axis=0)
    layer_output = own_output.reshape(requests, drafts, local_width).astype(jnp.bfloat16)
    return (layer_output, new_entries)


def per_device(*args):
    hidden, _, q_weight, kv_weight, _, head_kind, ret_keys, _, stream_keys = args[:9]
    devices = lax.axis_size("seq")
    kv_heads, head_dim = head_kind.shape[0], ret_keys.shape[3]
    whole_heads = (
        (hidden.shape[0] * hidden.shape[1]) % 8 == 0
        and q_weight.shape[1] % (devices * head_dim) == 0
        and kv_weight.shape[1] == devices * head_dim
        and devices == 2 * kv_heads
        and ret_keys.shape[1] == stream_keys.shape[1]
    )
    return (per_device_heads if whole_heads else per_device_any)(*args)


def solution(mesh):
    in_specs = (
        P("groups", None, "seq"),
        P("seq"),
        P("seq", None),
        P("seq", None),
        P("seq", None),
        P(),
        P("groups", None, "seq", None),
        P("groups", None, "seq", None),
        P("groups", None, "seq", None),
        P("groups", None, "seq", None),
        P("groups"),
        P("groups"),
        P("groups"),
    )
    out_specs = (P("groups", None, "seq"), P("groups", None, None))
    return jax.shard_map(
        per_device, mesh=mesh, in_specs=in_specs, out_specs=out_specs, check_vma=False
    )
```

```python
import functools

import jax
import jax.numpy as jnp
from jax import lax
from jax.experimental import pallas as pl
from jax.experimental.pallas import tpu as pltpu
from jax.sharding import PartitionSpec as P


SINK_CAP = 128


epsilon = 1e-05
floor_score = -1e30


def exchanged(parts):
    return lax.all_to_all(parts, "seq", 0, 0, tiled=True)


def summed_over_devices(value):
    devices = lax.axis_size("seq")
    step = 1
    while step < devices:
        value = value + lax.ppermute(value, "seq", [(i, i ^ step) for i in range(devices)])
        step *= 2
    return value


def column_blocks(rows, blocks):
    return rows.reshape(rows.shape[0], blocks, -1).transpose(1, 0, 2)


def block_stats(queries, cache_keys, cache_values, visible, score_scale):
    scores = (
        jnp.einsum("bhqd,bhld->bhql", queries, cache_keys, preferred_element_type=jnp.float32)
        * score_scale
    )
    scores = jnp.where(visible, scores, floor_score)
    peak_score = jnp.max(scores, axis=-1)
    weights = jnp.where(visible, jnp.exp(scores - peak_score[..., None]), 0.0)
    weight_total = jnp.sum(weights, axis=-1)
    block_out = jnp.einsum(
        "bhql,bhld->bhqd",
        weights.astype(jnp.bfloat16),
        cache_values,
        preferred_element_type=jnp.float32,
    )
    return (peak_score, weight_total, block_out)


def spread_rows(values_in, selector):
    return jnp.einsum("brq,gr->bgq", values_in, selector, precision=lax.Precision.HIGHEST)


def spread_vectors(values_in, selector):
    return jnp.einsum("brqd,gr->bgqd", values_in, selector, precision=lax.Precision.HIGHEST)


def per_device_any(
    hidden,
    norm_gain,
    q_weight,
    kv_weight,
    out_weight,
    head_kind,
    ret_keys,
    ret_values,
    stream_keys,
    stream_values,
    cache_len,
    sink_len,
    window_len,
):
    requests, drafts, local_width = hidden.shape
    kv_heads = head_kind.shape[0]
    head_dim = ret_keys.shape[3]
    retrieval = ret_keys.shape[1]
    running = stream_keys.shape[1]
    head_count = q_weight.shape[1] // head_dim
    group_size = head_count // kv_heads
    query_rows = drafts * group_size
    devices = lax.axis_size("seq")
    position = lax.axis_index("seq")
    tokens = requests * drafts
    hidden32 = hidden.astype(jnp.float32)
    squares = summed_over_devices(jnp.sum(hidden32 * hidden32, axis=-1))
    inverse = lax.rsqrt(squares / (local_width * devices) + epsilon)
    normed = (hidden32 * inverse[..., None] * norm_gain.astype(jnp.float32)).astype(jnp.bfloat16)
    flat_rows = normed.reshape(tokens, local_width)
    part_query = jnp.dot(flat_rows, q_weight, preferred_element_type=jnp.float32)
    part_fresh = jnp.dot(flat_rows, kv_weight, preferred_element_type=jnp.float32)
    sums = jnp.sum(
        exchanged(
            jnp.concatenate(
                [column_blocks(part_query, devices), column_blocks(part_fresh, devices)], axis=-1
            )
        ),
        axis=0,
    ).astype(jnp.bfloat16)
    gathered = exchanged(jnp.broadcast_to(sums[None], (devices, *sums.shape)))
    query_width = q_weight.shape[1] // devices
    queries = gathered[..., :query_width].transpose(1, 0, 2).reshape(tokens, -1)
    new_entries = gathered[..., query_width:].transpose(1, 0, 2).reshape(tokens, -1)
    grouped = (
        queries.reshape(requests, drafts, kv_heads, group_size, head_dim)
        .transpose(0, 2, 1, 3, 4)
        .reshape(requests, kv_heads, query_rows, head_dim)
    )
    fresh_split = new_entries.reshape(requests, drafts, 2, kv_heads, head_dim)
    new_keys = fresh_split[:, :, 0].transpose(0, 2, 1, 3)
    new_values = fresh_split[:, :, 1].transpose(0, 2, 1, 3)
    kind_flag = head_kind == 1
    rank_ret = jnp.cumsum(head_kind) - 1
    rank_str = jnp.cumsum(1 - head_kind) - 1
    select_ret = (
        kind_flag[:, None] & (rank_ret[:, None] == jnp.arange(retrieval)[None, :])
    ).astype(jnp.float32)
    select_str = (
        jnp.logical_not(kind_flag)[:, None] & (rank_str[:, None] == jnp.arange(running)[None, :])
    ).astype(jnp.float32)
    ret_queries = jnp.einsum(
        "bgqd,gr->brqd",
        grouped,
        select_ret.astype(jnp.bfloat16),
        preferred_element_type=jnp.float32,
    ).astype(jnp.bfloat16)
    str_queries = jnp.einsum(
        "bgqd,gr->brqd",
        grouped,
        select_str.astype(jnp.bfloat16),
        preferred_element_type=jnp.float32,
    ).astype(jnp.bfloat16)
    score_scale = head_dim ** (-0.5)
    cache_block = ret_keys.shape[2]
    cache_pos = position * cache_block + jnp.arange(cache_block)
    ret_visible = (cache_pos[None, :] < cache_len[:, None])[:, None, None, :]
    slot_block = stream_keys.shape[2]
    slot_pos = (position * slot_block + jnp.arange(slot_block))[None, :]
    sink_part = slot_pos < sink_len[:, None]
    recent_part = (slot_pos >= SINK_CAP) & (slot_pos < SINK_CAP + window_len[:, None])
    str_visible = (sink_part | recent_part)[:, None, None, :]
    ret_peak, ret_total, ret_out = block_stats(
        ret_queries, ret_keys, ret_values, ret_visible, score_scale
    )
    str_peak, str_total, str_out = block_stats(
        str_queries, stream_keys, stream_values, str_visible, score_scale
    )
    peak_all = spread_rows(ret_peak, select_ret) + spread_rows(str_peak, select_str)
    total_all = spread_rows(ret_total, select_ret) + spread_rows(str_total, select_str)
    out_all = spread_vectors(ret_out, select_ret) + spread_vectors(str_out, select_str)
    token_of_row = jnp.arange(query_rows) // group_size
    new_visible = jnp.arange(drafts)[None, :] <= token_of_row[:, None]
    new_peak, new_total, new_out = block_stats(
        grouped, new_keys, new_values, new_visible, score_scale
    )
    own_width = out_weight.shape[0]
    block_heads = max(1, own_width // head_dim)

    def by_token(value):
        split = value.reshape(requests, kv_heads, drafts, group_size, -1)
        return split.transpose(0, 2, 1, 3, 4).reshape(tokens, head_count, -1)

    first_head = (jnp.arange(devices) * own_width) // head_dim
    block_head = first_head[:, None] + jnp.arange(block_heads)[None, :]

    def head_blocks(value):
        rows = by_token(value).reshape(tokens, head_count)
        return jnp.take(rows, block_head.reshape(-1), axis=1).reshape(tokens, devices, -1).transpose(1, 0, 2)

    received = exchanged(
        jnp.concatenate(
            [
                column_blocks(by_token(out_all).reshape(tokens, -1), devices),
                head_blocks(peak_all),
                head_blocks(total_all),
            ],
            axis=-1,
        )
    )
    got_out = received[..., :own_width].reshape(devices, tokens, block_heads, -1)
    got_peak = received[..., own_width : own_width + block_heads]
    got_total = received[..., own_width + block_heads :]

    def own_heads(value):
        blocks = column_blocks(by_token(value).reshape(tokens, -1), devices)
        return lax.dynamic_index_in_dim(blocks, position, 0, False).reshape(tokens, block_heads, -1)

    own_new_out = own_heads(new_out)
    own_new_peak = lax.dynamic_index_in_dim(head_blocks(new_peak), position, 0, False)
    own_new_total = lax.dynamic_index_in_dim(head_blocks(new_total), position, 0, False)
    top_score = jnp.maximum(jnp.max(got_peak, axis=0), own_new_peak)
    cache_factor = jnp.exp(got_peak - top_score[None])
    new_factor = jnp.exp(own_new_peak - top_score)
    denominator = jnp.sum(got_total * cache_factor, axis=0) + own_new_total * new_factor
    attended = (
        jnp.sum(got_out * cache_factor[..., None], axis=0) + own_new_out * new_factor[..., None]
    ) / denominator[..., None]
    own_attention = attended.reshape(tokens, own_width).astype(jnp.bfloat16)
    part_output = jnp.dot(own_attention, out_weight, preferred_element_type=jnp.float32)
    own_output = jnp.sum(exchanged(column_blocks(part_output, devices)), axis=0)
    layer_output = own_output.reshape(requests, drafts, local_width).astype(jnp.bfloat16)
    return (layer_output, new_entries.reshape(requests, drafts, 2 * kv_heads * head_dim))


def flat_tokens(ref):
    return jnp.concatenate([ref[b].astype(jnp.float32) for b in range(ref.shape[0])], axis=0)


def squares_kernel(hidden_ref, out_ref):
    rows = flat_tokens(hidden_ref)
    out_ref[...] = jnp.broadcast_to(jnp.sum(rows * rows, axis=1, keepdims=True), out_ref.shape)


def from_peer(value, distance):
    devices = lax.axis_size("seq")
    return lax.ppermute(value, "seq", [(i, i ^ distance) for i in range(devices)])


def from_peers(value, low, radix):
    return [from_peer(value, low * step) for step in range(1, radix)]


def paired_sum(values):
    while len(values) > 1:
        values = [left + right for left, right in zip(values[::2], values[1::2])]
    return values[0]


def chunk_of(position, near, distance, far):
    return far * near + ((position & (near - 1)) ^ distance)


def projection_kernel(width, parts, near, distances, *refs):
    squares = refs[:parts]
    hidden_ref, gain_ref, query_ref, fresh_ref = refs[parts : parts + 4]
    out_refs = refs[parts + 4 :]
    total = paired_sum([ref[...] for ref in squares])
    inverse = lax.rsqrt(total[:, :1] / width + epsilon)
    gain = gain_ref[...].astype(jnp.float32)
    normed = (flat_tokens(hidden_ref) * inverse * gain).astype(jnp.bfloat16)
    tokens = normed.shape[0]
    position = lax.axis_index("seq")
    far, _, lanes = out_refs[0].shape
    query_width = query_ref.shape[1] // (near * far)
    pieces = query_width // lanes

    def times(ref, chunk, size):
        columns = ref[:, pl.ds(pl.multiple_of(chunk * size, size), size)]
        return jnp.dot(normed, columns, preferred_element_type=jnp.float32)

    for distance, out in zip(distances, out_refs):
        for group in range(far):
            chunk = chunk_of(position, near, distance, group)
            part = times(query_ref, chunk, query_width)
            for piece in range(pieces):
                out[group, piece * tokens : (piece + 1) * tokens, :] = part[
                    :, piece * lanes : (piece + 1) * lanes
                ]
            out[group, pieces * tokens :, :] = times(fresh_ref, chunk, lanes)


def sum_kernel(*refs):
    refs[-1][...] = paired_sum([ref[...] for ref in refs[:-1]]).astype(refs[-1].dtype)


def head_of(kind_ref, flag, rank):
    found, before = jnp.int32(0), jnp.int32(0)
    for head in range(kind_ref.shape[0]):
        is_kind = kind_ref[head] == flag
        found = jnp.where(is_kind & (before == rank), head, found)
        before = before + is_kind.astype(jnp.int32)
    return found


def diagonal_of(rows, lanes):
    return lax.broadcasted_iota(jnp.int32, (rows, lanes), 0) == lax.broadcasted_iota(
        jnp.int32, (rows, lanes), 1
    )


def as_row(column, lanes):
    return jnp.sum(
        jnp.where(diagonal_of(column.shape[0], lanes), column, 0.0), axis=0, keepdims=True
    )


def as_column(row, rows):
    return jnp.sum(jnp.where(diagonal_of(rows, row.shape[1]), row, 0.0), axis=1, keepdims=True)


def masked_weights(scores, visible):
    scores = jnp.where(visible, scores, floor_score)
    peak = jnp.max(scores, axis=1, keepdims=True)
    weights = jnp.exp(scores - jnp.maximum(peak, 0.5 * floor_score))
    return peak, jnp.sum(weights, axis=1, keepdims=True), weights.astype(jnp.bfloat16)


def dot_keys(queries, keys):
    return lax.dot_general(
        queries, keys, (((1,), (1,)), ((), ())), preferred_element_type=jnp.float32
    )


def thirds(row):
    rest, pieces = row, []
    for _ in range(3):
        pieces.append(rest.astype(jnp.bfloat16))
        rest = rest - pieces[-1].astype(jnp.float32)
    return pieces


def stat_rows(peak, total, lanes, sublanes):
    return row_stats(as_row(peak, lanes), as_row(total, lanes), sublanes)


def row_stats(peak, total, sublanes):
    lanes = peak.shape[1]
    pieces = [*thirds(peak), *thirds(total)]
    wide = [piece.astype(jnp.float32) for piece in pieces]
    pad = jnp.zeros((sublanes - len(wide), lanes), jnp.float32)
    return jnp.concatenate([*wide, pad], axis=0)


def joined_thirds(rows):
    return (rows[0] + rows[1]) + rows[2]


def attention_kernel(
    drafts,
    kind_ref,
    cache_ref,
    sink_ref,
    window_ref,
    ret_key_ref,
    ret_value_ref,
    str_key_ref,
    str_value_ref,
    *refs,
):
    near = (len(refs) - 2) // 2
    part_refs, out_refs = refs[:near], refs[near : 2 * near]
    entries_ref, out_ref = refs[2 * near :]
    requests, retrieval, block, head_dim = ret_value_ref.shape
    position = lax.axis_index("seq")
    for distance, part_ref in enumerate(part_refs):
        for group in range(part_ref.shape[0]):
            chunk = chunk_of(position, near, distance, group)
            entries_ref[chunk] = part_ref[group]
    tokens = requests * drafts
    chunks, all_rows, _ = entries_ref.shape
    head_rows = all_rows - tokens
    per_head = chunks // kind_ref.shape[0]
    rows = per_head * head_rows
    row = lax.broadcasted_iota(jnp.int32, (rows, 1), 0)
    request_of_row = (row % tokens) // drafts

    def by_request(values):
        picked = values[0]
        for b in range(1, requests):
            picked = jnp.where(request_of_row == b, values[b], picked)
        return picked

    def limit(ref):
        return by_request([ref[b] for b in range(requests)])

    def weighed(flag, rank, keys, visible):
        head = head_of(kind_ref, flag, rank)
        queries = jnp.concatenate(
            [entries_ref[head * per_head + half, :head_rows, :] for half in range(per_head)], axis=0
        )
        own = [jnp.where(request_of_row == b, queries, 0) for b in range(requests)]
        scores = dot_keys(jnp.concatenate(own, axis=1), jnp.concatenate(keys, axis=1))
        return head, *masked_weights(scores * head_dim ** (-0.5), visible)

    def mix(weights, values):
        return jnp.dot(
            weights, jnp.concatenate(values, axis=1), preferred_element_type=jnp.float32
        )

    def store(head, peak, total, mixed):
        mixed = by_request([mixed[:, b * head_dim : (b + 1) * head_dim] for b in range(requests)])
        for half in range(per_head):
            span = slice(half * head_rows, (half + 1) * head_rows)
            block_rows = jnp.concatenate(
                [mixed[span], stat_rows(peak[span], total[span], head_dim, tokens)], axis=0
            )
            out_ref[head * per_head + half] = block_rows.astype(jnp.bfloat16)

    def of_rank(ref, rank):
        return [ref[b, rank] for b in range(requests)]

    slots = str_key_ref.shape[2]
    slot = position * slots + lax.broadcasted_iota(jnp.int32, (rows, slots), 1)
    recent = (slot >= SINK_CAP) & (slot < SINK_CAP + limit(window_ref))
    held = (slot < limit(sink_ref)) | recent
    running = range(str_key_ref.shape[1])
    ready = [weighed(0, rank, of_rank(str_key_ref, rank), held) for rank in running]
    for rank in running:
        head, peak, total, weights = ready[rank]
        store(head, peak, total, mix(weights, of_rank(str_value_ref, rank)))
    place = position * block + lax.broadcasted_iota(jnp.int32, (rows, block), 1)
    filled = place < limit(cache_ref)
    ready = [weighed(1, rank, of_rank(ret_key_ref, rank), filled) for rank in range(retrieval)]
    for rank in range(retrieval):
        head, peak, total, weights = ready[rank]
        store(head, peak, total, mix(weights, of_rank(ret_value_ref, rank)))
    for distance, part_ref in enumerate(out_refs):
        for group in range(part_ref.shape[0]):
            part_ref[group] = out_ref[chunk_of(position, near, distance, group)]


def merged(parts, rows):
    stats = [part[rows:] for part in parts]

    def stacked(first):
        return joined_thirds(
            [
                jnp.concatenate([stat[r : r + 1] for stat in stats], axis=0)
                for r in range(first, first + 3)
            ]
        )

    peaks, totals = stacked(0), stacked(3)
    peak = jnp.max(peaks, axis=0, keepdims=True)
    factors = jnp.exp(peaks - peak)
    total = jnp.sum(factors * totals, axis=0, keepdims=True)
    mixed = [
        as_column(factors[index : index + 1], rows) * part[:rows]
        for index, part in enumerate(parts)
    ]
    return peak, total, functools.reduce(jnp.add, mixed)


def merge_kernel(tokens, near, *refs):
    parts, out_refs = refs[:near], refs[near:]
    rows = out_refs[0].shape[0] - tokens
    group = lax.axis_index("seq") // near
    for distance, out in enumerate(out_refs):
        chunk = group ^ distance
        peak, total, mixed = merged([part[chunk].astype(jnp.float32) for part in parts], rows)
        stats = row_stats(peak, total, tokens)
        out[...] = jnp.concatenate([mixed, stats], axis=0).astype(out.dtype)


def fresh_kernel(kv_heads, requests, drafts, entries_ref, out_ref):
    position = lax.axis_index("seq")
    tokens = requests * drafts
    chunks, all_rows, head_dim = entries_ref.shape
    rows = all_rows - tokens
    head = position // (chunks // kv_heads)
    queries = entries_ref[position, :rows, :]
    keys = entries_ref[head, rows:, :]
    values = entries_ref[kv_heads + head, rows:, :]
    of_row = lax.broadcasted_iota(jnp.int32, (rows, tokens), 0) % tokens
    of_key = lax.broadcasted_iota(jnp.int32, (rows, tokens), 1)
    visible = (of_row // drafts == of_key // drafts) & (of_key <= of_row)
    peak, total, weights = masked_weights(dot_keys(queries, keys) * head_dim ** (-0.5), visible)
    out_ref[:rows, :] = jnp.dot(weights, values, preferred_element_type=jnp.float32)
    out_ref[rows:, :] = stat_rows(peak, total, head_dim, tokens)


def output_kernel(tokens, *refs):
    *part_refs, fresh_ref, weight_ref, out_ref = refs
    rows = fresh_ref.shape[0] - tokens
    parts = [part[...].astype(jnp.float32) for part in part_refs]
    _, total, mixed = merged([*parts, fresh_ref[...]], rows)
    attended = mixed / as_column(total, rows)
    attention = jnp.concatenate(
        [attended[r : r + tokens] for r in range(0, rows, tokens)], axis=1
    ).astype(jnp.bfloat16)
    chunks, _, width = out_ref.shape
    for chunk in range(chunks):
        out_ref[chunk] = jnp.dot(
            attention,
            weight_ref[:, chunk * width : (chunk + 1) * width],
            preferred_element_type=jnp.float32,
        ).astype(jnp.bfloat16)


def on_core(kernel, out_shape, limit, *args, streamed=(), scratch=(), cost=None):
    vmem = pl.BlockSpec(memory_space=pltpu.VMEM)
    smem = pl.BlockSpec(memory_space=pltpu.SMEM)
    scalars = [arg.dtype == jnp.int32 for arg in args]
    placed = [
        arg if scalar else pltpu.with_memory_space_constraint(arg, pltpu.VMEM)
        for arg, scalar in zip(args, scalars)
    ]
    specs = [smem if scalar else vmem for scalar in scalars]
    return pl.pallas_call(
        kernel,
        out_shape=out_shape,
        in_specs=specs + [pl.BlockSpec(memory_space=pltpu.HBM)] * len(streamed),
        scratch_shapes=scratch,
        compiler_params=pltpu.CompilerParams(vmem_limit_bytes=limit * 2**20),
        cost_estimate=cost,
    )(*placed, *(pltpu.with_memory_space_constraint(arg, pltpu.HBM) for arg in streamed))


def shaped(*shape, dtype=jnp.float32):
    return jax.ShapeDtypeStruct(shape, dtype)


def per_device_heads(
    hidden,
    norm_gain,
    q_weight,
    kv_weight,
    out_weight,
    head_kind,
    ret_keys,
    ret_values,
    stream_keys,
    stream_values,
    cache_len,
    sink_len,
    window_len,
):
    requests, drafts, local_width = hidden.shape
    kv_heads = head_kind.shape[0]
    head_dim = ret_keys.shape[3]
    devices = lax.axis_size("seq")
    tokens = requests * drafts
    query_width = q_weight.shape[1] // devices
    rows = tokens * (query_width // head_dim)
    near = min(4, devices)
    far = devices // near
    hint = pl.CostEstimate(
        flops=2 * tokens * devices * devices * q_weight.size,
        bytes_accessed=hidden.size,
        transcendentals=0,
    )
    squares = on_core(squares_kernel, shaped(tokens, head_dim), 4, hidden, cost=hint)
    squares = paired_sum([squares, *from_peers(squares, 1, near)])
    squares = [squares, *from_peers(squares, near, far)]
    gain = norm_gain[None, :]

    def projected(distances):
        return on_core(
            functools.partial(projection_kernel, local_width * devices, far, near, distances),
            [shaped(far, rows + tokens, head_dim)] * len(distances),
            8,
            *squares,
            hidden,
            gain,
            q_weight,
            kv_weight,
        )

    distances = [*range(near // 2, near), *range(near // 2)]
    part_entries = projected(distances[: near // 2]) + projected(distances[near // 2 :])
    own = part_entries[distances.index(0)]
    others = [
        from_peer(part_entries[distances.index(distance)], distance) for distance in range(1, near)
    ]
    chip_entries = on_core(
        sum_kernel, shaped(far, rows + tokens, head_dim), 4, own, *others, cost=hint
    )
    own_entries = on_core(
        sum_kernel,
        shaped(far, rows + tokens, head_dim, dtype=jnp.bfloat16),
        4,
        chip_entries,
        *from_peers(chip_entries, near, far),
    )
    blocks = (devices, rows + tokens, head_dim)
    *part_out, entries = on_core(
        functools.partial(attention_kernel, drafts),
        [shaped(far, *blocks[1:], dtype=jnp.bfloat16)] * near
        + [pltpu.VMEM(blocks, jnp.bfloat16)],
        16,
        head_kind,
        cache_len,
        sink_len,
        window_len,
        ret_keys,
        ret_values,
        stream_keys,
        stream_values,
        own_entries,
        *from_peers(own_entries, 1, near),
        scratch=[pltpu.VMEM(blocks, jnp.bfloat16)],
    )
    new_entries = entries[:, rows:, :].transpose(1, 0, 2).reshape(requests, drafts, -1)
    own_out = part_out[0]
    near_out = [from_peer(part_out[distance], distance) for distance in reversed(range(1, near))]
    fresh = on_core(
        functools.partial(fresh_kernel, kv_heads, requests, drafts),
        shaped(rows + tokens, head_dim),
        4,
        entries,
    )
    chip_out = on_core(
        functools.partial(merge_kernel, tokens, near),
        [shaped(rows + tokens, head_dim, dtype=jnp.bfloat16)] * far,
        4,
        own_out,
        *near_out,
        cost=hint,
    )
    far_out = [
        from_peer(chip_out[distance], near * distance) for distance in reversed(range(1, far))
    ]
    part_output = on_core(
        functools.partial(output_kernel, tokens),
        shaped(devices, tokens, out_weight.shape[1] // devices, dtype=jnp.bfloat16),
        8,
        chip_out[0],
        *far_out,
        fresh,
        out_weight,
    )
    own_output = jnp.sum(exchanged(part_output).astype(jnp.float32), axis=0)
    layer_output = own_output.reshape(requests, drafts, local_width).astype(jnp.bfloat16)
    return (layer_output, new_entries)


def per_device(*args):
    hidden, _, q_weight, kv_weight, _, head_kind, ret_keys, _, stream_keys = args[:9]
    devices = lax.axis_size("seq")
    kv_heads, head_dim = head_kind.shape[0], ret_keys.shape[3]
    whole_heads = (
        (hidden.shape[0] * hidden.shape[1]) % 8 == 0
        and q_weight.shape[1] % (devices * head_dim) == 0
        and kv_weight.shape[1] == devices * head_dim
        and devices == 2 * kv_heads
        and ret_keys.shape[1] == stream_keys.shape[1]
    )
    return (per_device_heads if whole_heads else per_device_any)(*args)


def solution(mesh):
    in_specs = (
        P("groups", None, "seq"),
        P("seq"),
        P("seq", None),
        P("seq", None),
        P("seq", None),
        P(),
        P("groups", None, "seq", None),
        P("groups", None, "seq", None),
        P("groups", None, "seq", None),
        P("groups", None, "seq", None),
        P("groups"),
        P("groups"),
        P("groups"),
    )
    out_specs = (P("groups", None, "seq"), P("groups", None, None))
    return jax.shard_map(
        per_device, mesh=mesh, in_specs=in_specs, out_specs=out_specs, check_vma=False
    )
```

```python
import functools

import jax
import jax.numpy as jnp
from jax import lax
from jax.experimental import pallas as pl
from jax.experimental.pallas import tpu as pltpu
from jax.sharding import PartitionSpec as P


SINK_CAP = 128


epsilon = 1e-05
floor_score = -1e30


def exchanged(parts):
    return lax.all_to_all(parts, "seq", 0, 0, tiled=True)


def summed_over_devices(value):
    devices = lax.axis_size("seq")
    step = 1
    while step < devices:
        value = value + lax.ppermute(value, "seq", [(i, i ^ step) for i in range(devices)])
        step *= 2
    return value


def column_blocks(rows, blocks):
    return rows.reshape(rows.shape[0], blocks, -1).transpose(1, 0, 2)


def block_stats(queries, cache_keys, cache_values, visible, score_scale):
    scores = (
        jnp.einsum("bhqd,bhld->bhql", queries, cache_keys, preferred_element_type=jnp.float32)
        * score_scale
    )
    scores = jnp.where(visible, scores, floor_score)
    peak_score = jnp.max(scores, axis=-1)
    weights = jnp.where(visible, jnp.exp(scores - peak_score[..., None]), 0.0)
    weight_total = jnp.sum(weights, axis=-1)
    block_out = jnp.einsum(
        "bhql,bhld->bhqd",
        weights.astype(jnp.bfloat16),
        cache_values,
        preferred_element_type=jnp.float32,
    )
    return (peak_score, weight_total, block_out)


def spread_rows(values_in, selector):
    return jnp.einsum("brq,gr->bgq", values_in, selector, precision=lax.Precision.HIGHEST)


def spread_vectors(values_in, selector):
    return jnp.einsum("brqd,gr->bgqd", values_in, selector, precision=lax.Precision.HIGHEST)


def per_device_any(
    hidden,
    norm_gain,
    q_weight,
    kv_weight,
    out_weight,
    head_kind,
    ret_keys,
    ret_values,
    stream_keys,
    stream_values,
    cache_len,
    sink_len,
    window_len,
):
    requests, drafts, local_width = hidden.shape
    kv_heads = head_kind.shape[0]
    head_dim = ret_keys.shape[3]
    retrieval = ret_keys.shape[1]
    running = stream_keys.shape[1]
    head_count = q_weight.shape[1] // head_dim
    group_size = head_count // kv_heads
    query_rows = drafts * group_size
    devices = lax.axis_size("seq")
    position = lax.axis_index("seq")
    tokens = requests * drafts
    hidden32 = hidden.astype(jnp.float32)
    squares = summed_over_devices(jnp.sum(hidden32 * hidden32, axis=-1))
    inverse = lax.rsqrt(squares / (local_width * devices) + epsilon)
    normed = (hidden32 * inverse[..., None] * norm_gain.astype(jnp.float32)).astype(jnp.bfloat16)
    flat_rows = normed.reshape(tokens, local_width)
    part_query = jnp.dot(flat_rows, q_weight, preferred_element_type=jnp.float32)
    part_fresh = jnp.dot(flat_rows, kv_weight, preferred_element_type=jnp.float32)
    sums = jnp.sum(
        exchanged(
            jnp.concatenate(
                [column_blocks(part_query, devices), column_blocks(part_fresh, devices)], axis=-1
            )
        ),
        axis=0,
    ).astype(jnp.bfloat16)
    gathered = exchanged(jnp.broadcast_to(sums[None], (devices, *sums.shape)))
    query_width = q_weight.shape[1] // devices
    queries = gathered[..., :query_width].transpose(1, 0, 2).reshape(tokens, -1)
    new_entries = gathered[..., query_width:].transpose(1, 0, 2).reshape(tokens, -1)
    grouped = (
        queries.reshape(requests, drafts, kv_heads, group_size, head_dim)
        .transpose(0, 2, 1, 3, 4)
        .reshape(requests, kv_heads, query_rows, head_dim)
    )
    fresh_split = new_entries.reshape(requests, drafts, 2, kv_heads, head_dim)
    new_keys = fresh_split[:, :, 0].transpose(0, 2, 1, 3)
    new_values = fresh_split[:, :, 1].transpose(0, 2, 1, 3)
    kind_flag = head_kind == 1
    rank_ret = jnp.cumsum(head_kind) - 1
    rank_str = jnp.cumsum(1 - head_kind) - 1
    select_ret = (
        kind_flag[:, None] & (rank_ret[:, None] == jnp.arange(retrieval)[None, :])
    ).astype(jnp.float32)
    select_str = (
        jnp.logical_not(kind_flag)[:, None] & (rank_str[:, None] == jnp.arange(running)[None, :])
    ).astype(jnp.float32)
    ret_queries = jnp.einsum(
        "bgqd,gr->brqd",
        grouped,
        select_ret.astype(jnp.bfloat16),
        preferred_element_type=jnp.float32,
    ).astype(jnp.bfloat16)
    str_queries = jnp.einsum(
        "bgqd,gr->brqd",
        grouped,
        select_str.astype(jnp.bfloat16),
        preferred_element_type=jnp.float32,
    ).astype(jnp.bfloat16)
    score_scale = head_dim ** (-0.5)
    cache_block = ret_keys.shape[2]
    cache_pos = position * cache_block + jnp.arange(cache_block)
    ret_visible = (cache_pos[None, :] < cache_len[:, None])[:, None, None, :]
    slot_block = stream_keys.shape[2]
    slot_pos = (position * slot_block + jnp.arange(slot_block))[None, :]
    sink_part = slot_pos < sink_len[:, None]
    recent_part = (slot_pos >= SINK_CAP) & (slot_pos < SINK_CAP + window_len[:, None])
    str_visible = (sink_part | recent_part)[:, None, None, :]
    ret_peak, ret_total, ret_out = block_stats(
        ret_queries, ret_keys, ret_values, ret_visible, score_scale
    )
    str_peak, str_total, str_out = block_stats(
        str_queries, stream_keys, stream_values, str_visible, score_scale
    )
    peak_all = spread_rows(ret_peak, select_ret) + spread_rows(str_peak, select_str)
    total_all = spread_rows(ret_total, select_ret) + spread_rows(str_total, select_str)
    out_all = spread_vectors(ret_out, select_ret) + spread_vectors(str_out, select_str)
    token_of_row = jnp.arange(query_rows) // group_size
    new_visible = jnp.arange(drafts)[None, :] <= token_of_row[:, None]
    new_peak, new_total, new_out = block_stats(
        grouped, new_keys, new_values, new_visible, score_scale
    )
    own_width = out_weight.shape[0]
    block_heads = max(1, own_width // head_dim)

    def by_token(value):
        split = value.reshape(requests, kv_heads, drafts, group_size, -1)
        return split.transpose(0, 2, 1, 3, 4).reshape(tokens, head_count, -1)

    first_head = (jnp.arange(devices) * own_width) // head_dim
    block_head = first_head[:, None] + jnp.arange(block_heads)[None, :]

    def head_blocks(value):
        rows = by_token(value).reshape(tokens, head_count)
        return jnp.take(rows, block_head.reshape(-1), axis=1).reshape(tokens, devices, -1).transpose(1, 0, 2)

    received = exchanged(
        jnp.concatenate(
            [
                column_blocks(by_token(out_all).reshape(tokens, -1), devices),
                head_blocks(peak_all),
                head_blocks(total_all),
            ],
            axis=-1,
        )
    )
    got_out = received[..., :own_width].reshape(devices, tokens, block_heads, -1)
    got_peak = received[..., own_width : own_width + block_heads]
    got_total = received[..., own_width + block_heads :]

    def own_heads(value):
        blocks = column_blocks(by_token(value).reshape(tokens, -1), devices)
        return lax.dynamic_index_in_dim(blocks, position, 0, False).reshape(tokens, block_heads, -1)

    own_new_out = own_heads(new_out)
    own_new_peak = lax.dynamic_index_in_dim(head_blocks(new_peak), position, 0, False)
    own_new_total = lax.dynamic_index_in_dim(head_blocks(new_total), position, 0, False)
    top_score = jnp.maximum(jnp.max(got_peak, axis=0), own_new_peak)
    cache_factor = jnp.exp(got_peak - top_score[None])
    new_factor = jnp.exp(own_new_peak - top_score)
    denominator = jnp.sum(got_total * cache_factor, axis=0) + own_new_total * new_factor
    attended = (
        jnp.sum(got_out * cache_factor[..., None], axis=0) + own_new_out * new_factor[..., None]
    ) / denominator[..., None]
    own_attention = attended.reshape(tokens, own_width).astype(jnp.bfloat16)
    part_output = jnp.dot(own_attention, out_weight, preferred_element_type=jnp.float32)
    own_output = jnp.sum(exchanged(column_blocks(part_output, devices)), axis=0)
    layer_output = own_output.reshape(requests, drafts, local_width).astype(jnp.bfloat16)
    return (layer_output, new_entries.reshape(requests, drafts, 2 * kv_heads * head_dim))


def flat_tokens(ref):
    return jnp.concatenate([ref[b].astype(jnp.float32) for b in range(ref.shape[0])], axis=0)


def squares_kernel(hidden_ref, *out_refs):
    rows = flat_tokens(hidden_ref)
    total = jnp.sum(rows * rows, axis=1, keepdims=True)
    for out in out_refs:
        out[...] = jnp.broadcast_to(total, out.shape)


def from_peer(value, distance):
    devices = lax.axis_size("seq")
    return lax.ppermute(value, "seq", [(i, i ^ distance) for i in range(devices)])


def steps_of(radix):
    return (0, *sorted(range(1, radix), key=lambda step: (-step.bit_length(), step)))


def from_peers(values, low):
    return [from_peer(values[step - 1], low * step) for step in steps_of(len(values) + 1)[1:]]


def by_step(values):
    placed = dict(zip(steps_of(len(values)), values))
    return [placed[step] for step in range(len(values))]


def paired_sum(values):
    while len(values) > 1:
        values = [left + right for left, right in zip(values[::2], values[1::2])]
    return values[0]


def chunk_of(position, near, distance, far):
    return far * near + ((position & (near - 1)) ^ distance)


def projection_kernel(width, parts, near, distances, *refs):
    squares = refs[:parts]
    hidden_ref, gain_ref, query_ref, fresh_ref = refs[parts : parts + 4]
    out_refs = refs[parts + 4 :]
    total = paired_sum([ref[...] for ref in by_step(squares)])
    inverse = lax.rsqrt(total[:, :1] / width + epsilon)
    gain = gain_ref[...].astype(jnp.float32)
    normed = (flat_tokens(hidden_ref) * inverse * gain).astype(jnp.bfloat16)
    tokens = normed.shape[0]
    position = lax.axis_index("seq")
    far, _, lanes = out_refs[0].shape
    query_width = query_ref.shape[1] // (near * far)
    pieces = query_width // lanes

    def times(ref, chunk, size):
        columns = ref[:, pl.ds(pl.multiple_of(chunk * size, size), size)]
        return jnp.dot(normed, columns, preferred_element_type=jnp.float32)

    for distance, out in zip(distances, out_refs):
        for group in range(far):
            chunk = chunk_of(position, near, distance, group)
            part = times(query_ref, chunk, query_width)
            for piece in range(pieces):
                out[group, piece * tokens : (piece + 1) * tokens, :] = part[
                    :, piece * lanes : (piece + 1) * lanes
                ]
            out[group, pieces * tokens :, :] = times(fresh_ref, chunk, lanes)


def sum_kernel(count, *refs):
    total = paired_sum([ref[...] for ref in by_step(refs[:count])])
    for out in refs[count:]:
        out[...] = total.astype(out.dtype)


def head_of(kind_ref, flag, rank):
    found, before = jnp.int32(0), jnp.int32(0)
    for head in range(kind_ref.shape[0]):
        is_kind = kind_ref[head] == flag
        found = jnp.where(is_kind & (before == rank), head, found)
        before = before + is_kind.astype(jnp.int32)
    return found


def diagonal_of(rows, lanes):
    return lax.broadcasted_iota(jnp.int32, (rows, lanes), 0) == lax.broadcasted_iota(
        jnp.int32, (rows, lanes), 1
    )


def as_row(column, lanes):
    return jnp.sum(
        jnp.where(diagonal_of(column.shape[0], lanes), column, 0.0), axis=0, keepdims=True
    )


def as_column(row, rows):
    return jnp.sum(jnp.where(diagonal_of(rows, row.shape[1]), row, 0.0), axis=1, keepdims=True)


def masked_weights(scores, visible):
    scores = jnp.where(visible, scores, floor_score)
    peak = jnp.max(scores, axis=1, keepdims=True)
    weights = jnp.exp(scores - jnp.maximum(peak, 0.5 * floor_score))
    return peak, jnp.sum(weights, axis=1, keepdims=True), weights.astype(jnp.bfloat16)


def dot_keys(queries, keys):
    return lax.dot_general(
        queries, keys, (((1,), (1,)), ((), ())), preferred_element_type=jnp.float32
    )


def thirds(row):
    rest, pieces = row, []
    for _ in range(3):
        pieces.append(rest.astype(jnp.bfloat16))
        rest = rest - pieces[-1].astype(jnp.float32)
    return pieces


def stat_rows(peak, total, lanes, sublanes):
    return row_stats(as_row(peak, lanes), as_row(total, lanes), sublanes)


def row_stats(peak, total, sublanes):
    lanes = peak.shape[1]
    pieces = [*thirds(peak), *thirds(total)]
    wide = [piece.astype(jnp.float32) for piece in pieces]
    pad = jnp.zeros((sublanes - len(wide), lanes), jnp.float32)
    return jnp.concatenate([*wide, pad], axis=0)


def joined_thirds(rows):
    return (rows[0] + rows[1]) + rows[2]


def attention_kernel(
    drafts,
    kind_ref,
    cache_ref,
    sink_ref,
    window_ref,
    ret_key_ref,
    ret_value_ref,
    str_key_ref,
    str_value_ref,
    *refs,
):
    near = (len(refs) - 2) // 2
    part_refs, out_refs = refs[:near], refs[near : 2 * near]
    entries_ref, out_ref = refs[2 * near :]
    requests, retrieval, block, head_dim = ret_value_ref.shape
    position = lax.axis_index("seq")
    for distance, part_ref in enumerate(by_step(part_refs)):
        for group in range(part_ref.shape[0]):
            chunk = chunk_of(position, near, distance, group)
            entries_ref[chunk] = part_ref[group]
    tokens = requests * drafts
    chunks, all_rows, _ = entries_ref.shape
    head_rows = all_rows - tokens
    per_head = chunks // kind_ref.shape[0]
    rows = per_head * head_rows
    row = lax.broadcasted_iota(jnp.int32, (rows, 1), 0)
    request_of_row = (row % tokens) // drafts

    def by_request(values):
        picked = values[0]
        for b in range(1, requests):
            picked = jnp.where(request_of_row == b, values[b], picked)
        return picked

    def limit(ref):
        return by_request([ref[b] for b in range(requests)])

    def weighed(flag, rank, keys, visible):
        head = head_of(kind_ref, flag, rank)
        queries = jnp.concatenate(
            [entries_ref[head * per_head + half, :head_rows, :] for half in range(per_head)], axis=0
        )
        own = [jnp.where(request_of_row == b, queries, 0) for b in range(requests)]
        scores = dot_keys(jnp.concatenate(own, axis=1), jnp.concatenate(keys, axis=1))
        return head, *masked_weights(scores * head_dim ** (-0.5), visible)

    def mix(weights, values):
        return jnp.dot(
            weights, jnp.concatenate(values, axis=1), preferred_element_type=jnp.float32
        )

    def store(head, peak, total, mixed):
        mixed = by_request([mixed[:, b * head_dim : (b + 1) * head_dim] for b in range(requests)])
        for half in range(per_head):
            span = slice(half * head_rows, (half + 1) * head_rows)
            block_rows = jnp.concatenate(
                [mixed[span], stat_rows(peak[span], total[span], head_dim, tokens)], axis=0
            )
            out_ref[head * per_head + half] = block_rows.astype(jnp.bfloat16)

    def of_rank(ref, rank):
        return [ref[b, rank] for b in range(requests)]

    slots = str_key_ref.shape[2]
    slot = position * slots + lax.broadcasted_iota(jnp.int32, (rows, slots), 1)
    recent = (slot >= SINK_CAP) & (slot < SINK_CAP + limit(window_ref))
    held = (slot < limit(sink_ref)) | recent
    running = range(str_key_ref.shape[1])
    ready = [weighed(0, rank, of_rank(str_key_ref, rank), held) for rank in running]
    for rank in running:
        head, peak, total, weights = ready[rank]
        store(head, peak, total, mix(weights, of_rank(str_value_ref, rank)))
    place = position * block + lax.broadcasted_iota(jnp.int32, (rows, block), 1)
    filled = place < limit(cache_ref)
    ready = [weighed(1, rank, of_rank(ret_key_ref, rank), filled) for rank in range(retrieval)]
    for rank in range(retrieval):
        head, peak, total, weights = ready[rank]
        store(head, peak, total, mix(weights, of_rank(ret_value_ref, rank)))
    for distance, part_ref in enumerate(out_refs):
        for group in range(part_ref.shape[0]):
            part_ref[group] = out_ref[chunk_of(position, near, distance, group)]


def merged(parts, rows):
    stats = [part[rows:] for part in parts]

    def stacked(first):
        return joined_thirds(
            [
                jnp.concatenate([stat[r : r + 1] for stat in stats], axis=0)
                for r in range(first, first + 3)
            ]
        )

    peaks, totals = stacked(0), stacked(3)
    peak = jnp.max(peaks, axis=0, keepdims=True)
    factors = jnp.exp(peaks - peak)
    total = jnp.sum(factors * totals, axis=0, keepdims=True)
    mixed = [
        as_column(factors[index : index + 1], rows) * part[:rows]
        for index, part in enumerate(parts)
    ]
    return peak, total, functools.reduce(jnp.add, mixed)


def merge_kernel(tokens, near, *refs):
    parts, out_refs = refs[:near], refs[near:]
    rows = out_refs[0].shape[0] - tokens
    group = lax.axis_index("seq") // near
    for distance, out in enumerate(out_refs):
        chunk = group ^ distance
        peak, total, mixed = merged([part[chunk].astype(jnp.float32) for part in parts], rows)
        stats = row_stats(peak, total, tokens)
        out[...] = jnp.concatenate([mixed, stats], axis=0).astype(out.dtype)


def fresh_kernel(kv_heads, requests, drafts, entries_ref, out_ref):
    position = lax.axis_index("seq")
    tokens = requests * drafts
    chunks, all_rows, head_dim = entries_ref.shape
    rows = all_rows - tokens
    head = position // (chunks // kv_heads)
    queries = entries_ref[position, :rows, :]
    keys = entries_ref[head, rows:, :]
    values = entries_ref[kv_heads + head, rows:, :]
    of_row = lax.broadcasted_iota(jnp.int32, (rows, tokens), 0) % tokens
    of_key = lax.broadcasted_iota(jnp.int32, (rows, tokens), 1)
    visible = (of_row // drafts == of_key // drafts) & (of_key <= of_row)
    peak, total, weights = masked_weights(dot_keys(queries, keys) * head_dim ** (-0.5), visible)
    out_ref[:rows, :] = jnp.dot(weights, values, preferred_element_type=jnp.float32)
    out_ref[rows:, :] = stat_rows(peak, total, head_dim, tokens)


def mixed_kernel(tokens, near, distances, *refs):
    count = len(refs) - 3 - len(distances)
    part_refs, (fresh_ref, weight_ref) = refs[:count], refs[count : count + 2]
    attention_ref, out_refs = refs[count + 2], refs[count + 3 :]
    rows = fresh_ref.shape[0] - tokens
    parts = [part[...].astype(jnp.float32) for part in part_refs]
    _, total, mixed = merged([*parts, fresh_ref[...]], rows)
    attended = mixed / as_column(total, rows)
    attention_ref[...] = jnp.concatenate(
        [attended[r : r + tokens] for r in range(0, rows, tokens)], axis=1
    ).astype(jnp.bfloat16)
    output_kernel(near, distances, attention_ref, weight_ref, *out_refs)


def output_kernel(near, distances, attention_ref, weight_ref, *out_refs):
    position = lax.axis_index("seq")
    for distance, out in zip(distances, out_refs):
        far, _, width = out.shape
        for group in range(far):
            chunk = chunk_of(position, near, distance, group)
            columns = weight_ref[:, pl.ds(pl.multiple_of(chunk * width, width), width)]
            out[group] = jnp.dot(
                attention_ref[...], columns, preferred_element_type=jnp.float32
            ).astype(out.dtype)


def fold_kernel(near, *refs):
    parts, out_refs = refs[:near], refs[near:]
    group = lax.axis_index("seq") // near
    for distance, out in enumerate(out_refs):
        chunk = group ^ distance
        out[...] = paired_sum([part[chunk].astype(jnp.float32) for part in parts]).astype(out.dtype)


def last_kernel(*refs):
    total = paired_sum([ref[...].astype(jnp.float32) for ref in refs[:-1]])
    drafts = refs[-1].shape[1]
    for request in range(refs[-1].shape[0]):
        span = slice(request * drafts, (request + 1) * drafts)
        refs[-1][request] = total[span].astype(refs[-1].dtype)


def on_core(kernel, out_shape, limit, *args, streamed=(), scratch=(), cost=None):
    vmem = pl.BlockSpec(memory_space=pltpu.VMEM)
    smem = pl.BlockSpec(memory_space=pltpu.SMEM)
    scalars = [arg.dtype == jnp.int32 for arg in args]
    placed = [
        arg if scalar else pltpu.with_memory_space_constraint(arg, pltpu.VMEM)
        for arg, scalar in zip(args, scalars)
    ]
    specs = [smem if scalar else vmem for scalar in scalars]
    return pl.pallas_call(
        kernel,
        out_shape=out_shape,
        in_specs=specs + [pl.BlockSpec(memory_space=pltpu.HBM)] * len(streamed),
        scratch_shapes=scratch,
        compiler_params=pltpu.CompilerParams(vmem_limit_bytes=limit * 2**20),
        cost_estimate=cost,
    )(*placed, *(pltpu.with_memory_space_constraint(arg, pltpu.HBM) for arg in streamed))


def shaped(*shape, dtype=jnp.float32):
    return jax.ShapeDtypeStruct(shape, dtype)


def per_device_heads(
    hidden,
    norm_gain,
    q_weight,
    kv_weight,
    out_weight,
    head_kind,
    ret_keys,
    ret_values,
    stream_keys,
    stream_values,
    cache_len,
    sink_len,
    window_len,
):
    requests, drafts, local_width = hidden.shape
    kv_heads = head_kind.shape[0]
    head_dim = ret_keys.shape[3]
    devices = lax.axis_size("seq")
    tokens = requests * drafts
    query_width = q_weight.shape[1] // devices
    rows = tokens * (query_width // head_dim)
    near = min(4, devices)
    far = devices // near
    hint = pl.CostEstimate(
        flops=2 * tokens * devices * devices * q_weight.size,
        bytes_accessed=hidden.size,
        transcendentals=0,
    )
    def copies(count, shape, dtype, *values, cost=None):
        return on_core(
            functools.partial(sum_kernel, len(values)),
            [shaped(*shape, dtype=dtype)] * count,
            4,
            *values,
            cost=cost,
        )

    own, *sent = on_core(
        squares_kernel, [shaped(tokens, head_dim)] * near, 4, hidden, cost=hint
    )
    own, *sent = copies(
        far, (tokens, head_dim), jnp.float32, own, *from_peers(sent, 1)
    )
    squares = [own, *from_peers(sent, near)]
    gain = norm_gain[None, :]

    def projected(distances):
        return on_core(
            functools.partial(projection_kernel, local_width * devices, far, near, distances),
            [shaped(far, rows + tokens, head_dim)] * len(distances),
            8,
            *squares,
            hidden,
            gain,
            q_weight,
            kv_weight,
        )

    distances = [*range(near // 2, near), *range(near // 2)]
    part_entries = projected(distances[: near // 2]) + projected(distances[near // 2 :])
    own = part_entries[distances.index(0)]
    others = [
        from_peer(part_entries[distances.index(step)], step) for step in steps_of(near)[1:]
    ]
    block = (far, rows + tokens, head_dim)
    own, *sent = copies(far, block, jnp.float32, own, *others, cost=hint)
    own, *sent = copies(near, block, jnp.bfloat16, own, *from_peers(sent, near))
    blocks = (devices, rows + tokens, head_dim)
    *part_out, entries = on_core(
        functools.partial(attention_kernel, drafts),
        [shaped(far, *blocks[1:], dtype=jnp.bfloat16)] * near
        + [pltpu.VMEM(blocks, jnp.bfloat16)],
        16,
        head_kind,
        cache_len,
        sink_len,
        window_len,
        ret_keys,
        ret_values,
        stream_keys,
        stream_values,
        own,
        *from_peers(sent, 1),
        scratch=[pltpu.VMEM(blocks, jnp.bfloat16)],
    )
    new_entries = entries[:, rows:, :].transpose(1, 0, 2).reshape(requests, drafts, -1)
    own_out = part_out[0]
    near_out = from_peers(part_out[1:], 1)
    fresh = on_core(
        functools.partial(fresh_kernel, kv_heads, requests, drafts),
        shaped(rows + tokens, head_dim),
        4,
        entries,
    )
    chip_out = on_core(
        functools.partial(merge_kernel, tokens, near),
        [shaped(rows + tokens, head_dim, dtype=jnp.bfloat16)] * far,
        4,
        own_out,
        *near_out,
        cost=hint,
    )
    far_out = from_peers(chip_out[1:], near)
    width = out_weight.shape[1] // devices
    distances = range(near - 1, near // 2 - 1, -1)
    attention, *part_output = on_core(
        functools.partial(mixed_kernel, tokens, near, distances),
        [pltpu.VMEM((tokens, out_weight.shape[0]), jnp.bfloat16)]
        + [shaped(far, tokens, width, dtype=jnp.bfloat16)] * len(distances),
        8,
        chip_out[0],
        *far_out,
        fresh,
        out_weight,
    )
    near_output = [from_peer(part, distance) for distance, part in zip(distances, part_output)]
    distances = range(near // 2 - 1, -1, -1)
    *part_output, own_output = on_core(
        functools.partial(output_kernel, near, distances),
        [shaped(far, tokens, width, dtype=jnp.bfloat16)] * (len(distances) - 1)
        + [shaped(far, tokens, width)],
        8,
        attention,
        out_weight,
    )
    near_output += [from_peer(part, distance) for distance, part in zip(distances, part_output)]
    own_output, *chip_output = on_core(
        functools.partial(fold_kernel, near),
        [shaped(tokens, width)] + [shaped(tokens, width, dtype=jnp.bfloat16)] * (far - 1),
        4,
        own_output,
        *near_output[::-1],
    )
    layer_output = on_core(
        last_kernel,
        shaped(requests, drafts, width, dtype=jnp.bfloat16),
        4,
        own_output,
        *from_peers(chip_output, near),
    )
    return (layer_output, new_entries)


def per_device(*args):
    hidden, _, q_weight, kv_weight, _, head_kind, ret_keys, _, stream_keys = args[:9]
    devices = lax.axis_size("seq")
    kv_heads, head_dim = head_kind.shape[0], ret_keys.shape[3]
    whole_heads = (
        (hidden.shape[0] * hidden.shape[1]) % 8 == 0
        and q_weight.shape[1] % (devices * head_dim) == 0
        and kv_weight.shape[1] == devices * head_dim
        and devices == 2 * kv_heads
        and ret_keys.shape[1] == stream_keys.shape[1]
    )
    return (per_device_heads if whole_heads else per_device_any)(*args)


def solution(mesh):
    in_specs = (
        P("groups", None, "seq"),
        P("seq"),
        P("seq", None),
        P("seq", None),
        P("seq", None),
        P(),
        P("groups", None, "seq", None),
        P("groups", None, "seq", None),
        P("groups", None, "seq", None),
        P("groups", None, "seq", None),
        P("groups"),
        P("groups"),
        P("groups"),
    )
    out_specs = (P("groups", None, "seq"), P("groups", None, None))
    return jax.shard_map(
        per_device, mesh=mesh, in_specs=in_specs, out_specs=out_specs, check_vma=False
    )
```

```python
import functools

import jax
import jax.numpy as jnp
from jax import lax
from jax.experimental import pallas as pl
from jax.experimental.pallas import tpu as pltpu
from jax.sharding import PartitionSpec as P


SINK_CAP = 128


epsilon = 1e-05
floor_score = -1e30


def exchanged(parts):
    return lax.all_to_all(parts, "seq", 0, 0, tiled=True)


def summed_over_devices(value):
    devices = lax.axis_size("seq")
    step = 1
    while step < devices:
        value = value + lax.ppermute(value, "seq", [(i, i ^ step) for i in range(devices)])
        step *= 2
    return value


def column_blocks(rows, blocks):
    return rows.reshape(rows.shape[0], blocks, -1).transpose(1, 0, 2)


def block_stats(queries, cache_keys, cache_values, visible, score_scale):
    scores = (
        jnp.einsum("bhqd,bhld->bhql", queries, cache_keys, preferred_element_type=jnp.float32)
        * score_scale
    )
    scores = jnp.where(visible, scores, floor_score)
    peak_score = jnp.max(scores, axis=-1)
    weights = jnp.where(visible, jnp.exp(scores - peak_score[..., None]), 0.0)
    weight_total = jnp.sum(weights, axis=-1)
    block_out = jnp.einsum(
        "bhql,bhld->bhqd",
        weights.astype(jnp.bfloat16),
        cache_values,
        preferred_element_type=jnp.float32,
    )
    return (peak_score, weight_total, block_out)


def spread_rows(values_in, selector):
    return jnp.einsum("brq,gr->bgq", values_in, selector, precision=lax.Precision.HIGHEST)


def spread_vectors(values_in, selector):
    return jnp.einsum("brqd,gr->bgqd", values_in, selector, precision=lax.Precision.HIGHEST)


def per_device_any(
    hidden,
    norm_gain,
    q_weight,
    kv_weight,
    out_weight,
    head_kind,
    ret_keys,
    ret_values,
    stream_keys,
    stream_values,
    cache_len,
    sink_len,
    window_len,
):
    requests, drafts, local_width = hidden.shape
    kv_heads = head_kind.shape[0]
    head_dim = ret_keys.shape[3]
    retrieval = ret_keys.shape[1]
    running = stream_keys.shape[1]
    head_count = q_weight.shape[1] // head_dim
    group_size = head_count // kv_heads
    query_rows = drafts * group_size
    devices = lax.axis_size("seq")
    position = lax.axis_index("seq")
    tokens = requests * drafts
    hidden32 = hidden.astype(jnp.float32)
    squares = summed_over_devices(jnp.sum(hidden32 * hidden32, axis=-1))
    inverse = lax.rsqrt(squares / (local_width * devices) + epsilon)
    normed = (hidden32 * inverse[..., None] * norm_gain.astype(jnp.float32)).astype(jnp.bfloat16)
    flat_rows = normed.reshape(tokens, local_width)
    part_query = jnp.dot(flat_rows, q_weight, preferred_element_type=jnp.float32)
    part_fresh = jnp.dot(flat_rows, kv_weight, preferred_element_type=jnp.float32)
    sums = jnp.sum(
        exchanged(
            jnp.concatenate(
                [column_blocks(part_query, devices), column_blocks(part_fresh, devices)], axis=-1
            )
        ),
        axis=0,
    ).astype(jnp.bfloat16)
    gathered = exchanged(jnp.broadcast_to(sums[None], (devices, *sums.shape)))
    query_width = q_weight.shape[1] // devices
    queries = gathered[..., :query_width].transpose(1, 0, 2).reshape(tokens, -1)
    new_entries = gathered[..., query_width:].transpose(1, 0, 2).reshape(tokens, -1)
    grouped = (
        queries.reshape(requests, drafts, kv_heads, group_size, head_dim)
        .transpose(0, 2, 1, 3, 4)
        .reshape(requests, kv_heads, query_rows, head_dim)
    )
    fresh_split = new_entries.reshape(requests, drafts, 2, kv_heads, head_dim)
    new_keys = fresh_split[:, :, 0].transpose(0, 2, 1, 3)
    new_values = fresh_split[:, :, 1].transpose(0, 2, 1, 3)
    kind_flag = head_kind == 1
    rank_ret = jnp.cumsum(head_kind) - 1
    rank_str = jnp.cumsum(1 - head_kind) - 1
    select_ret = (
        kind_flag[:, None] & (rank_ret[:, None] == jnp.arange(retrieval)[None, :])
    ).astype(jnp.float32)
    select_str = (
        jnp.logical_not(kind_flag)[:, None] & (rank_str[:, None] == jnp.arange(running)[None, :])
    ).astype(jnp.float32)
    ret_queries = jnp.einsum(
        "bgqd,gr->brqd",
        grouped,
        select_ret.astype(jnp.bfloat16),
        preferred_element_type=jnp.float32,
    ).astype(jnp.bfloat16)
    str_queries = jnp.einsum(
        "bgqd,gr->brqd",
        grouped,
        select_str.astype(jnp.bfloat16),
        preferred_element_type=jnp.float32,
    ).astype(jnp.bfloat16)
    score_scale = head_dim ** (-0.5)
    cache_block = ret_keys.shape[2]
    cache_pos = position * cache_block + jnp.arange(cache_block)
    ret_visible = (cache_pos[None, :] < cache_len[:, None])[:, None, None, :]
    slot_block = stream_keys.shape[2]
    slot_pos = (position * slot_block + jnp.arange(slot_block))[None, :]
    sink_part = slot_pos < sink_len[:, None]
    recent_part = (slot_pos >= SINK_CAP) & (slot_pos < SINK_CAP + window_len[:, None])
    str_visible = (sink_part | recent_part)[:, None, None, :]
    ret_peak, ret_total, ret_out = block_stats(
        ret_queries, ret_keys, ret_values, ret_visible, score_scale
    )
    str_peak, str_total, str_out = block_stats(
        str_queries, stream_keys, stream_values, str_visible, score_scale
    )
    peak_all = spread_rows(ret_peak, select_ret) + spread_rows(str_peak, select_str)
    total_all = spread_rows(ret_total, select_ret) + spread_rows(str_total, select_str)
    out_all = spread_vectors(ret_out, select_ret) + spread_vectors(str_out, select_str)
    token_of_row = jnp.arange(query_rows) // group_size
    new_visible = jnp.arange(drafts)[None, :] <= token_of_row[:, None]
    new_peak, new_total, new_out = block_stats(
        grouped, new_keys, new_values, new_visible, score_scale
    )
    own_width = out_weight.shape[0]
    block_heads = max(1, own_width // head_dim)

    def by_token(value):
        split = value.reshape(requests, kv_heads, drafts, group_size, -1)
        return split.transpose(0, 2, 1, 3, 4).reshape(tokens, head_count, -1)

    first_head = (jnp.arange(devices) * own_width) // head_dim
    block_head = first_head[:, None] + jnp.arange(block_heads)[None, :]

    def head_blocks(value):
        rows = by_token(value).reshape(tokens, head_count)
        return jnp.take(rows, block_head.reshape(-1), axis=1).reshape(tokens, devices, -1).transpose(1, 0, 2)

    received = exchanged(
        jnp.concatenate(
            [
                column_blocks(by_token(out_all).reshape(tokens, -1), devices),
                head_blocks(peak_all),
                head_blocks(total_all),
            ],
            axis=-1,
        )
    )
    got_out = received[..., :own_width].reshape(devices, tokens, block_heads, -1)
    got_peak = received[..., own_width : own_width + block_heads]
    got_total = received[..., own_width + block_heads :]

    def own_heads(value):
        blocks = column_blocks(by_token(value).reshape(tokens, -1), devices)
        return lax.dynamic_index_in_dim(blocks, position, 0, False).reshape(tokens, block_heads, -1)

    own_new_out = own_heads(new_out)
    own_new_peak = lax.dynamic_index_in_dim(head_blocks(new_peak), position, 0, False)
    own_new_total = lax.dynamic_index_in_dim(head_blocks(new_total), position, 0, False)
    top_score = jnp.maximum(jnp.max(got_peak, axis=0), own_new_peak)
    cache_factor = jnp.exp(got_peak - top_score[None])
    new_factor = jnp.exp(own_new_peak - top_score)
    denominator = jnp.sum(got_total * cache_factor, axis=0) + own_new_total * new_factor
    attended = (
        jnp.sum(got_out * cache_factor[..., None], axis=0) + own_new_out * new_factor[..., None]
    ) / denominator[..., None]
    own_attention = attended.reshape(tokens, own_width).astype(jnp.bfloat16)
    part_output = jnp.dot(own_attention, out_weight, preferred_element_type=jnp.float32)
    own_output = jnp.sum(exchanged(column_blocks(part_output, devices)), axis=0)
    layer_output = own_output.reshape(requests, drafts, local_width).astype(jnp.bfloat16)
    return (layer_output, new_entries.reshape(requests, drafts, 2 * kv_heads * head_dim))


def flat_tokens(ref):
    return jnp.concatenate([ref[b].astype(jnp.float32) for b in range(ref.shape[0])], axis=0)


def squares_kernel(hidden_ref, *out_refs):
    rows = flat_tokens(hidden_ref)
    total = jnp.sum(rows * rows, axis=1, keepdims=True)
    for out in out_refs:
        out[...] = jnp.broadcast_to(total, out.shape)


def from_peer(value, distance):
    devices = lax.axis_size("seq")
    return lax.ppermute(value, "seq", [(i, i ^ distance) for i in range(devices)])


def steps_of(radix, low):
    order = (lambda step: -step) if low == 1 else (lambda step: (-step.bit_length(), step))
    return (0, *sorted(range(1, radix), key=order))


def from_peers(values, low):
    return [from_peer(values[step - 1], low * step) for step in steps_of(len(values) + 1, low)[1:]]


def by_step(values, low):
    placed = dict(zip(steps_of(len(values), low), values))
    return [placed[step] for step in range(len(values))]


def paired_sum(values):
    while len(values) > 1:
        values = [left + right for left, right in zip(values[::2], values[1::2])]
    return values[0]


def chunk_of(position, near, distance, far):
    return far * near + ((position & (near - 1)) ^ distance)


def projection_kernel(width, parts, near, distances, *refs):
    squares = refs[:parts]
    hidden_ref, gain_ref, query_ref, fresh_ref = refs[parts : parts + 4]
    out_refs = refs[parts + 4 :]
    total = paired_sum([ref[...] for ref in by_step(squares, near)])
    inverse = lax.rsqrt(total[:, :1] / width + epsilon)
    gain = gain_ref[...].astype(jnp.float32)
    normed = (flat_tokens(hidden_ref) * inverse * gain).astype(jnp.bfloat16)
    tokens = normed.shape[0]
    position = lax.axis_index("seq")
    far, _, lanes = out_refs[0].shape
    query_width = query_ref.shape[1] // (near * far)
    pieces = query_width // lanes

    def times(ref, chunk, size):
        columns = ref[:, pl.ds(pl.multiple_of(chunk * size, size), size)]
        return jnp.dot(normed, columns, preferred_element_type=jnp.float32)

    for distance, out in zip(distances, out_refs):
        for group in range(far):
            chunk = chunk_of(position, near, distance, group)
            part = times(query_ref, chunk, query_width)
            for piece in range(pieces):
                out[group, piece * tokens : (piece + 1) * tokens, :] = part[
                    :, piece * lanes : (piece + 1) * lanes
                ]
            out[group, pieces * tokens :, :] = times(fresh_ref, chunk, lanes)


def sum_kernel(count, low, *refs):
    total = paired_sum([ref[...] for ref in by_step(refs[:count], low)])
    for out in refs[count:]:
        out[...] = total.astype(out.dtype)


def head_of(kind_ref, flag, rank):
    found, before = jnp.int32(0), jnp.int32(0)
    for head in range(kind_ref.shape[0]):
        is_kind = kind_ref[head] == flag
        found = jnp.where(is_kind & (before == rank), head, found)
        before = before + is_kind.astype(jnp.int32)
    return found


def diagonal_of(rows, lanes):
    return lax.broadcasted_iota(jnp.int32, (rows, lanes), 0) == lax.broadcasted_iota(
        jnp.int32, (rows, lanes), 1
    )


def as_row(column, lanes):
    return jnp.sum(
        jnp.where(diagonal_of(column.shape[0], lanes), column, 0.0), axis=0, keepdims=True
    )


def as_column(row, rows):
    return jnp.sum(jnp.where(diagonal_of(rows, row.shape[1]), row, 0.0), axis=1, keepdims=True)


def masked_weights(scores, visible):
    scores = jnp.where(visible, scores, floor_score)
    peak = jnp.max(scores, axis=1, keepdims=True)
    weights = jnp.exp(scores - jnp.maximum(peak, 0.5 * floor_score))
    return peak, jnp.sum(weights, axis=1, keepdims=True), weights.astype(jnp.bfloat16)


def dot_keys(queries, keys):
    return lax.dot_general(
        queries, keys, (((1,), (1,)), ((), ())), preferred_element_type=jnp.float32
    )


def thirds(row):
    rest, pieces = row, []
    for _ in range(3):
        pieces.append(rest.astype(jnp.bfloat16))
        rest = rest - pieces[-1].astype(jnp.float32)
    return pieces


def stat_rows(peak, total, lanes, sublanes):
    return row_stats(as_row(peak, lanes), as_row(total, lanes), sublanes)


def row_stats(peak, total, sublanes):
    lanes = peak.shape[1]
    pieces = [*thirds(peak), *thirds(total)]
    wide = [piece.astype(jnp.float32) for piece in pieces]
    pad = jnp.zeros((sublanes - len(wide), lanes), jnp.float32)
    return jnp.concatenate([*wide, pad], axis=0)


def joined_thirds(rows):
    return (rows[0] + rows[1]) + rows[2]


def attention_kernel(
    drafts,
    kind_ref,
    cache_ref,
    sink_ref,
    window_ref,
    ret_key_ref,
    ret_value_ref,
    str_key_ref,
    str_value_ref,
    *refs,
):
    near = (len(refs) - 2) // 2
    part_refs, out_refs = refs[:near], refs[near : 2 * near]
    entries_ref, out_ref = refs[2 * near :]
    requests, retrieval, block, head_dim = ret_value_ref.shape
    position = lax.axis_index("seq")
    for distance, part_ref in enumerate(by_step(part_refs, 1)):
        for group in range(part_ref.shape[0]):
            chunk = chunk_of(position, near, distance, group)
            entries_ref[chunk] = part_ref[group]
    tokens = requests * drafts
    chunks, all_rows, _ = entries_ref.shape
    head_rows = all_rows - tokens
    per_head = chunks // kind_ref.shape[0]
    rows = per_head * head_rows
    row = lax.broadcasted_iota(jnp.int32, (rows, 1), 0)
    request_of_row = (row % tokens) // drafts

    def by_request(values):
        picked = values[0]
        for b in range(1, requests):
            picked = jnp.where(request_of_row == b, values[b], picked)
        return picked

    def limit(ref):
        return by_request([ref[b] for b in range(requests)])

    def weighed(flag, rank, keys, visible):
        head = head_of(kind_ref, flag, rank)
        queries = jnp.concatenate(
            [entries_ref[head * per_head + half, :head_rows, :] for half in range(per_head)], axis=0
        )
        scores = by_request([dot_keys(queries, one_keys) for one_keys in keys])
        return head, *masked_weights(scores * head_dim ** (-0.5), visible)

    def mix(weights, values):
        return jnp.dot(
            weights, jnp.concatenate(values, axis=1), preferred_element_type=jnp.float32
        )

    def store(head, peak, total, mixed):
        mixed = by_request([mixed[:, b * head_dim : (b + 1) * head_dim] for b in range(requests)])
        for half in range(per_head):
            span = slice(half * head_rows, (half + 1) * head_rows)
            block_rows = jnp.concatenate(
                [mixed[span], stat_rows(peak[span], total[span], head_dim, tokens)], axis=0
            )
            out_ref[head * per_head + half] = block_rows.astype(jnp.bfloat16)

    def of_rank(ref, rank):
        return [ref[b, rank] for b in range(requests)]

    slots = str_key_ref.shape[2]
    slot = position * slots + lax.broadcasted_iota(jnp.int32, (rows, slots), 1)
    recent = (slot >= SINK_CAP) & (slot < SINK_CAP + limit(window_ref))
    held = (slot < limit(sink_ref)) | recent
    running = range(str_key_ref.shape[1])
    ready = [weighed(0, rank, of_rank(str_key_ref, rank), held) for rank in running]
    for rank in running:
        head, peak, total, weights = ready[rank]
        store(head, peak, total, mix(weights, of_rank(str_value_ref, rank)))
    place = position * block + lax.broadcasted_iota(jnp.int32, (rows, block), 1)
    filled = place < limit(cache_ref)
    ready = [weighed(1, rank, of_rank(ret_key_ref, rank), filled) for rank in range(retrieval)]
    for rank in range(retrieval):
        head, peak, total, weights = ready[rank]
        store(head, peak, total, mix(weights, of_rank(ret_value_ref, rank)))
    for distance, part_ref in enumerate(out_refs):
        for group in range(part_ref.shape[0]):
            part_ref[group] = out_ref[chunk_of(position, near, distance, group)]


def merged(parts, rows):
    stats = [part[rows:] for part in parts]

    def stacked(first):
        return joined_thirds(
            [
                jnp.concatenate([stat[r : r + 1] for stat in stats], axis=0)
                for r in range(first, first + 3)
            ]
        )

    peaks, totals = stacked(0), stacked(3)
    peak = jnp.max(peaks, axis=0, keepdims=True)
    factors = jnp.exp(peaks - peak)
    total = jnp.sum(factors * totals, axis=0, keepdims=True)
    mixed = [
        as_column(factors[index : index + 1], rows) * part[:rows]
        for index, part in enumerate(parts)
    ]
    return peak, total, functools.reduce(jnp.add, mixed)


def merge_kernel(tokens, near, *refs):
    parts, out_refs = refs[:near], refs[near:]
    rows = out_refs[0].shape[0] - tokens
    group = lax.axis_index("seq") // near
    for distance, out in enumerate(out_refs):
        chunk = group ^ distance
        peak, total, mixed = merged([part[chunk].astype(jnp.float32) for part in parts], rows)
        stats = row_stats(peak, total, tokens)
        out[...] = jnp.concatenate([mixed, stats], axis=0).astype(out.dtype)


def fresh_kernel(kv_heads, requests, drafts, entries_ref, out_ref):
    position = lax.axis_index("seq")
    tokens = requests * drafts
    chunks, all_rows, head_dim = entries_ref.shape
    rows = all_rows - tokens
    head = position // (chunks // kv_heads)
    queries = entries_ref[position, :rows, :]
    keys = entries_ref[head, rows:, :]
    values = entries_ref[kv_heads + head, rows:, :]
    of_row = lax.broadcasted_iota(jnp.int32, (rows, tokens), 0) % tokens
    of_key = lax.broadcasted_iota(jnp.int32, (rows, tokens), 1)
    visible = (of_row // drafts == of_key // drafts) & (of_key <= of_row)
    peak, total, weights = masked_weights(dot_keys(queries, keys) * head_dim ** (-0.5), visible)
    out_ref[:rows, :] = jnp.dot(weights, values, preferred_element_type=jnp.float32)
    out_ref[rows:, :] = stat_rows(peak, total, head_dim, tokens)


def mixed_kernel(tokens, near, distances, *refs):
    count = len(refs) - 3 - len(distances)
    part_refs, (fresh_ref, weight_ref) = refs[:count], refs[count : count + 2]
    attention_ref, out_refs = refs[count + 2], refs[count + 3 :]
    rows = fresh_ref.shape[0] - tokens
    parts = [part[...].astype(jnp.float32) for part in part_refs]
    _, total, mixed = merged([*parts, fresh_ref[...]], rows)
    attended = mixed / as_column(total, rows)
    attention_ref[...] = jnp.concatenate(
        [attended[r : r + tokens] for r in range(0, rows, tokens)], axis=1
    ).astype(jnp.bfloat16)
    output_kernel(near, distances, attention_ref, weight_ref, *out_refs)


def output_kernel(near, distances, attention_ref, weight_ref, *out_refs):
    position = lax.axis_index("seq")
    for distance, out in zip(distances, out_refs):
        far, _, width = out.shape
        for group in range(far):
            chunk = chunk_of(position, near, distance, group)
            columns = weight_ref[:, pl.ds(pl.multiple_of(chunk * width, width), width)]
            out[group] = jnp.dot(
                attention_ref[...], columns, preferred_element_type=jnp.float32
            ).astype(out.dtype)


def fold_kernel(near, *refs):
    parts, out_refs = refs[:near], refs[near:]
    group = lax.axis_index("seq") // near
    for distance, out in enumerate(out_refs):
        chunk = group ^ distance
        out[...] = paired_sum([part[chunk].astype(jnp.float32) for part in parts]).astype(out.dtype)


def last_kernel(*refs):
    total = paired_sum([ref[...].astype(jnp.float32) for ref in refs[:-1]])
    drafts = refs[-1].shape[1]
    for request in range(refs[-1].shape[0]):
        span = slice(request * drafts, (request + 1) * drafts)
        refs[-1][request] = total[span].astype(refs[-1].dtype)


def on_core(kernel, out_shape, limit, *args, streamed=(), scratch=(), cost=None):
    vmem = pl.BlockSpec(memory_space=pltpu.VMEM)
    smem = pl.BlockSpec(memory_space=pltpu.SMEM)
    scalars = [arg.dtype == jnp.int32 for arg in args]
    placed = [
        arg if scalar else pltpu.with_memory_space_constraint(arg, pltpu.VMEM)
        for arg, scalar in zip(args, scalars)
    ]
    specs = [smem if scalar else vmem for scalar in scalars]
    return pl.pallas_call(
        kernel,
        out_shape=out_shape,
        in_specs=specs + [pl.BlockSpec(memory_space=pltpu.HBM)] * len(streamed),
        scratch_shapes=scratch,
        compiler_params=pltpu.CompilerParams(vmem_limit_bytes=limit * 2**20),
        cost_estimate=cost,
    )(*placed, *(pltpu.with_memory_space_constraint(arg, pltpu.HBM) for arg in streamed))


def shaped(*shape, dtype=jnp.float32):
    return jax.ShapeDtypeStruct(shape, dtype)


def per_device_heads(
    hidden,
    norm_gain,
    q_weight,
    kv_weight,
    out_weight,
    head_kind,
    ret_keys,
    ret_values,
    stream_keys,
    stream_values,
    cache_len,
    sink_len,
    window_len,
):
    requests, drafts, local_width = hidden.shape
    kv_heads = head_kind.shape[0]
    head_dim = ret_keys.shape[3]
    devices = lax.axis_size("seq")
    tokens = requests * drafts
    query_width = q_weight.shape[1] // devices
    rows = tokens * (query_width // head_dim)
    near = min(4, devices)
    far = devices // near
    hint = pl.CostEstimate(
        flops=2 * tokens * devices * devices * q_weight.size,
        bytes_accessed=hidden.size,
        transcendentals=0,
    )
    def copies(count, shape, dtype, low, *values, cost=None):
        return on_core(
            functools.partial(sum_kernel, len(values), low),
            [shaped(*shape, dtype=dtype)] * count,
            4,
            *values,
            cost=cost,
        )

    own, *sent = on_core(
        squares_kernel, [shaped(tokens, head_dim)] * near, 4, hidden
    )
    own, *sent = copies(
        far, (tokens, head_dim), jnp.float32, 1, own, *from_peers(sent, 1), cost=hint
    )
    squares = [own, *from_peers(sent, near)]
    gain = norm_gain[None, :]

    def projected(distances):
        return on_core(
            functools.partial(projection_kernel, local_width * devices, far, near, distances),
            [shaped(far, rows + tokens, head_dim)] * len(distances),
            8,
            *squares,
            hidden,
            gain,
            q_weight,
            kv_weight,
        )

    distances = [*range(near // 2, near), *range(near // 2)]
    part_entries = projected(distances[: near // 2]) + projected(distances[near // 2 :])
    own = part_entries[distances.index(0)]
    others = [
        from_peer(part_entries[distances.index(step)], step) for step in steps_of(near, 1)[1:]
    ]
    block = (far, rows + tokens, head_dim)
    own, *sent = copies(far, block, jnp.float32, 1, own, *others, cost=hint)
    own, *sent = copies(near, block, jnp.bfloat16, near, own, *from_peers(sent, near))
    blocks = (devices, rows + tokens, head_dim)
    *part_out, entries = on_core(
        functools.partial(attention_kernel, drafts),
        [shaped(far, *blocks[1:], dtype=jnp.bfloat16)] * near
        + [pltpu.VMEM(blocks, jnp.bfloat16)],
        16,
        head_kind,
        cache_len,
        sink_len,
        window_len,
        ret_keys,
        ret_values,
        stream_keys,
        stream_values,
        own,
        *from_peers(sent, 1),
        scratch=[pltpu.VMEM(blocks, jnp.bfloat16)],
    )
    new_entries = entries[:, rows:, :].transpose(1, 0, 2).reshape(requests, drafts, -1)
    own_out = part_out[0]
    near_out = from_peers(part_out[1:], 1)
    fresh = on_core(
        functools.partial(fresh_kernel, kv_heads, requests, drafts),
        shaped(rows + tokens, head_dim),
        4,
        entries,
    )
    chip_out = on_core(
        functools.partial(merge_kernel, tokens, near),
        [shaped(rows + tokens, head_dim, dtype=jnp.bfloat16)] * far,
        4,
        own_out,
        *near_out,
        cost=hint,
    )
    far_out = from_peers(chip_out[1:], near)
    width = out_weight.shape[1] // devices
    distances = range(near - 1, 0, -1)
    attention, *part_output = on_core(
        functools.partial(mixed_kernel, tokens, near, distances),
        [pltpu.VMEM((tokens, out_weight.shape[0]), jnp.bfloat16)]
        + [shaped(far, tokens, width, dtype=jnp.bfloat16)] * len(distances),
        8,
        chip_out[0],
        *far_out,
        fresh,
        out_weight,
    )
    near_output = [from_peer(part, distance) for distance, part in zip(distances, part_output)]
    distances = (0,)
    *part_output, own_output = on_core(
        functools.partial(output_kernel, near, distances),
        [shaped(far, tokens, width, dtype=jnp.bfloat16)] * (len(distances) - 1)
        + [shaped(far, tokens, width)],
        8,
        attention,
        out_weight,
    )
    near_output += [from_peer(part, distance) for distance, part in zip(distances, part_output)]
    own_output, *chip_output = on_core(
        functools.partial(fold_kernel, near),
        [shaped(tokens, width)] + [shaped(tokens, width, dtype=jnp.bfloat16)] * (far - 1),
        4,
        own_output,
        *near_output[::-1],
    )
    layer_output = on_core(
        last_kernel,
        shaped(requests, drafts, width, dtype=jnp.bfloat16),
        4,
        own_output,
        *from_peers(chip_output, near),
    )
    return (layer_output, new_entries)


def per_device(*args):
    hidden, _, q_weight, kv_weight, _, head_kind, ret_keys, _, stream_keys = args[:9]
    devices = lax.axis_size("seq")
    kv_heads, head_dim = head_kind.shape[0], ret_keys.shape[3]
    whole_heads = (
        (hidden.shape[0] * hidden.shape[1]) % 8 == 0
        and q_weight.shape[1] % (devices * head_dim) == 0
        and kv_weight.shape[1] == devices * head_dim
        and devices == 2 * kv_heads
        and ret_keys.shape[1] == stream_keys.shape[1]
    )
    return (per_device_heads if whole_heads else per_device_any)(*args)


def solution(mesh):
    in_specs = (
        P("groups", None, "seq"),
        P("seq"),
        P("seq", None),
        P("seq", None),
        P("seq", None),
        P(),
        P("groups", None, "seq", None),
        P("groups", None, "seq", None),
        P("groups", None, "seq", None),
        P("groups", None, "seq", None),
        P("groups"),
        P("groups"),
        P("groups"),
    )
    out_specs = (P("groups", None, "seq"), P("groups", None, None))
    return jax.shard_map(
        per_device, mesh=mesh, in_specs=in_specs, out_specs=out_specs, check_vma=False
    )
```

```python
import functools

import jax
import jax.numpy as jnp
from jax import lax
from jax.experimental import pallas as pl
from jax.experimental.pallas import tpu as pltpu
from jax.sharding import PartitionSpec as P


SINK_CAP = 128


epsilon = 1e-05
floor_score = -1e30


def exchanged(parts):
    return lax.all_to_all(parts, "seq", 0, 0, tiled=True)


def summed_over_devices(value):
    devices = lax.axis_size("seq")
    step = 1
    while step < devices:
        value = value + lax.ppermute(value, "seq", [(i, i ^ step) for i in range(devices)])
        step *= 2
    return value


def column_blocks(rows, blocks):
    return rows.reshape(rows.shape[0], blocks, -1).transpose(1, 0, 2)


def block_stats(queries, cache_keys, cache_values, visible, score_scale):
    scores = (
        jnp.einsum("bhqd,bhld->bhql", queries, cache_keys, preferred_element_type=jnp.float32)
        * score_scale
    )
    scores = jnp.where(visible, scores, floor_score)
    peak_score = jnp.max(scores, axis=-1)
    weights = jnp.where(visible, jnp.exp(scores - peak_score[..., None]), 0.0)
    weight_total = jnp.sum(weights, axis=-1)
    block_out = jnp.einsum(
        "bhql,bhld->bhqd",
        weights.astype(jnp.bfloat16),
        cache_values,
        preferred_element_type=jnp.float32,
    )
    return (peak_score, weight_total, block_out)


def spread_rows(values_in, selector):
    return jnp.einsum("brq,gr->bgq", values_in, selector, precision=lax.Precision.HIGHEST)


def spread_vectors(values_in, selector):
    return jnp.einsum("brqd,gr->bgqd", values_in, selector, precision=lax.Precision.HIGHEST)


def per_device_any(
    hidden,
    norm_gain,
    q_weight,
    kv_weight,
    out_weight,
    head_kind,
    ret_keys,
    ret_values,
    stream_keys,
    stream_values,
    cache_len,
    sink_len,
    window_len,
):
    requests, drafts, local_width = hidden.shape
    kv_heads = head_kind.shape[0]
    head_dim = ret_keys.shape[3]
    retrieval = ret_keys.shape[1]
    running = stream_keys.shape[1]
    head_count = q_weight.shape[1] // head_dim
    group_size = head_count // kv_heads
    query_rows = drafts * group_size
    devices = lax.axis_size("seq")
    position = lax.axis_index("seq")
    tokens = requests * drafts
    hidden32 = hidden.astype(jnp.float32)
    squares = summed_over_devices(jnp.sum(hidden32 * hidden32, axis=-1))
    inverse = lax.rsqrt(squares / (local_width * devices) + epsilon)
    normed = (hidden32 * inverse[..., None] * norm_gain.astype(jnp.float32)).astype(jnp.bfloat16)
    flat_rows = normed.reshape(tokens, local_width)
    part_query = jnp.dot(flat_rows, q_weight, preferred_element_type=jnp.float32)
    part_fresh = jnp.dot(flat_rows, kv_weight, preferred_element_type=jnp.float32)
    sums = jnp.sum(
        exchanged(
            jnp.concatenate(
                [column_blocks(part_query, devices), column_blocks(part_fresh, devices)], axis=-1
            )
        ),
        axis=0,
    ).astype(jnp.bfloat16)
    gathered = exchanged(jnp.broadcast_to(sums[None], (devices, *sums.shape)))
    query_width = q_weight.shape[1] // devices
    queries = gathered[..., :query_width].transpose(1, 0, 2).reshape(tokens, -1)
    new_entries = gathered[..., query_width:].transpose(1, 0, 2).reshape(tokens, -1)
    grouped = (
        queries.reshape(requests, drafts, kv_heads, group_size, head_dim)
        .transpose(0, 2, 1, 3, 4)
        .reshape(requests, kv_heads, query_rows, head_dim)
    )
    fresh_split = new_entries.reshape(requests, drafts, 2, kv_heads, head_dim)
    new_keys = fresh_split[:, :, 0].transpose(0, 2, 1, 3)
    new_values = fresh_split[:, :, 1].transpose(0, 2, 1, 3)
    kind_flag = head_kind == 1
    rank_ret = jnp.cumsum(head_kind) - 1
    rank_str = jnp.cumsum(1 - head_kind) - 1
    select_ret = (
        kind_flag[:, None] & (rank_ret[:, None] == jnp.arange(retrieval)[None, :])
    ).astype(jnp.float32)
    select_str = (
        jnp.logical_not(kind_flag)[:, None] & (rank_str[:, None] == jnp.arange(running)[None, :])
    ).astype(jnp.float32)
    ret_queries = jnp.einsum(
        "bgqd,gr->brqd",
        grouped,
        select_ret.astype(jnp.bfloat16),
        preferred_element_type=jnp.float32,
    ).astype(jnp.bfloat16)
    str_queries = jnp.einsum(
        "bgqd,gr->brqd",
        grouped,
        select_str.astype(jnp.bfloat16),
        preferred_element_type=jnp.float32,
    ).astype(jnp.bfloat16)
    score_scale = head_dim ** (-0.5)
    cache_block = ret_keys.shape[2]
    cache_pos = position * cache_block + jnp.arange(cache_block)
    ret_visible = (cache_pos[None, :] < cache_len[:, None])[:, None, None, :]
    slot_block = stream_keys.shape[2]
    slot_pos = (position * slot_block + jnp.arange(slot_block))[None, :]
    sink_part = slot_pos < sink_len[:, None]
    recent_part = (slot_pos >= SINK_CAP) & (slot_pos < SINK_CAP + window_len[:, None])
    str_visible = (sink_part | recent_part)[:, None, None, :]
    ret_peak, ret_total, ret_out = block_stats(
        ret_queries, ret_keys, ret_values, ret_visible, score_scale
    )
    str_peak, str_total, str_out = block_stats(
        str_queries, stream_keys, stream_values, str_visible, score_scale
    )
    peak_all = spread_rows(ret_peak, select_ret) + spread_rows(str_peak, select_str)
    total_all = spread_rows(ret_total, select_ret) + spread_rows(str_total, select_str)
    out_all = spread_vectors(ret_out, select_ret) + spread_vectors(str_out, select_str)
    token_of_row = jnp.arange(query_rows) // group_size
    new_visible = jnp.arange(drafts)[None, :] <= token_of_row[:, None]
    new_peak, new_total, new_out = block_stats(
        grouped, new_keys, new_values, new_visible, score_scale
    )
    own_width = out_weight.shape[0]
    block_heads = max(1, own_width // head_dim)

    def by_token(value):
        split = value.reshape(requests, kv_heads, drafts, group_size, -1)
        return split.transpose(0, 2, 1, 3, 4).reshape(tokens, head_count, -1)

    first_head = (jnp.arange(devices) * own_width) // head_dim
    block_head = first_head[:, None] + jnp.arange(block_heads)[None, :]

    def head_blocks(value):
        rows = by_token(value).reshape(tokens, head_count)
        return jnp.take(rows, block_head.reshape(-1), axis=1).reshape(tokens, devices, -1).transpose(1, 0, 2)

    received = exchanged(
        jnp.concatenate(
            [
                column_blocks(by_token(out_all).reshape(tokens, -1), devices),
                head_blocks(peak_all),
                head_blocks(total_all),
            ],
            axis=-1,
        )
    )
    got_out = received[..., :own_width].reshape(devices, tokens, block_heads, -1)
    got_peak = received[..., own_width : own_width + block_heads]
    got_total = received[..., own_width + block_heads :]

    def own_heads(value):
        blocks = column_blocks(by_token(value).reshape(tokens, -1), devices)
        return lax.dynamic_index_in_dim(blocks, position, 0, False).reshape(tokens, block_heads, -1)

    own_new_out = own_heads(new_out)
    own_new_peak = lax.dynamic_index_in_dim(head_blocks(new_peak), position, 0, False)
    own_new_total = lax.dynamic_index_in_dim(head_blocks(new_total), position, 0, False)
    top_score = jnp.maximum(jnp.max(got_peak, axis=0), own_new_peak)
    cache_factor = jnp.exp(got_peak - top_score[None])
    new_factor = jnp.exp(own_new_peak - top_score)
    denominator = jnp.sum(got_total * cache_factor, axis=0) + own_new_total * new_factor
    attended = (
        jnp.sum(got_out * cache_factor[..., None], axis=0) + own_new_out * new_factor[..., None]
    ) / denominator[..., None]
    own_attention = attended.reshape(tokens, own_width).astype(jnp.bfloat16)
    part_output = jnp.dot(own_attention, out_weight, preferred_element_type=jnp.float32)
    own_output = jnp.sum(exchanged(column_blocks(part_output, devices)), axis=0)
    layer_output = own_output.reshape(requests, drafts, local_width).astype(jnp.bfloat16)
    return (layer_output, new_entries.reshape(requests, drafts, 2 * kv_heads * head_dim))


def flat_tokens(ref):
    return jnp.concatenate([ref[b].astype(jnp.float32) for b in range(ref.shape[0])], axis=0)


def squares_kernel(hidden_ref, *out_refs):
    rows = flat_tokens(hidden_ref)
    total = jnp.sum(rows * rows, axis=1, keepdims=True)
    for out in out_refs:
        out[...] = jnp.broadcast_to(total, out.shape)


def from_peer(value, distance):
    devices = lax.axis_size("seq")
    return lax.ppermute(value, "seq", [(i, i ^ distance) for i in range(devices)])


def steps_of(radix, low):
    order = (lambda step: (-step.bit_length(), step)) if low > 1 else (lambda step: -step)
    return (0, *sorted(range(1, radix), key=order))


def from_peers(values, low):
    return [from_peer(values[step - 1], low * step) for step in steps_of(len(values) + 1, low)[1:]]


def by_step(values, low):
    placed = dict(zip(steps_of(len(values), low), values))
    return [placed[step] for step in range(len(values))]


def paired_sum(values):
    while len(values) > 1:
        values = [left + right for left, right in zip(values[::2], values[1::2])]
    return values[0]


def chunk_of(position, near, distance, far):
    return far * near + ((position & (near - 1)) ^ distance)


def projection_kernel(width, parts, near, distances, *refs):
    squares = refs[:parts]
    hidden_ref, gain_ref, query_ref, fresh_ref = refs[parts : parts + 4]
    out_refs = refs[parts + 4 :]
    total = paired_sum([ref[...] for ref in by_step(squares, near)])
    inverse = lax.rsqrt(total[:, :1] / width + epsilon)
    gain = gain_ref[...].astype(jnp.float32)
    normed = (flat_tokens(hidden_ref) * inverse * gain).astype(jnp.bfloat16)
    tokens = normed.shape[0]
    position = lax.axis_index("seq")
    far, _, lanes = out_refs[0].shape
    query_width = query_ref.shape[1] // (near * far)
    pieces = query_width // lanes

    def times(ref, chunk, size):
        columns = ref[:, pl.ds(pl.multiple_of(chunk * size, size), size)]
        return jnp.dot(normed, columns, preferred_element_type=jnp.float32)

    for distance, out in zip(distances, out_refs):
        for group in range(far):
            chunk = chunk_of(position, near, distance, group)
            part = times(query_ref, chunk, query_width)
            for piece in range(pieces):
                out[group, piece * tokens : (piece + 1) * tokens, :] = part[
                    :, piece * lanes : (piece + 1) * lanes
                ]
            out[group, pieces * tokens :, :] = times(fresh_ref, chunk, lanes)


def sum_kernel(count, low, *refs):
    total = paired_sum([ref[...] for ref in by_step(refs[:count], low)])
    for out in refs[count:]:
        out[...] = total.astype(out.dtype)


def head_of(kind_ref, flag, rank):
    found, before = jnp.int32(0), jnp.int32(0)
    for head in range(kind_ref.shape[0]):
        is_kind = kind_ref[head] == flag
        found = jnp.where(is_kind & (before == rank), head, found)
        before = before + is_kind.astype(jnp.int32)
    return found


def diagonal_of(rows, lanes):
    return lax.broadcasted_iota(jnp.int32, (rows, lanes), 0) == lax.broadcasted_iota(
        jnp.int32, (rows, lanes), 1
    )


def as_row(column, lanes):
    return jnp.sum(
        jnp.where(diagonal_of(column.shape[0], lanes), column, 0.0), axis=0, keepdims=True
    )


def as_column(row, rows):
    return jnp.sum(jnp.where(diagonal_of(rows, row.shape[1]), row, 0.0), axis=1, keepdims=True)


def masked_weights(scores, visible):
    scores = jnp.where(visible, scores, floor_score)
    peak = jnp.max(scores, axis=1, keepdims=True)
    weights = jnp.exp(scores - jnp.maximum(peak, 0.5 * floor_score))
    return peak, jnp.sum(weights, axis=1, keepdims=True), weights.astype(jnp.bfloat16)


def dot_keys(queries, keys):
    return lax.dot_general(
        queries, keys, (((1,), (1,)), ((), ())), preferred_element_type=jnp.float32
    )


def thirds(row):
    rest, pieces = row, []
    for _ in range(3):
        pieces.append(rest.astype(jnp.bfloat16))
        rest = rest - pieces[-1].astype(jnp.float32)
    return pieces


def stat_rows(peak, total, lanes, sublanes):
    return row_stats(as_row(peak, lanes), as_row(total, lanes), sublanes)


def row_stats(peak, total, sublanes):
    lanes = peak.shape[1]
    pieces = [*thirds(peak), *thirds(total)]
    wide = [piece.astype(jnp.float32) for piece in pieces]
    pad = jnp.zeros((sublanes - len(wide), lanes), jnp.float32)
    return jnp.concatenate([*wide, pad], axis=0)


def joined_thirds(rows):
    return (rows[0] + rows[1]) + rows[2]


def attention_kernel(
    drafts,
    kind_ref,
    cache_ref,
    sink_ref,
    window_ref,
    ret_key_ref,
    ret_value_ref,
    str_key_ref,
    str_value_ref,
    *refs,
):
    near = (len(refs) - 2) // 2
    part_refs, out_refs = refs[:near], refs[near : 2 * near]
    entries_ref, out_ref = refs[2 * near :]
    requests, retrieval, block, head_dim = ret_value_ref.shape
    position = lax.axis_index("seq")
    for distance, part_ref in enumerate(by_step(part_refs, 1)):
        for group in range(part_ref.shape[0]):
            chunk = chunk_of(position, near, distance, group)
            entries_ref[chunk] = part_ref[group]
    tokens = requests * drafts
    chunks, all_rows, _ = entries_ref.shape
    head_rows = all_rows - tokens
    per_head = chunks // kind_ref.shape[0]
    rows = per_head * head_rows
    row = lax.broadcasted_iota(jnp.int32, (rows, 1), 0)
    request_of_row = (row % tokens) // drafts

    def by_request(values):
        picked = values[0]
        for b in range(1, requests):
            picked = jnp.where(request_of_row == b, values[b], picked)
        return picked

    def limit(ref):
        return by_request([ref[b] for b in range(requests)])

    def weighed(flag, rank, keys, visible):
        head = head_of(kind_ref, flag, rank)
        queries = jnp.concatenate(
            [entries_ref[head * per_head + half, :head_rows, :] for half in range(per_head)], axis=0
        )
        scores = by_request([dot_keys(queries, one_keys) for one_keys in keys])
        return head, *masked_weights(scores * head_dim ** (-0.5), visible)

    def mix(weights, values):
        return jnp.dot(
            weights, jnp.concatenate(values, axis=1), preferred_element_type=jnp.float32
        )

    def store(head, peak, total, mixed):
        mixed = by_request([mixed[:, b * head_dim : (b + 1) * head_dim] for b in range(requests)])
        for half in range(per_head):
            span = slice(half * head_rows, (half + 1) * head_rows)
            block_rows = jnp.concatenate(
                [mixed[span], stat_rows(peak[span], total[span], head_dim, tokens)], axis=0
            )
            out_ref[head * per_head + half] = block_rows.astype(jnp.bfloat16)

    def of_rank(ref, rank):
        return [ref[b, rank] for b in range(requests)]

    slots = str_key_ref.shape[2]
    slot = position * slots + lax.broadcasted_iota(jnp.int32, (rows, slots), 1)
    recent = (slot >= SINK_CAP) & (slot < SINK_CAP + limit(window_ref))
    held = (slot < limit(sink_ref)) | recent
    running = range(str_key_ref.shape[1])
    ready = [weighed(0, rank, of_rank(str_key_ref, rank), held) for rank in running]
    for rank in running:
        head, peak, total, weights = ready[rank]
        store(head, peak, total, mix(weights, of_rank(str_value_ref, rank)))
    place = position * block + lax.broadcasted_iota(jnp.int32, (rows, block), 1)
    filled = place < limit(cache_ref)
    ready = [weighed(1, rank, of_rank(ret_key_ref, rank), filled) for rank in range(retrieval)]
    for rank in range(retrieval):
        head, peak, total, weights = ready[rank]
        store(head, peak, total, mix(weights, of_rank(ret_value_ref, rank)))
    for distance, part_ref in enumerate(out_refs):
        for group in range(part_ref.shape[0]):
            part_ref[group] = out_ref[chunk_of(position, near, distance, group)]


def merged(parts, rows):
    stats = [part[rows:] for part in parts]

    def stacked(first):
        return joined_thirds(
            [
                jnp.concatenate([stat[r : r + 1] for stat in stats], axis=0)
                for r in range(first, first + 3)
            ]
        )

    peaks, totals = stacked(0), stacked(3)
    peak = jnp.max(peaks, axis=0, keepdims=True)
    factors = jnp.exp(peaks - peak)
    total = jnp.sum(factors * totals, axis=0, keepdims=True)
    mixed = [
        as_column(factors[index : index + 1], rows) * part[:rows]
        for index, part in enumerate(parts)
    ]
    return peak, total, functools.reduce(jnp.add, mixed)


def merge_kernel(tokens, near, *refs):
    parts, out_refs = refs[:near], refs[near:]
    rows = out_refs[0].shape[0] - tokens
    group = lax.axis_index("seq") // near
    for distance, out in enumerate(out_refs):
        chunk = group ^ distance
        peak, total, mixed = merged([part[chunk].astype(jnp.float32) for part in parts], rows)
        stats = row_stats(peak, total, tokens)
        out[...] = jnp.concatenate([mixed, stats], axis=0).astype(out.dtype)


def fresh_kernel(kv_heads, requests, drafts, entries_ref, out_ref):
    position = lax.axis_index("seq")
    tokens = requests * drafts
    chunks, all_rows, head_dim = entries_ref.shape
    rows = all_rows - tokens
    head = position // (chunks // kv_heads)
    queries = entries_ref[position, :rows, :]
    keys = entries_ref[head, rows:, :]
    values = entries_ref[kv_heads + head, rows:, :]
    of_row = lax.broadcasted_iota(jnp.int32, (rows, tokens), 0) % tokens
    of_key = lax.broadcasted_iota(jnp.int32, (rows, tokens), 1)
    visible = (of_row // drafts == of_key // drafts) & (of_key <= of_row)
    peak, total, weights = masked_weights(dot_keys(queries, keys) * head_dim ** (-0.5), visible)
    out_ref[:rows, :] = jnp.dot(weights, values, preferred_element_type=jnp.float32)
    out_ref[rows:, :] = stat_rows(peak, total, head_dim, tokens)


def mixed_kernel(tokens, near, distances, *refs):
    count = len(refs) - 3 - len(distances)
    part_refs, (fresh_ref, weight_ref) = refs[:count], refs[count : count + 2]
    attention_ref, out_refs = refs[count + 2], refs[count + 3 :]
    rows = fresh_ref.shape[0] - tokens
    parts = [part[...].astype(jnp.float32) for part in part_refs]
    _, total, mixed = merged([*parts, fresh_ref[...]], rows)
    attended = mixed / as_column(total, rows)
    attention_ref[...] = jnp.concatenate(
        [attended[r : r + tokens] for r in range(0, rows, tokens)], axis=1
    ).astype(jnp.bfloat16)
    output_kernel(near, distances, attention_ref, weight_ref, *out_refs)


def output_kernel(near, distances, attention_ref, weight_ref, *out_refs):
    position = lax.axis_index("seq")
    for distance, out in zip(distances, out_refs):
        far, _, width = out.shape
        for group in range(far):
            chunk = chunk_of(position, near, distance, group)
            columns = weight_ref[:, pl.ds(pl.multiple_of(chunk * width, width), width)]
            out[group] = jnp.dot(
                attention_ref[...], columns, preferred_element_type=jnp.float32
            ).astype(out.dtype)


def fold_kernel(near, *refs):
    parts, out_refs = refs[:near], refs[near:]
    group = lax.axis_index("seq") // near
    for distance, out in enumerate(out_refs):
        chunk = group ^ distance
        out[...] = paired_sum([part[chunk].astype(jnp.float32) for part in parts]).astype(out.dtype)


def last_kernel(*refs):
    total = paired_sum([ref[...].astype(jnp.float32) for ref in refs[:-1]])
    drafts = refs[-1].shape[1]
    for request in range(refs[-1].shape[0]):
        span = slice(request * drafts, (request + 1) * drafts)
        refs[-1][request] = total[span].astype(refs[-1].dtype)


def on_core(kernel, out_shape, limit, *args, streamed=(), scratch=(), cost=None):
    vmem = pl.BlockSpec(memory_space=pltpu.VMEM)
    smem = pl.BlockSpec(memory_space=pltpu.SMEM)
    scalars = [arg.dtype == jnp.int32 for arg in args]
    placed = [
        arg if scalar else pltpu.with_memory_space_constraint(arg, pltpu.VMEM)
        for arg, scalar in zip(args, scalars)
    ]
    specs = [smem if scalar else vmem for scalar in scalars]
    return pl.pallas_call(
        kernel,
        out_shape=out_shape,
        in_specs=specs + [pl.BlockSpec(memory_space=pltpu.HBM)] * len(streamed),
        scratch_shapes=scratch,
        compiler_params=pltpu.CompilerParams(vmem_limit_bytes=limit * 2**20),
        cost_estimate=cost,
    )(*placed, *(pltpu.with_memory_space_constraint(arg, pltpu.HBM) for arg in streamed))


def shaped(*shape, dtype=jnp.float32):
    return jax.ShapeDtypeStruct(shape, dtype)


def per_device_heads(
    hidden,
    norm_gain,
    q_weight,
    kv_weight,
    out_weight,
    head_kind,
    ret_keys,
    ret_values,
    stream_keys,
    stream_values,
    cache_len,
    sink_len,
    window_len,
):
    requests, drafts, local_width = hidden.shape
    kv_heads = head_kind.shape[0]
    head_dim = ret_keys.shape[3]
    devices = lax.axis_size("seq")
    tokens = requests * drafts
    query_width = q_weight.shape[1] // devices
    rows = tokens * (query_width // head_dim)
    near = min(4, devices)
    far = devices // near
    hint = pl.CostEstimate(
        flops=2 * tokens * devices * devices * q_weight.size,
        bytes_accessed=hidden.size,
        transcendentals=0,
    )
    def copies(count, shape, dtype, low, *values, cost=None):
        return on_core(
            functools.partial(sum_kernel, len(values), low),
            [shaped(*shape, dtype=dtype)] * count,
            4,
            *values,
            cost=cost,
        )

    own, *sent = on_core(
        squares_kernel, [shaped(tokens, head_dim)] * near, 4, hidden
    )
    own, *sent = copies(
        far, (tokens, head_dim), jnp.float32, 1, own, *from_peers(sent, 1), cost=hint
    )
    squares = [own, *from_peers(sent, near)]
    gain = norm_gain[None, :]

    def projected(distances):
        return on_core(
            functools.partial(projection_kernel, local_width * devices, far, near, distances),
            [shaped(far, rows + tokens, head_dim)] * len(distances),
            8,
            *squares,
            hidden,
            gain,
            q_weight,
            kv_weight,
        )

    distances = [*range(near // 2, near), *range(near // 2)]
    part_entries = projected(distances[: near // 2]) + projected(distances[near // 2 :])
    own = part_entries[distances.index(0)]
    others = [
        from_peer(part_entries[distances.index(step)], step) for step in steps_of(near, 1)[1:]
    ]
    block = (far, rows + tokens, head_dim)
    own, *sent = copies(far, block, jnp.float32, 1, own, *others, cost=hint)
    wide = [from_peer(sent[step - 1], near * step) for step in steps_of(far, 1)[1:]]
    own, *sent = copies(near, block, jnp.bfloat16, 1, own, *wide)
    blocks = (devices, rows + tokens, head_dim)
    *part_out, entries = on_core(
        functools.partial(attention_kernel, drafts),
        [shaped(far, *blocks[1:], dtype=jnp.bfloat16)] * near
        + [pltpu.VMEM(blocks, jnp.bfloat16)],
        16,
        head_kind,
        cache_len,
        sink_len,
        window_len,
        ret_keys,
        ret_values,
        stream_keys,
        stream_values,
        own,
        *from_peers(sent, 1),
        scratch=[pltpu.VMEM(blocks, jnp.bfloat16)],
    )
    new_entries = entries[:, rows:, :].transpose(1, 0, 2).reshape(requests, drafts, -1)
    own_out = part_out[0]
    near_out = from_peers(part_out[1:], 1)
    fresh = on_core(
        functools.partial(fresh_kernel, kv_heads, requests, drafts),
        shaped(rows + tokens, head_dim),
        4,
        entries,
    )
    chip_out = on_core(
        functools.partial(merge_kernel, tokens, near),
        [shaped(rows + tokens, head_dim, dtype=jnp.bfloat16)] * far,
        4,
        own_out,
        *near_out,
        cost=hint,
    )
    far_out = from_peers(chip_out[1:], near)
    width = out_weight.shape[1] // devices
    distances = range(near - 1, 0, -1)
    attention, *part_output = on_core(
        functools.partial(mixed_kernel, tokens, near, distances),
        [pltpu.VMEM((tokens, out_weight.shape[0]), jnp.bfloat16)]
        + [shaped(far, tokens, width, dtype=jnp.bfloat16)] * len(distances),
        8,
        chip_out[0],
        *far_out,
        fresh,
        out_weight,
    )
    near_output = [from_peer(part, distance) for distance, part in zip(distances, part_output)]
    distances = (0,)
    *part_output, own_output = on_core(
        functools.partial(output_kernel, near, distances),
        [shaped(far, tokens, width, dtype=jnp.bfloat16)] * (len(distances) - 1)
        + [shaped(far, tokens, width)],
        8,
        attention,
        out_weight,
    )
    near_output += [from_peer(part, distance) for distance, part in zip(distances, part_output)]
    own_output, *chip_output = on_core(
        functools.partial(fold_kernel, near),
        [shaped(tokens, width)] + [shaped(tokens, width, dtype=jnp.bfloat16)] * (far - 1),
        4,
        own_output,
        *near_output[::-1],
    )
    layer_output = on_core(
        last_kernel,
        shaped(requests, drafts, width, dtype=jnp.bfloat16),
        4,
        own_output,
        *from_peers(chip_output, near),
    )
    return (layer_output, new_entries)


def per_device(*args):
    hidden, _, q_weight, kv_weight, _, head_kind, ret_keys, _, stream_keys = args[:9]
    devices = lax.axis_size("seq")
    kv_heads, head_dim = head_kind.shape[0], ret_keys.shape[3]
    whole_heads = (
        (hidden.shape[0] * hidden.shape[1]) % 8 == 0
        and q_weight.shape[1] % (devices * head_dim) == 0
        and kv_weight.shape[1] == devices * head_dim
        and devices == 2 * kv_heads
        and ret_keys.shape[1] == stream_keys.shape[1]
    )
    return (per_device_heads if whole_heads else per_device_any)(*args)


def solution(mesh):
    in_specs = (
        P("groups", None, "seq"),
        P("seq"),
        P("seq", None),
        P("seq", None),
        P("seq", None),
        P(),
        P("groups", None, "seq", None),
        P("groups", None, "seq", None),
        P("groups", None, "seq", None),
        P("groups", None, "seq", None),
        P("groups"),
        P("groups"),
        P("groups"),
    )
    out_specs = (P("groups", None, "seq"), P("groups", None, None))
    return jax.shard_map(
        per_device, mesh=mesh, in_specs=in_specs, out_specs=out_specs, check_vma=False
    )
```
